256 devices in a mesh: cam: 8 (over z), tm: 32 (over x, y, core).
Axes of the slice: x: 4, y: 4, z: 8, core: 2. Of those that a mesh axis runs over, the one named last changes fastest.
Arguments:
- embeds: bfloat16 [8, 4096, 2048], P(None, 'tm', 'cam'), may hold values from -6 to 6
- w_in: bfloat16 [2048, 2304], replicated, may hold values from -0.125 to 0.125
- log_decay: float32 [8, 32, 4096], P('cam', None, 'tm'), may hold values from -1 to 0, as said below
- clip_keep: float32 [32], replicated, may hold values from 0.55 to 0.8
- clip_starts: int32 [8, 3], P('cam'), may hold values from 1 to 4095
- valid_len: int32 [8], P('cam'), may hold values from 2048 to 4096, as said below
- norm_gain: float32 [2048], replicated, may hold values from 0.1 to 1.9
- g_out: bfloat16 [8, 4096, 2048], P('cam', 'tm'), may hold values from -6 to 6
Outputs:
- layer_out: bfloat16 [8, 4096, 2048], P('cam', 'tm')
- d_embeds: bfloat16 [8, 4096, 2048], P(None, 'tm', 'cam')
- d_w_in: float32 [2048, 2304], P(('cam', 'tm'))
The draws below stay inside these ranges and needn't reach their ends.
Inputs may be any that keep to these rules, and one draw needn't show every extreme that they name: `log_decay`: negative. `valid_len`: some camera's valid length is 4096 in every draw.
All inputs are finite; a program needn't handle non-finite values.
Results may differ from the reference program's by a relative error of at most 0.014.
Values may be sent and summed in bfloat16 or wider, within the bound.
A program may use at most 128 MiB of HBM per device.

```python
import math
import jax
import jax.numpy as jnp
from jax import lax

D = 2048
H = 32
P_SIZE = 64
N = 128
Q = 128
NCLIP = 3
T_DEV = 128
CAM = 8
L = 4096
HP = 2048
E = 2304


def draw_log_decay(key, part):
    share = 0.5
    slow_mask = jax.random.uniform(jax.random.fold_in(key, 11), (H,)) < share
    slow_rate = jax.random.uniform(jax.random.fold_in(key, 12), (H,), minval=0.3, maxval=1.0) * (math.log(10.0) / (6 * L))
    fast_rate = 1.0 / jax.random.uniform(jax.random.fold_in(key, 13), (H,), minval=30.0, maxval=50.0)
    base_rate = jnp.where(slow_mask, slow_rate, fast_rate)
    spread_log = math.log(2.0)
    block_factor = jnp.exp(jax.random.uniform(jax.random.fold_in(key, 14), (CAM, H, L // T_DEV), minval=-spread_log, maxval=spread_log))
    block_factor = jnp.repeat(block_factor, T_DEV, axis=2)
    jitter = jnp.exp(jax.random.uniform(jax.random.fold_in(key, 15), (CAM, H, L), minval=-spread_log, maxval=spread_log))
    return (-(base_rate[None, :, None] * block_factor * jitter)).astype(jnp.float32)


def draw_valid_len(key, part):
    lengths = jax.random.randint(jax.random.fold_in(key, 21), (CAM,), L // 2, L + 1)
    full_index = jax.random.randint(jax.random.fold_in(key, 22), (), 0, CAM)
    return jnp.where(jnp.arange(CAM) == full_index, L, lengths).astype(jnp.int32)


def set_ends(array, key, least, high):
    extent = array.shape
    spot = [jax.random.randint(jax.random.fold_in(key, axis), (), 0, extent[axis]) for axis in range(len(extent))]
    array = array.at[tuple(spot)].set(least)
    longest = extent.index(max(extent))
    spot[longest] = (spot[longest] + 1) % extent[longest]
    return array.at[tuple(spot)].set(high)


def strengthened(drawn, stream_key, source, target, parts, factor):
    def block_of(position):
        return (jnp.arange(drawn.shape[position]) // (drawn.shape[position] // parts)).reshape((-1,) + (1,) * (drawn.ndim - 1 - position))

    near = jax.random.permutation(stream_key, parts)[block_of(target)]
    second = (block_of(target) + parts // 2) % parts
    return jnp.where((block_of(source) == near) | (block_of(source) == second), factor * drawn, drawn)


def level_of(key, dims, split, least, high):
    def one(dim, parts):
        steps = jax.random.uniform(jax.random.fold_in(jax.random.fold_in(key, 6), dim), (parts,), jnp.float32, least / len(split), high / len(split))
        return jnp.repeat(jnp.exp(steps), dims[dim] // parts).reshape((-1,) + (1,) * (len(dims) - dim - 1))

    gain = one(*split[0])
    for cut in split[1:]:
        gain = gain * one(*cut)
    return gain


def bell_draw(stream_key, dims, width, reach, pieces=(), held_as=jnp.bfloat16):
    entries = width * jax.random.normal(stream_key, dims, jnp.float32)
    if pieces:
        entries = entries * level_of(stream_key, dims, pieces, -0.22, 0.18)
    return jnp.clip(entries, -reach, reach).astype(held_as)


def heavy_noise(rng, shape, width, bound, pieces, heavy, kind=jnp.bfloat16):
    entries = width * jax.random.normal(rng, shape, jnp.float32)
    if pieces:
        entries = entries * level_of(rng, shape, pieces, -0.22, 0.18)
    return jnp.clip(strengthened(entries, jax.random.fold_in(rng, 3), *heavy), -bound, bound).astype(kind)


def setup_inputs(seed: int = 0) -> dict:
    keys = jax.random.split(jax.random.key(seed), 9)
    return {
        "embeds": heavy_noise(keys[0], (CAM, L, D), 1.0, 6.0, ((1, 32), (2, 8)), (1, 2, 32, 2.75)),
        "w_in": bell_draw(keys[1], (D, E), D ** -0.5, 0.125),
        "log_decay": draw_log_decay(jax.random.fold_in(keys[8], 71), 0),
        "clip_keep": jnp.clip(jax.random.uniform(keys[3], (H,), jnp.float32, 0.55, 0.8), 0.55, 0.8),
        "clip_starts": set_ends(jax.random.randint(keys[4], (CAM, NCLIP), 1, L), jax.random.fold_in(keys[4], 1), 1, L - 1).astype(jnp.int32),
        "valid_len": draw_valid_len(jax.random.fold_in(keys[8], 71), 0),
        "norm_gain": jnp.clip(1.0 + 0.18 * jax.random.normal(keys[6], (HP,), jnp.float32), 0.1, 1.9),
        "g_out": bell_draw(keys[7], (CAM, L, HP), 1.0, 6.0, ((0, 8), (1, 32))),
    }


epsilon = 1e-05
precise = lax.Precision.HIGHEST

def group_scan(x_vals, b_vals, c_vals, log_rates):
    length = x_vals.shape[0]
    groups = length // Q
    x_blocks = x_vals.reshape(groups, Q, H, P_SIZE)
    b_blocks = b_vals.reshape(groups, Q, N)
    c_blocks = c_vals.reshape(groups, Q, N)
    r_blocks = log_rates.reshape(H, groups, Q).transpose(1, 0, 2)
    causal = jnp.arange(Q)[:, None] >= jnp.arange(Q)[None, :]

    def advance(carried, blocks):
        x_group, b_group, c_group, r_group = blocks
        cum_rate = jnp.cumsum(r_group, axis=1)
        gaps = cum_rate[:, :, None] - cum_rate[:, None, :]
        weights = jnp.where(causal[None], jnp.exp(jnp.where(causal[None], gaps, 0.0)), 0.0)
        scores = jnp.einsum('tn,sn->ts', c_group, b_group, precision=precise)
        y_in = jnp.einsum('hts,shp->thp', weights * scores[None], x_group, precision=precise)
        y_out = jnp.exp(cum_rate).T[:, :, None] * jnp.einsum('hpn,tn->thp', carried, c_group, precision=precise)
        tail_decay = jnp.exp(cum_rate[:, -1:] - cum_rate)
        updated = jnp.exp(cum_rate[:, -1])[:, None, None] * carried + jnp.einsum('shp,sn->hpn', x_group * tail_decay.T[:, :, None], b_group, precision=precise)
        return (updated, y_in + y_out)
    start_state = jnp.zeros((H, P_SIZE, N), jnp.float32)
    _, outputs = lax.scan(advance, start_state, (x_blocks, b_blocks, c_blocks, r_blocks))
    return outputs.reshape(length, H, P_SIZE)

def reference(embeds, w_in, log_decay, clip_keep, clip_starts, valid_len, norm_gain, g_out):
    positions = jnp.arange(L, dtype=jnp.int32)
    keep_log = jnp.log(clip_keep)

    def camera(grad_total, camera_items):
        emb_c, rate_c, starts_c, len_c, cot_c = camera_items
        projected = jnp.dot(emb_c, w_in, preferred_element_type=jnp.float32).astype(jnp.bfloat16)
        is_start = jnp.any(positions[:, None] == starts_c[None, :].astype(jnp.int32), axis=1)
        log_rates = rate_c + jnp.where(is_start[None, :], keep_log[:, None], 0.0)
        valid_rows = (positions < len_c.astype(jnp.int32)).astype(jnp.float32)

        def forward(proj_float):
            x_vals = proj_float[:, :HP].reshape(L, H, P_SIZE) * valid_rows[:, None, None]
            raw_out = group_scan(x_vals, proj_float[:, HP:HP + N], proj_float[:, HP + N:], log_rates)
            inv_rms = lax.rsqrt(lax.optimization_barrier(jnp.mean(raw_out * raw_out, axis=-1, keepdims=True)) + epsilon)
            return (raw_out * inv_rms).reshape(L, HP) * norm_gain[None, :] * valid_rows[:, None]
        layer_f, pullback = jax.vjp(forward, projected.astype(jnp.float32))
        d_proj, = pullback(cot_c.astype(jnp.float32))
        d_proj = d_proj.astype(jnp.bfloat16)
        d_emb = lax.dot_general(d_proj, w_in, (((1,), (1,)), ((), ())), preferred_element_type=jnp.float32).astype(jnp.bfloat16)
        d_weight = lax.dot_general(emb_c, d_proj, (((0,), (0,)), ((), ())), preferred_element_type=jnp.float32)
        return (grad_total + d_weight, (layer_f.astype(jnp.bfloat16), d_emb))
    grad_total, (results, d_embs) = lax.scan(camera, jnp.zeros((D, E), jnp.float32), (embeds, log_decay, clip_starts, valid_len, g_out))
    return (results, d_embs, grad_total * (1.0 / math.sqrt(CAM * L)))
```

```python
import math

import jax
import jax.numpy as jnp
from jax import lax
from jax.sharding import PartitionSpec as P

D = 2048
H = 32
P_SIZE = 64
N = 128
Q = 128
HP = 2048


epsilon = 1e-05
precise = lax.Precision.HIGHEST


def prefix_states(block_log, state, reverse):
    size = lax.axis_size("tm")
    extra = jnp.broadcast_to(block_log[:, None, None], (H, 8, N))
    packed = jnp.concatenate([state, extra], axis=1)
    mine = lax.all_to_all(packed, "tm", split_axis=0, concat_axis=0, tiled=True)
    logs = mine[:, P_SIZE, 0]
    parts = mine[:, :P_SIZE].reshape(size, P_SIZE * N)
    cum = jnp.cumsum(logs)
    at = jnp.arange(size)
    if reverse:
        reach = at[None, :] > at[:, None]
        gap = (cum - logs)[None, :] - cum[:, None]
    else:
        reach = at[None, :] < at[:, None]
        gap = (cum - logs)[:, None] - cum[None, :]
    factors = jnp.where(reach, jnp.exp(jnp.where(reach, gap, 0.0)), 0.0)
    entered = jnp.dot(factors, parts, precision=precise).astype(jnp.bfloat16)
    entered = entered.reshape(size, P_SIZE, N)
    return lax.all_to_all(entered, "tm", split_axis=0, concat_axis=0, tiled=True).astype(jnp.float32)


def on_device(embeds, w_in, log_decay, clip_keep, clip_starts, valid_len, norm_gain, g_out):
    n_cam = lax.axis_size("cam")
    n_tm = lax.axis_size("tm")
    t_dev = embeds.shape[1]
    groups = t_dev // Q
    x_rows = lax.all_to_all(embeds, "cam", split_axis=0, concat_axis=2, tiled=True)[0]
    projected = jnp.dot(x_rows, w_in, preferred_element_type=jnp.float32).astype(jnp.bfloat16)
    positions = lax.axis_index("tm") * t_dev + jnp.arange(t_dev, dtype=jnp.int32)
    is_start = jnp.any(positions[:, None] == clip_starts[0][None, :], axis=1)
    log_rates = log_decay[0] + jnp.where(is_start[None, :], jnp.log(clip_keep)[:, None], 0.0)
    valid_rows = (positions < valid_len[0]).astype(jnp.float32)
    proj_float = projected.astype(jnp.float32)
    x_blocks = (proj_float[:, :HP].reshape(t_dev, H, P_SIZE) * valid_rows[:, None, None]).reshape(
        groups, Q, H, P_SIZE
    )
    b_blocks = proj_float[:, HP : HP + N].reshape(groups, Q, N)
    c_blocks = proj_float[:, HP + N :].reshape(groups, Q, N)
    cum_rate = jnp.cumsum(log_rates.reshape(H, groups, Q), axis=2).transpose(1, 0, 2)
    group_log = cum_rate[:, :, -1]
    causal = jnp.arange(Q)[:, None] >= jnp.arange(Q)[None, :]
    gaps = cum_rate[:, :, :, None] - cum_rate[:, :, None, :]
    weights = jnp.where(causal, jnp.exp(jnp.where(causal, gaps, 0.0)), 0.0)
    scores = jnp.einsum("ktn,ksn->kts", c_blocks, b_blocks, precision=precise)
    mixing = weights * scores[:, None]
    y_in = jnp.einsum("khts,kshp->kthp", mixing, x_blocks, precision=precise)
    tail_decay = jnp.exp(group_log[:, :, None] - cum_rate).transpose(0, 2, 1)
    lift_decay = jnp.exp(cum_rate).transpose(0, 2, 1)
    local_state = jnp.einsum(
        "kshp,ksn->khpn", x_blocks * tail_decay[:, :, :, None], b_blocks, precision=precise
    )
    zero_before = [jnp.zeros((H, P_SIZE, N), jnp.float32)]
    zero_end = jnp.exp(group_log[-1])[:, None, None] * zero_before[-1] + local_state[-1]
    block_log = jnp.sum(group_log, axis=0)
    s_in = prefix_states(block_log, zero_end, False)
    lead_log = jnp.cumsum(group_log, axis=0) - group_log
    state_before = jnp.exp(lead_log)[:, :, None, None] * s_in[None] + jnp.stack(zero_before)
    y_out = lift_decay[:, :, :, None] * jnp.einsum(
        "khpn,ktn->kthp", state_before, c_blocks, precision=precise
    )
    raw_out = (y_in + y_out).reshape(t_dev, H, P_SIZE)
    inv_rms = lax.rsqrt(jnp.mean(raw_out * raw_out, axis=-1, keepdims=True) + epsilon)
    normed = raw_out * inv_rms
    layer_out = (normed.reshape(t_dev, HP) * norm_gain[None, :] * valid_rows[:, None]).astype(
        jnp.bfloat16
    )
    d_normed = (g_out[0].astype(jnp.float32) * norm_gain[None, :] * valid_rows[:, None]).reshape(
        t_dev, H, P_SIZE
    )
    d_output = inv_rms * (d_normed - normed * jnp.mean(d_normed * normed, axis=-1, keepdims=True))
    d_blocks = d_output.reshape(groups, Q, H, P_SIZE)
    back_state = jnp.einsum(
        "kthp,ktn->khpn", d_blocks * lift_decay[:, :, :, None], c_blocks, precision=precise
    )
    zero_after = [jnp.zeros((H, P_SIZE, N), jnp.float32)]
    zero_start = jnp.exp(group_log[0])[:, None, None] * zero_after[0] + back_state[0]
    r_out = prefix_states(block_log, zero_start, True)
    trail_log = jnp.cumsum(group_log[::-1], axis=0)[::-1] - group_log
    grad_after = jnp.exp(trail_log)[:, :, None, None] * r_out[None] + jnp.stack(zero_after)
    d_inputs = jnp.einsum("khts,kthp->kshp", mixing, d_blocks, precision=precise)
    d_inputs = d_inputs + tail_decay[:, :, :, None] * jnp.einsum(
        "khpn,ksn->kshp", grad_after, b_blocks, precision=precise
    )
    pair_terms = weights * jnp.einsum("kthp,kshp->khts", d_blocks, x_blocks, precision=precise)
    d_c = jnp.einsum("khts,ksn->ktn", pair_terms, b_blocks, precision=precise)
    d_c = d_c + jnp.einsum(
        "kthp,khpn->ktn", d_blocks * lift_decay[:, :, :, None], state_before, precision=precise
    )
    d_b = jnp.einsum("khts,ktn->ksn", pair_terms, c_blocks, precision=precise)
    d_b = d_b + jnp.einsum(
        "kshp,khpn->ksn", x_blocks * tail_decay[:, :, :, None], grad_after, precision=precise
    )
    du_rows = d_inputs.reshape(t_dev, HP) * valid_rows[:, None]
    d_proj = jnp.concatenate(
        [du_rows, d_b.reshape(t_dev, N), d_c.reshape(t_dev, N)], axis=1
    ).astype(jnp.bfloat16)
    all_proj = lax.all_gather(d_proj, "cam").reshape(n_cam * t_dev, HP + 2 * N)
    width = D // n_cam
    w_mine = lax.dynamic_slice_in_dim(w_in, lax.axis_index("cam") * width, width, axis=0)
    d_embeds = lax.dot_general(
        all_proj, w_mine, (((1,), (1,)), ((), ())), preferred_element_type=jnp.float32
    ).astype(jnp.bfloat16).reshape(n_cam, t_dev, width)
    grad_scale = 1.0 / math.sqrt(n_cam * t_dev * n_tm)
    row_terms = grad_scale * lax.dot_general(
        embeds.reshape(n_cam * t_dev, width), all_proj, (((0,), (0,)), ((), ())), preferred_element_type=jnp.float32
    )
    d_w_in = lax.psum_scatter(row_terms, "tm", scatter_dimension=0, tiled=True)
    return (layer_out[None], d_embeds, d_w_in)


def solution(mesh):
    return jax.shard_map(
        on_device,
        mesh=mesh,
        in_specs=(
            P(None, "tm", "cam"),
            P(),
            P("cam", None, "tm"),
            P(),
            P("cam", None),
            P("cam"),
            P(),
            P("cam", "tm", None),
        ),
        out_specs=(P("cam", "tm", None), P(None, "tm", "cam"), P(("cam", "tm"), None)),
        check_vma=False,
    )
```

```python
import functools
import math

import jax
import jax.numpy as jnp
from jax import lax
from jax.experimental import pallas as pl
from jax.experimental.pallas import tpu as pltpu
from jax.sharding import PartitionSpec as P

D = 2048
H = 32
P_SIZE = 64
N = 128
Q = 128
HP = 2048


epsilon = 1e-05
precise = lax.Precision.HIGHEST
MESH = pl.DeviceIdType.MESH
NX, NY, NZ = 4, 4, 8


def prefix_states(block_log, state, reverse):
    size = lax.axis_size("tm")
    extra = jnp.broadcast_to(block_log[:, None, None], (H, 8, N))
    packed = jnp.concatenate([state, extra], axis=1)
    mine = lax.all_to_all(packed, "tm", split_axis=0, concat_axis=0, tiled=True)
    logs = mine[:, P_SIZE, 0]
    parts = mine[:, :P_SIZE].reshape(size, P_SIZE * N)
    cum = jnp.cumsum(logs)
    at = jnp.arange(size)
    if reverse:
        reach = at[None, :] > at[:, None]
        gap = (cum - logs)[None, :] - cum[:, None]
    else:
        reach = at[None, :] < at[:, None]
        gap = (cum - logs)[:, None] - cum[None, :]
    factors = jnp.where(reach, jnp.exp(jnp.where(reach, gap, 0.0)), 0.0)
    entered = jnp.dot(factors, parts, precision=precise).astype(jnp.bfloat16)
    entered = entered.reshape(size, P_SIZE, N)
    return lax.all_to_all(entered, "tm", split_axis=0, concat_axis=0, tiled=True).astype(jnp.float32)


def place():
    tm = lax.axis_index("tm")
    return tm // (2 * NY), (tm // 2) % NY, lax.axis_index("cam"), tm % 2


def at(x, y, z, core):
    return (z, (x * NY + y) * 2 + core)


def greet(peers):
    barrier = pltpu.get_barrier_semaphore()
    for peer in peers:
        pl.semaphore_signal(barrier, inc=1, device_id=peer, device_id_type=MESH)
    pl.semaphore_wait(barrier, len(peers))


def send(src, dst, sem_a, sem_b, peer):
    return pltpu.make_async_remote_copy(
        src_ref=src, dst_ref=dst, send_sem=sem_a, recv_sem=sem_b, device_id=peer, device_id_type=MESH
    )


def grad_kernel(scale, dp_ref, xt_ref, w_ref, emb_ref, dw_ref, wv, xg, pg, rows, s2, r2, s3, r3, own,
                w_sem, x_send, x_recv, p_send, p_recv, e_send, e_recv, send2, recv2, send3, recv3):
    x, y, z, core = place()
    half = dp_ref.shape[1] // 2
    width = wv.shape[1]
    t = dp_ref.shape[0]
    for j in range(NZ):
        c = (z + 1 + j) % NZ
        pltpu.make_async_copy(w_ref.at[pl.ds(pl.multiple_of(c * width, width), width)], wv.at[j], w_sem.at[j]).start()
    peers = []
    for j in range(1, NX):
        peers += [at((x + j) % NX, y, z, core), at((x + j) % NX, y, z, 1 - core)]
    for j in range(1, NY):
        peers += [at(x, (y + j) % NY, z, core), at(x, (y + j) % NY, z, 1 - core)]
    for j in range(1, NZ):
        peers += [at(x, y, (z + j) % NZ, core), at(x, y, (z + j) % NZ, 1 - core)]
    peers += [at(x, y, z, 1 - core)]
    greet(peers)

    def columns(color):
        return dp_ref.at[:, pl.ds(color * half, half)]

    def lanes(slot):
        return xg.at[:, :, pl.ds(pl.multiple_of(slot * t, t), t)]

    def x_line(j):
        k, slot = (x + j) % NX, x * 2 + core
        peer = at(k, y, z, 0)
        return (send(xt_ref.at[k], lanes(slot), x_send.at[0, j], x_recv.at[slot], peer),
                send(columns(0), pg.at[slot], p_send.at[0, j], p_recv.at[slot], peer))

    def y_line(j):
        k, slot = (y + j) % NY, y * 2 + core
        peer = at(x, k, z, 1)
        return (send(xt_ref.at[:, k], lanes(slot), x_send.at[1, j], x_recv.at[slot], peer),
                send(columns(1), pg.at[slot], p_send.at[1, j], p_recv.at[slot], peer))

    for j in (2, 1, 3):
        for copy in x_line(j) + y_line(j):
            copy.start()

    @pl.when(core == 0)
    def _():
        for copy in y_line(0):
            copy.start()
        pltpu.make_async_copy(xt_ref.at[x], lanes(x * 2), x_recv.at[x * 2]).start()
        pltpu.make_async_copy(columns(0), pg.at[x * 2], p_recv.at[x * 2]).start()

    @pl.when(core == 1)
    def _():
        for copy in x_line(0):
            copy.start()
        pltpu.make_async_copy(xt_ref.at[:, y], lanes(y * 2 + 1), x_recv.at[y * 2 + 1]).start()
        pltpu.make_async_copy(columns(1), pg.at[y * 2 + 1], p_recv.at[y * 2 + 1]).start()

    def emb_copy(j):
        return send(rows.at[j], emb_ref.at[z], e_send.at[j], e_recv.at[j], at(x, y, (z + 1 + j) % NZ, core))

    emb_home = pltpu.make_async_copy(rows.at[NZ - 1], emb_ref.at[z], e_send.at[NZ - 1])
    for j in range(NZ):
        pltpu.make_async_copy(w_ref.at[pl.ds(0, width)], wv.at[j], w_sem.at[j]).wait()
        rows[j] = lax.dot_general(
            dp_ref[...], wv[j], (((1,), (1,)), ((), ())), preferred_element_type=jnp.float32
        ).astype(jnp.bfloat16)
        if j < NZ - 1:
            emb_copy(j).start()
        else:
            emb_home.start()

    for slot in range(8):
        pltpu.make_async_copy(xt_ref.at[0], lanes(slot), x_recv.at[slot]).wait()
        pltpu.make_async_copy(columns(0), pg.at[slot], p_recv.at[slot]).wait()

    p = (1 - core) * y + core * x

    def second(j):
        k = (p + 1 + j) % NX
        peer = at((1 - core) * x + core * k, (1 - core) * k + core * y, z, core)
        return send(s2.at[j], r2.at[j], send2.at[j], recv2.at[j], peer)

    right = pg[...].reshape(8 * t, half)
    for j in range(NX):
        k = (p + 1 + j) % NX
        part = jnp.dot(xg[k], right, preferred_element_type=jnp.float32)
        if j < NX - 1:
            s2[j] = part.astype(jnp.bfloat16)
            second(j).start()
        else:
            own[...] = part
    for j in range(NX - 1):
        second(j).wait_recv()
    total = own[...] + r2[0].astype(jnp.float32) + r2[1].astype(jnp.float32) + r2[2].astype(jnp.float32)
    total = (total * scale).astype(jnp.float32)
    own[...] = total
    me = z * 2 + core
    for slot in range(2 * NZ):
        s3[slot] = own[8 * slot:8 * slot + 8].astype(jnp.bfloat16)

    def third(j):
        slot = (me + j) % (2 * NZ)
        return send(s3.at[slot], r3.at[me], send3.at[j], recv3.at[me], at(x, y, slot // 2, slot % 2))

    for j in range(1, 2 * NZ):
        third(j).start()
    r3[me] = s3[me]
    for j in range(1, 2 * NZ):
        slot = (me + j) % (2 * NZ)
        send(s3.at[0], r3.at[slot], send3.at[j], recv3.at[slot], at(x, y, slot // 2, slot % 2)).wait_recv()
    for color in range(2):
        acc = r3[color].astype(jnp.float32)
        for c in range(1, NZ):
            acc = acc + r3[2 * c + color].astype(jnp.float32)
        dw_ref[:, color * half:(color + 1) * half] = acc

    for j in range(1, NX):
        for copy in x_line(j) + y_line(j):
            copy.wait_send()

    @pl.when(core == 0)
    def _():
        for copy in y_line(0):
            copy.wait_send()

    @pl.when(core == 1)
    def _():
        for copy in x_line(0):
            copy.wait_send()

    for j in range(NX - 1):
        second(j).wait_send()
    for j in range(1, 2 * NZ):
        third(j).wait_send()
    for j in range(NZ - 1):
        emb_copy(j).wait_send()
    for j in range(NZ - 1):
        emb_copy(j).wait_recv()
    emb_home.wait()


def grads(d_proj, x_rows, w_in, scale):
    t, e = d_proj.shape
    d = x_rows.shape[1]
    half, width, part = e // 2, d // NZ, d // NX // NY
    xt = x_rows.T.reshape(NZ, NX, NY, part // NZ, t).transpose(1, 2, 0, 3, 4).reshape(NX, NY, part, t)
    dma = pltpu.SemaphoreType.DMA
    vmem = pl.BlockSpec(memory_space=pltpu.VMEM)
    hbm = pl.BlockSpec(memory_space=pl.ANY)
    return pl.pallas_call(
        functools.partial(grad_kernel, scale),
        name="grads",
        out_shape=(jax.ShapeDtypeStruct((NZ, t, width), jnp.bfloat16),
                   jax.ShapeDtypeStruct((part // NZ // 2, e), jnp.float32)),
        in_specs=[vmem, vmem, hbm],
        out_specs=(hbm, vmem),
        scratch_shapes=[
            pltpu.VMEM((NZ, width, e), jnp.bfloat16),
            pltpu.VMEM((NX, part, 8 * t), jnp.bfloat16),
            pltpu.VMEM((8, t, half), jnp.bfloat16),
            pltpu.VMEM((NZ, t, width), jnp.bfloat16),
            pltpu.VMEM((NX - 1, part, half), jnp.bfloat16),
            pltpu.VMEM((NX - 1, part, half), jnp.bfloat16),
            pltpu.VMEM((2 * NZ, part // NZ // 2, half), jnp.bfloat16),
            pltpu.VMEM((2 * NZ, part // NZ // 2, half), jnp.bfloat16),
            pltpu.VMEM((part, half), jnp.float32),
            dma((NZ,)), dma((2, NX)), dma((8,)), dma((2, NX)), dma((8,)), dma((NZ,)), dma((NZ,)),
            dma((NX,)), dma((NX,)), dma((2 * NZ,)), dma((2 * NZ,)),
        ],
        compiler_params=pltpu.CompilerParams(collective_id=0, has_side_effects=True, vmem_limit_bytes=60 * 1024 * 1024),
    )(d_proj, xt, w_in)


def on_device(embeds, w_in, log_decay, clip_keep, clip_starts, valid_len, norm_gain, g_out):
    n_cam = lax.axis_size("cam")
    n_tm = lax.axis_size("tm")
    t_dev = embeds.shape[1]
    groups = t_dev // Q
    x_rows = lax.all_to_all(embeds, "cam", split_axis=0, concat_axis=2, tiled=True)[0]
    projected = jnp.dot(x_rows, w_in, preferred_element_type=jnp.float32).astype(jnp.bfloat16)
    positions = lax.axis_index("tm") * t_dev + jnp.arange(t_dev, dtype=jnp.int32)
    is_start = jnp.any(positions[:, None] == clip_starts[0][None, :], axis=1)
    log_rates = log_decay[0] + jnp.where(is_start[None, :], jnp.log(clip_keep)[:, None], 0.0)
    valid_rows = (positions < valid_len[0]).astype(jnp.float32)
    proj_float = projected.astype(jnp.float32)
    x_blocks = (proj_float[:, :HP].reshape(t_dev, H, P_SIZE) * valid_rows[:, None, None]).reshape(
        groups, Q, H, P_SIZE
    )
    b_blocks = proj_float[:, HP : HP + N].reshape(groups, Q, N)
    c_blocks = proj_float[:, HP + N :].reshape(groups, Q, N)
    cum_rate = jnp.cumsum(log_rates.reshape(H, groups, Q), axis=2).transpose(1, 0, 2)
    group_log = cum_rate[:, :, -1]
    causal = jnp.arange(Q)[:, None] >= jnp.arange(Q)[None, :]
    gaps = cum_rate[:, :, :, None] - cum_rate[:, :, None, :]
    weights = jnp.where(causal, jnp.exp(jnp.where(causal, gaps, 0.0)), 0.0)
    scores = jnp.einsum("ktn,ksn->kts", c_blocks, b_blocks, precision=precise)
    mixing = weights * scores[:, None]
    y_in = jnp.einsum("khts,kshp->kthp", mixing, x_blocks, precision=precise)
    tail_decay = jnp.exp(group_log[:, :, None] - cum_rate).transpose(0, 2, 1)
    lift_decay = jnp.exp(cum_rate).transpose(0, 2, 1)
    local_state = jnp.einsum(
        "kshp,ksn->khpn", x_blocks * tail_decay[:, :, :, None], b_blocks, precision=precise
    )
    zero_before = [jnp.zeros((H, P_SIZE, N), jnp.float32)]
    zero_end = jnp.exp(group_log[-1])[:, None, None] * zero_before[-1] + local_state[-1]
    block_log = jnp.sum(group_log, axis=0)
    s_in = prefix_states(block_log, zero_end, False)
    lead_log = jnp.cumsum(group_log, axis=0) - group_log
    state_before = jnp.exp(lead_log)[:, :, None, None] * s_in[None] + jnp.stack(zero_before)
    y_out = lift_decay[:, :, :, None] * jnp.einsum(
        "khpn,ktn->kthp", state_before, c_blocks, precision=precise
    )
    raw_out = (y_in + y_out).reshape(t_dev, H, P_SIZE)
    inv_rms = lax.rsqrt(jnp.mean(raw_out * raw_out, axis=-1, keepdims=True) + epsilon)
    normed = raw_out * inv_rms
    layer_out = (normed.reshape(t_dev, HP) * norm_gain[None, :] * valid_rows[:, None]).astype(
        jnp.bfloat16
    )
    d_normed = (g_out[0].astype(jnp.float32) * norm_gain[None, :] * valid_rows[:, None]).reshape(
        t_dev, H, P_SIZE
    )
    d_output = inv_rms * (d_normed - normed * jnp.mean(d_normed * normed, axis=-1, keepdims=True))
    d_blocks = d_output.reshape(groups, Q, H, P_SIZE)
    back_state = jnp.einsum(
        "kthp,ktn->khpn", d_blocks * lift_decay[:, :, :, None], c_blocks, precision=precise
    )
    zero_after = [jnp.zeros((H, P_SIZE, N), jnp.float32)]
    zero_start = jnp.exp(group_log[0])[:, None, None] * zero_after[0] + back_state[0]
    r_out = prefix_states(block_log, zero_start, True)
    trail_log = jnp.cumsum(group_log[::-1], axis=0)[::-1] - group_log
    grad_after = jnp.exp(trail_log)[:, :, None, None] * r_out[None] + jnp.stack(zero_after)
    d_inputs = jnp.einsum("khts,kthp->kshp", mixing, d_blocks, precision=precise)
    d_inputs = d_inputs + tail_decay[:, :, :, None] * jnp.einsum(
        "khpn,ksn->kshp", grad_after, b_blocks, precision=precise
    )
    pair_terms = weights * jnp.einsum("kthp,kshp->khts", d_blocks, x_blocks, precision=precise)
    d_c = jnp.einsum("khts,ksn->ktn", pair_terms, b_blocks, precision=precise)
    d_c = d_c + jnp.einsum(
        "kthp,khpn->ktn", d_blocks * lift_decay[:, :, :, None], state_before, precision=precise
    )
    d_b = jnp.einsum("khts,ktn->ksn", pair_terms, c_blocks, precision=precise)
    d_b = d_b + jnp.einsum(
        "kshp,khpn->ksn", x_blocks * tail_decay[:, :, :, None], grad_after, precision=precise
    )
    du_rows = d_inputs.reshape(t_dev, HP) * valid_rows[:, None]
    d_proj = jnp.concatenate(
        [du_rows, d_b.reshape(t_dev, N), d_c.reshape(t_dev, N)], axis=1
    ).astype(jnp.bfloat16)
    grad_scale = 1.0 / math.sqrt(n_cam * t_dev * n_tm)
    d_embeds, d_w_in = grads(d_proj, x_rows, w_in, grad_scale)
    return (layer_out[None], d_embeds, d_w_in)


def solution(mesh):
    return jax.shard_map(
        on_device,
        mesh=mesh,
        in_specs=(
            P(None, "tm", "cam"),
            P(),
            P("cam", None, "tm"),
            P(),
            P("cam", None),
            P("cam"),
            P(),
            P("cam", "tm", None),
        ),
        out_specs=(P("cam", "tm", None), P(None, "tm", "cam"), P(("cam", "tm"), None)),
        check_vma=False,
    )
```

```python
import functools
import math

import jax
import jax.numpy as jnp
from jax import lax
from jax.experimental import pallas as pl
from jax.experimental.pallas import tpu as pltpu
from jax.sharding import PartitionSpec as P

D = 2048
H = 32
P_SIZE = 64
N = 128
Q = 128
HP = 2048


epsilon = 1e-05
MESH = pl.DeviceIdType.MESH
NX, NY, NZ = 4, 4, 8


def place():
    tm = lax.axis_index("tm")
    return tm // (2 * NY), (tm // 2) % NY, lax.axis_index("cam"), tm % 2


def at(x, y, z, core):
    return (z, (x * NY + y) * 2 + core)


def greet(peers):
    barrier = pltpu.get_barrier_semaphore()
    for peer in peers:
        pl.semaphore_signal(barrier, inc=1, device_id=peer, device_id_type=MESH)
    pl.semaphore_wait(barrier, len(peers))


def send(src, dst, sem_a, sem_b, peer):
    return pltpu.make_async_remote_copy(
        src_ref=src, dst_ref=dst, send_sem=sem_a, recv_sem=sem_b, device_id=peer, device_id_type=MESH
    )


def grad_kernel(scale, dp_ref, xt_ref, w_ref, emb_ref, dw_ref, wv, xg, pg, rows, s2, r2, s3, r3, own,
                w_sem, x_send, x_recv, p_send, p_recv, e_send, e_recv, send2, recv2, send3, recv3):
    x, y, z, core = place()
    half = dp_ref.shape[1] // 2
    width = wv.shape[1]
    t = dp_ref.shape[0]
    for j in range(NZ):
        c = (z + 1 + j) % NZ
        pltpu.make_async_copy(w_ref.at[pl.ds(pl.multiple_of(c * width, width), width)], wv.at[j], w_sem.at[j]).start()
    peers = []
    for j in range(1, NX):
        peers += [at((x + j) % NX, y, z, core), at((x + j) % NX, y, z, 1 - core)]
    for j in range(1, NY):
        peers += [at(x, (y + j) % NY, z, core), at(x, (y + j) % NY, z, 1 - core)]
    for j in range(1, NZ):
        peers += [at(x, y, (z + j) % NZ, core), at(x, y, (z + j) % NZ, 1 - core)]
    peers += [at(x, y, z, 1 - core)]
    greet(peers)

    def columns(color):
        return dp_ref.at[:, pl.ds(color * half, half)]

    def lanes(slot):
        return xg.at[:, :, pl.ds(pl.multiple_of(slot * t, t), t)]

    def x_line(j):
        k, slot = (x + j) % NX, x * 2 + core
        peer = at(k, y, z, 0)
        return (send(xt_ref.at[k], lanes(slot), x_send.at[0, j], x_recv.at[slot], peer),
                send(columns(0), pg.at[slot], p_send.at[0, j], p_recv.at[slot], peer))

    def y_line(j):
        k, slot = (y + j) % NY, y * 2 + core
        peer = at(x, k, z, 1)
        return (send(xt_ref.at[:, k], lanes(slot), x_send.at[1, j], x_recv.at[slot], peer),
                send(columns(1), pg.at[slot], p_send.at[1, j], p_recv.at[slot], peer))

    for j in (2, 1, 3):
        for copy in x_line(j) + y_line(j):
            copy.start()

    @pl.when(core == 0)
    def _():
        for copy in y_line(0):
            copy.start()
        pltpu.make_async_copy(xt_ref.at[x], lanes(x * 2), x_recv.at[x * 2]).start()
        pltpu.make_async_copy(columns(0), pg.at[x * 2], p_recv.at[x * 2]).start()

    @pl.when(core == 1)
    def _():
        for copy in x_line(0):
            copy.start()
        pltpu.make_async_copy(xt_ref.at[:, y], lanes(y * 2 + 1), x_recv.at[y * 2 + 1]).start()
        pltpu.make_async_copy(columns(1), pg.at[y * 2 + 1], p_recv.at[y * 2 + 1]).start()

    def emb_copy(j):
        return send(rows.at[j], emb_ref.at[z], e_send.at[j], e_recv.at[j], at(x, y, (z + 1 + j) % NZ, core))

    emb_home = pltpu.make_async_copy(rows.at[NZ - 1], emb_ref.at[z], e_send.at[NZ - 1])
    for j in range(NZ):
        pltpu.make_async_copy(w_ref.at[pl.ds(0, width)], wv.at[j], w_sem.at[j]).wait()
        rows[j] = lax.dot_general(
            dp_ref[...], wv[j], (((1,), (1,)), ((), ())), preferred_element_type=jnp.float32
        ).astype(jnp.bfloat16)
        if j < NZ - 1:
            emb_copy(j).start()
        else:
            emb_home.start()

    for slot in range(8):
        pltpu.make_async_copy(xt_ref.at[0], lanes(slot), x_recv.at[slot]).wait()
        pltpu.make_async_copy(columns(0), pg.at[slot], p_recv.at[slot]).wait()

    p = (1 - core) * y + core * x

    def second(j):
        k = (p + 1 + j) % NX
        peer = at((1 - core) * x + core * k, (1 - core) * k + core * y, z, core)
        return send(s2.at[j], r2.at[j], send2.at[j], recv2.at[j], peer)

    right = pg[...].reshape(8 * t, half)
    for j in range(NX):
        k = (p + 1 + j) % NX
        part = jnp.dot(xg[k], right, preferred_element_type=jnp.float32)
        if j < NX - 1:
            s2[j] = part.astype(jnp.bfloat16)
            second(j).start()
        else:
            own[...] = part
    for j in range(NX - 1):
        second(j).wait_recv()
    total = own[...] + r2[0].astype(jnp.float32) + r2[1].astype(jnp.float32) + r2[2].astype(jnp.float32)
    total = (total * scale).astype(jnp.float32)
    own[...] = total
    me = z * 2 + core
    for slot in range(2 * NZ):
        s3[slot] = own[8 * slot:8 * slot + 8].astype(jnp.bfloat16)

    def third(j):
        slot = (me + j) % (2 * NZ)
        return send(s3.at[slot], r3.at[me], send3.at[j], recv3.at[me], at(x, y, slot // 2, slot % 2))

    for j in range(1, 2 * NZ):
        third(j).start()
    r3[me] = s3[me]
    for j in range(1, 2 * NZ):
        slot = (me + j) % (2 * NZ)
        send(s3.at[0], r3.at[slot], send3.at[j], recv3.at[slot], at(x, y, slot // 2, slot % 2)).wait_recv()
    for color in range(2):
        acc = r3[color].astype(jnp.float32)
        for c in range(1, NZ):
            acc = acc + r3[2 * c + color].astype(jnp.float32)
        dw_ref[:, color * half:(color + 1) * half] = acc

    for j in range(1, NX):
        for copy in x_line(j) + y_line(j):
            copy.wait_send()

    @pl.when(core == 0)
    def _():
        for copy in y_line(0):
            copy.wait_send()

    @pl.when(core == 1)
    def _():
        for copy in x_line(0):
            copy.wait_send()

    for j in range(NX - 1):
        second(j).wait_send()
    for j in range(1, 2 * NZ):
        third(j).wait_send()
    for j in range(NZ - 1):
        emb_copy(j).wait_send()
    for j in range(NZ - 1):
        emb_copy(j).wait_recv()
    emb_home.wait()


def grads(d_proj, x_rows, w_in, scale):
    t, e = d_proj.shape
    d = x_rows.shape[1]
    half, width, part = e // 2, d // NZ, d // NX // NY
    xt = x_rows.T.reshape(NZ, NX, NY, part // NZ, t).transpose(1, 2, 0, 3, 4).reshape(NX, NY, part, t)
    dma = pltpu.SemaphoreType.DMA
    vmem = pl.BlockSpec(memory_space=pltpu.VMEM)
    hbm = pl.BlockSpec(memory_space=pl.ANY)
    return pl.pallas_call(
        functools.partial(grad_kernel, scale),
        name="grads",
        out_shape=(jax.ShapeDtypeStruct((NZ, t, width), jnp.bfloat16),
                   jax.ShapeDtypeStruct((part // NZ // 2, e), jnp.float32)),
        in_specs=[vmem, vmem, hbm],
        out_specs=(hbm, vmem),
        scratch_shapes=[
            pltpu.VMEM((NZ, width, e), jnp.bfloat16),
            pltpu.VMEM((NX, part, 8 * t), jnp.bfloat16),
            pltpu.VMEM((8, t, half), jnp.bfloat16),
            pltpu.VMEM((NZ, t, width), jnp.bfloat16),
            pltpu.VMEM((NX - 1, part, half), jnp.bfloat16),
            pltpu.VMEM((NX - 1, part, half), jnp.bfloat16),
            pltpu.VMEM((2 * NZ, part // NZ // 2, half), jnp.bfloat16),
            pltpu.VMEM((2 * NZ, part // NZ // 2, half), jnp.bfloat16),
            pltpu.VMEM((part, half), jnp.float32),
            dma((NZ,)), dma((2, NX)), dma((8,)), dma((2, NX)), dma((8,)), dma((NZ,)), dma((NZ,)),
            dma((NX,)), dma((NX,)), dma((2 * NZ,)), dma((2 * NZ,)),
        ],
        compiler_params=pltpu.CompilerParams(collective_id=0, has_side_effects=True, vmem_limit_bytes=60 * 1024 * 1024),
    )(d_proj, xt, w_in)


def scan_kernel(lg_ref, w_ref, cum_ref, valid_ref, proj_ref, xt_ref, gt_ref, gain_ref, out_ref, dp_ref,
                tail, lift, xw, mix, yin, dt, dl, din, lot, lgot, snd1, got1, snd2, sin, snd3, got3, snd4, rin,
                l_send, l_recv, send1, recv1, send2, recv2, send3, recv3, send4, recv4):
    heads = H
    f32, b16 = jnp.float32, jnp.bfloat16
    me, cam = lax.axis_index("tm"), lax.axis_index("cam")
    n_tm = 2 * NX * NY
    hp = heads * P_SIZE
    barrier = pltpu.get_barrier_semaphore()

    def greet_one(j, _):
        pl.semaphore_signal(barrier, inc=1, device_id=(cam, (me + j) % n_tm), device_id_type=MESH)
        return 0

    lax.fori_loop(1, n_tm, greet_one, 0)
    pl.semaphore_wait(barrier, n_tm - 1)

    def exchange(src, dst, sem_a, sem_b):
        def copy(j):
            peer = (me + j) % n_tm
            return send(src.at[peer], dst.at[me], sem_a.at[j], sem_b.at[j], (cam, peer))

        def start():
            def body(j, _):
                copy(j).start()
                return 0
            lax.fori_loop(1, n_tm, body, 0)
            dst[me] = src[me]

        def arrive():
            def body(j, _):
                copy(j).wait_recv()
                return 0
            lax.fori_loop(1, n_tm, body, 0)

        def sent():
            def body(j, _):
                copy(j).wait_send()
                return 0
            lax.fori_loop(1, n_tm, body, 0)
        return start, arrive, sent

    logs = exchange(lg_ref, lgot, l_send, l_recv)
    fwd_out = exchange(snd1, got1, send1, recv1)
    fwd_back = exchange(snd2, sin, send2, recv2)
    bwd_out = exchange(snd3, got3, send3, recv3)
    bwd_back = exchange(snd4, rin, send4, recv4)
    logs[0]()

    b_nat, c_nat = proj_ref[:, hp:hp + N], proj_ref[:, hp + N:hp + 2 * N]
    b_t, c_t = xt_ref[hp:hp + N], xt_ref[hp + N:hp + 2 * N]
    cum = cum_ref[...]
    tail[...] = jnp.exp(cum[:, Q - 1:Q] - cum)
    lift[...] = jnp.exp(cum)
    valid = valid_ref[0:1]
    group = 4
    steps = heads // group

    def dot(a, b):
        return jnp.dot(a, b, preferred_element_type=f32)

    def dot_t(a, b):
        return lax.dot_general(a, b, (((1,), (1,)), ((), ())), preferred_element_type=f32)

    def t_dot(a, b):
        return lax.dot_general(a, b, (((0,), (0,)), ((), ())), preferred_element_type=f32)

    def each(body, init=0):
        return lax.fori_loop(0, steps, body, init)

    def rows(g, i):
        return pl.ds(pl.multiple_of((g * group + i) * P_SIZE, P_SIZE), P_SIZE)

    def local_states(g, _):
        for i in range(group):
            h = g * group + i
            xw[h] = (xt_ref[rows(g, i)].astype(f32) * tail[pl.ds(h, 1)]).astype(b16)
        states = dot(xw[pl.ds(g * group, group)].reshape(group * P_SIZE, Q), b_nat)
        snd1[pl.ds(g * group, group)] = states.astype(b16).reshape(group, P_SIZE, N)
        return 0

    each(local_states)
    fwd_out[0]()

    scores = dot(b_nat, c_t)

    def inside(g, _):
        for i in range(group):
            h = g * group + i
            mix[h] = (w_ref[h] * scores).astype(b16)
            yin[h] = dot(xt_ref[rows(g, i)], mix[h])
        return 0

    each(inside)
    logs[1]()
    fwd_out[1]()

    def scan(parts, out, reverse):
        def body(k, state):
            i = n_tm - 1 - k if reverse else k
            out[i] = state.astype(b16).reshape(P_SIZE, N)
            decay = jnp.exp(lgot[i])
            return decay[None] * state + parts[i].astype(f32).reshape(P_SIZE // 8, 8, N)
        lax.fori_loop(0, n_tm, body, jnp.zeros((P_SIZE // 8, 8, N), f32))

    scan(got1, snd2, False)
    fwd_back[0]()
    fwd_back[1]()

    def norm_step(g, _):
        carried = dot(sin[pl.ds(g * group, group)].reshape(group * P_SIZE, N), c_t)
        for i in range(group):
            h = g * group + i
            up = lift[pl.ds(h, 1)]
            raw = yin[h] + up * carried[i * P_SIZE:(i + 1) * P_SIZE]
            inv = lax.rsqrt(jnp.mean(raw * raw, axis=0, keepdims=True) + epsilon)
            normed = raw * inv
            gain = gain_ref[rows(g, i)] * valid
            lot[rows(g, i)] = normed * gain
            d_normed = gt_ref[rows(g, i)].astype(f32) * gain
            d_out = inv * (d_normed - normed * jnp.mean(d_normed * normed, axis=0, keepdims=True))
            dt[h] = d_out.astype(b16)
            dl[h] = (d_out * up).astype(b16)
        states = dot(dl[pl.ds(g * group, group)].reshape(group * P_SIZE, Q), c_nat)
        snd3[pl.ds(g * group, group)] = states.astype(b16).reshape(group, P_SIZE, N)
        return 0

    each(norm_step)
    bwd_out[0]()

    first = lax.broadcasted_iota(jnp.int32, (2 * P_SIZE, Q), 0) < P_SIZE

    def pairs(g, total):
        for i in range(0, group, 2):
            h = g * group + i
            d_two = dt[pl.ds(h, 2)].reshape(2 * P_SIZE, Q)
            zero = jnp.zeros_like(d_two)
            spread = jnp.concatenate([jnp.where(first, d_two, zero), jnp.where(first, zero, d_two)], axis=1)
            x_two = proj_ref[:, pl.ds(pl.multiple_of(h * P_SIZE, 2 * P_SIZE), 2 * P_SIZE)]
            both = dot(x_two, spread)
            total = total + w_ref[h] * both[:, :Q] + w_ref[h + 1] * both[:, Q:]
            din[h] = dot_t(dt[h], mix[h])
            din[h + 1] = dot_t(dt[h + 1], mix[h + 1])
        return total

    pair_sum = each(pairs, jnp.zeros((Q, Q), f32)).astype(b16)
    d_c = t_dot(pair_sum, b_nat) + t_dot(dl[...].reshape(hp, Q), sin[...].reshape(hp, N))
    d_b = dot(pair_sum, c_nat)
    dp_ref[:, hp + N:hp + 2 * N] = d_c.astype(b16)
    for k in range(hp // Q):
        out_ref[:, k * Q:(k + 1) * Q] = lot[k * Q:(k + 1) * Q].T.astype(b16)
    bwd_out[1]()
    scan(got3, snd4, True)
    bwd_back[0]()
    bwd_back[1]()
    d_b = d_b + t_dot(xw[...].reshape(hp, Q), rin[...].reshape(hp, N))
    dp_ref[:, hp:hp + N] = d_b.astype(b16)
    for k in range(heads // 2):
        after = dot(rin[2 * k:2 * k + 2].reshape(2 * P_SIZE, N), b_t)
        two = [din[2 * k + i] + tail[2 * k + i:2 * k + i + 1] * after[i * P_SIZE:(i + 1) * P_SIZE] for i in range(2)]
        dp_ref[:, k * Q:(k + 1) * Q] = (jnp.concatenate(two, axis=0) * valid).T.astype(b16)
    for _, _, sent in (logs, fwd_out, fwd_back, bwd_out, bwd_back):
        sent()


def scan_both(lg, weights, cum, valid, proj, proj_t, g_t, gain):
    n_tm = lg.shape[0]
    hp = H * P_SIZE
    dma = pltpu.SemaphoreType.DMA
    vmem = pl.BlockSpec(memory_space=pltpu.VMEM)
    f32, b16 = jnp.float32, jnp.bfloat16
    states = pltpu.VMEM((n_tm, P_SIZE, N), b16)
    return pl.pallas_call(
        scan_kernel,
        name="scan_both",
        out_shape=(jax.ShapeDtypeStruct((Q, hp), b16), jax.ShapeDtypeStruct((Q, hp + 2 * N), b16)),
        in_specs=[vmem] * 8,
        out_specs=(vmem, vmem),
        scratch_shapes=[
            pltpu.VMEM((H, Q), f32), pltpu.VMEM((H, Q), f32),
            pltpu.VMEM((H, P_SIZE, Q), b16), pltpu.VMEM((H, Q, Q), b16), pltpu.VMEM((H, P_SIZE, Q), f32),
            pltpu.VMEM((H, P_SIZE, Q), b16), pltpu.VMEM((H, P_SIZE, Q), b16), pltpu.VMEM((H, P_SIZE, Q), f32),
            pltpu.VMEM((hp, Q), f32), pltpu.VMEM((n_tm, 8, N), f32),
        ] + [states] * 8 + [dma((n_tm,))] * 10,
        compiler_params=pltpu.CompilerParams(collective_id=1, has_side_effects=True, vmem_limit_bytes=60 * 1024 * 1024),
    )(lg, weights, cum, valid, proj, proj_t, g_t, gain)


def on_device(embeds, w_in, log_decay, clip_keep, clip_starts, valid_len, norm_gain, g_out):
    n_cam = lax.axis_size("cam")
    n_tm = lax.axis_size("tm")
    t_dev = embeds.shape[1]
    x_rows = lax.all_to_all(embeds, "cam", split_axis=0, concat_axis=2, tiled=True)[0]
    projected = jnp.dot(x_rows, w_in, preferred_element_type=jnp.float32).astype(jnp.bfloat16)
    positions = lax.axis_index("tm") * t_dev + jnp.arange(t_dev, dtype=jnp.int32)
    is_start = jnp.any(positions[:, None] == clip_starts[0][None, :], axis=1)
    log_rates = log_decay[0] + jnp.where(is_start[None, :], jnp.log(clip_keep)[:, None], 0.0)
    valid_rows = (positions < valid_len[0]).astype(jnp.float32)
    cum_rate = jnp.cumsum(log_rates, axis=1)
    lg = jnp.broadcast_to(cum_rate[:, -1][:, None, None], (H, 8, N))
    causal = jnp.arange(Q)[:, None] <= jnp.arange(Q)[None, :]
    gaps = cum_rate[:, None, :] - cum_rate[:, :, None]
    weights = jnp.where(causal, jnp.exp(jnp.where(causal, gaps, 0.0)), 0.0)
    keep = jnp.where(jnp.arange(HP + 2 * N)[None, :] < HP, valid_rows[:, None], 1.0)
    proj = (projected.astype(jnp.float32) * keep).astype(jnp.bfloat16)
    gain = jnp.broadcast_to(norm_gain[:, None], (HP, Q))
    valid = jnp.broadcast_to(valid_rows[None, :], (8, Q))
    layer_out, d_proj = scan_both(lg, weights, cum_rate, valid, proj, proj.T, g_out[0].T, gain)
    grad_scale = 1.0 / math.sqrt(n_cam * t_dev * n_tm)
    d_embeds, d_w_in = grads(d_proj, x_rows, w_in, grad_scale)
    return (layer_out[None], d_embeds, d_w_in)


def solution(mesh):
    return jax.shard_map(
        on_device,
        mesh=mesh,
        in_specs=(
            P(None, "tm", "cam"),
            P(),
            P("cam", None, "tm"),
            P(),
            P("cam", None),
            P("cam"),
            P(),
            P("cam", "tm", None),
        ),
        out_specs=(P("cam", "tm", None), P(None, "tm", "cam"), P(("cam", "tm"), None)),
        check_vma=False,
    )
```

```python
import functools
import math

import jax
import jax.numpy as jnp
from jax import lax
from jax.experimental import pallas as pl
from jax.experimental.pallas import tpu as pltpu
from jax.sharding import PartitionSpec as P

D = 2048
H = 32
P_SIZE = 64
N = 128
Q = 128
HP = 2048
NCLIP = 3


epsilon = 1e-05
MESH = pl.DeviceIdType.MESH
NX, NY, NZ = 4, 4, 8


def at(x, y, z, core):
    return (z, (x * NY + y) * 2 + core)


def send(src, dst, sem_a, sem_b, peer):
    return pltpu.make_async_remote_copy(
        src_ref=src, dst_ref=dst, send_sem=sem_a, recv_sem=sem_b, device_id=peer, device_id_type=MESH
    )


def loop(start, end, body):
    def step(k, _):
        body(k)
        return 0
    lax.fori_loop(start, end, step, 0)


def layer_kernel(scale, starts_ref, len_ref, emb_ref, w_ref, rate_ref, keep_ref, gain_ref, g_ref,
                 out_ref, demb_ref, dw_ref,
                 wv, xin, acc, proj, xt, xtp, gt, gain, wts, cum, tail, lift, tot,
                 xw, mix, yin, dt, dl, din, lot, lg, lgot, snd1, got1, snd2, sin, snd3, got3, snd4, rin,
                 dp, xg, pg, rows_out, s2, r2, s3, r3, own,
                 w_sem, a_send, a_recv,
                 l_send, l_recv, send1, recv1, send2, recv2, send3, recv3, send4, recv4,
                 x_send, x_recv, p_send, p_recv, e_send, e_recv, send5, recv5, send6, recv6):
    f32, b16 = jnp.float32, jnp.bfloat16
    me, z = lax.axis_index("tm"), lax.axis_index("cam")
    n_tm = 2 * NX * NY
    x, y, core = me // (2 * NY), (me // 2) % NY, me % 2
    hp = H * P_SIZE
    width = emb_ref.shape[2]
    half = dp.shape[1] // 2
    group = 4

    def w_copy(j):
        c = (z + NZ - 1 - j) % NZ
        return pltpu.make_async_copy(w_ref.at[pl.ds(pl.multiple_of(c * width, width), width)], wv.at[c], w_sem.at[j])

    barrier = pltpu.get_barrier_semaphore()

    def greet(peer):
        pl.semaphore_signal(barrier, inc=1, device_id=peer, device_id_type=MESH)

    loop(1, NZ, lambda j: greet(((z + j) % NZ, me)))
    loop(1, NZ, lambda j: greet(((z + j) % NZ, me + 1 - 2 * core)))
    loop(1, n_tm, lambda j: greet((z, (me + j) % n_tm)))
    for j in (7, 0, 6, 1, 5, 2, 4, 3):
        w_copy(j).start()

    def dot(a, b):
        return jnp.dot(a, b, preferred_element_type=f32)

    def dot_t(a, b):
        return lax.dot_general(a, b, (((1,), (1,)), ((), ())), preferred_element_type=f32)

    def t_dot(a, b):
        return lax.dot_general(a, b, (((0,), (0,)), ((), ())), preferred_element_type=f32)

    def lanes_of(shape):
        return lax.broadcasted_iota(jnp.int32, shape, len(shape) - 1)

    def subs_of(shape):
        return lax.broadcasted_iota(jnp.int32, shape, 0)

    base = me * Q
    here = lanes_of((1, Q)) + base
    is_start = here == starts_ref[0, 0]
    for k in range(1, NCLIP):
        is_start = is_start | (here == starts_ref[0, k])
    keep_log = jnp.log(keep_ref[...])
    keep_col = jnp.sum(jnp.where(lanes_of((H, H)) == subs_of((H, H)), keep_log, 0.0), axis=1, keepdims=True)
    rates = rate_ref[0] + jnp.where(is_start, keep_col, 0.0)
    upper = (subs_of((Q, Q)) <= lanes_of((Q, Q)))
    running = jnp.dot(rates, upper.astype(f32), precision=lax.Precision.HIGHEST, preferred_element_type=f32)
    cum[...] = running
    tail[...] = jnp.exp(running[:, Q - 1:Q] - running)
    lift[...] = jnp.exp(running)
    tot[...] = jnp.broadcast_to(running[:, Q - 1:Q], (H, Q))
    valid = (here < len_ref[0]).astype(f32)
    valid_col = (subs_of((Q, Q)) + base < len_ref[0])

    def logs_of(h):
        lg[h] = jnp.broadcast_to(tot[pl.ds(h, 1)], (8, Q))

    loop(0, H, logs_of)

    pl.semaphore_wait(barrier, 2 * (NZ - 1) + n_tm - 1)

    def a_copy(j):
        lanes = pl.ds(pl.multiple_of(z * width, width), width)
        return send(emb_ref.at[(z + 1 + j) % NZ], xin.at[:, lanes], a_send.at[j], a_recv.at[j], ((z + 1 + j) % NZ, me))

    def block(c):
        return xin.at[:, pl.ds(pl.multiple_of(c * width, width), width)]

    a_home = pltpu.make_async_copy(emb_ref.at[z], block(z), a_recv.at[NZ - 1])
    for j in (3, 2, 4, 1, 5, 0, 6):
        a_copy(j).start()
    a_home.start()

    def exchange(src, dst, sem_a, sem_b):
        def copy(j):
            peer = (me + j) % n_tm
            return send(src.at[peer], dst.at[me], sem_a.at[j], sem_b.at[j], (z, peer))

        def start():
            loop(1, n_tm, lambda j: copy(j).start())
            dst[me] = src[me]

        return (start, lambda: loop(1, n_tm, lambda j: copy(j).wait_recv()),
                lambda: loop(1, n_tm, lambda j: copy(j).wait_send()))

    logs = exchange(lg, lgot, l_send, l_recv)
    fwd_out = exchange(snd1, got1, send1, recv1)
    fwd_back = exchange(snd2, sin, send2, recv2)
    bwd_out = exchange(snd3, got3, send3, recv3)
    bwd_back = exchange(snd4, rin, send4, recv4)
    logs[0]()

    def weights_of(h):
        row = jnp.broadcast_to(cum[pl.ds(h, 1)], (Q, Q))
        wts[h] = jnp.where(upper, jnp.exp(jnp.where(upper, row - row.T, 0.0)), 0.0)

    loop(0, H, weights_of)

    def columns_of(k):
        part = pl.ds(pl.multiple_of(k * Q, Q), Q)
        gt[part] = g_ref[0, :, part].astype(f32).T.astype(b16)
        gain[part] = jnp.broadcast_to(gain_ref[pl.ds(k, 1)], (Q, Q)).T * valid

    loop(0, hp // Q, columns_of)

    piece = Q // (2 * NY)
    for n, j in enumerate((7, 0, 6, 1, 5, 2, 4, 3)):
        c = (z + NZ - 1 - j) % NZ
        w_copy(j).wait()
        if j == NZ - 1:
            a_home.wait()
            c = z
        else:
            a_copy(j).wait_recv()
        got = block(c)[...]
        term = dot(got, wv[c])
        if n == 0:
            acc[...] = term
        else:
            acc[...] += term
        for k in range(width // Q):
            turned = got[:, k * Q:(k + 1) * Q].astype(f32).T.astype(b16)
            for m in range(Q // piece):
                feature = k * Q + m * piece
                xtp[feature // (NY * piece), (feature // piece) % NY, pl.ds(pl.multiple_of(c * piece, piece), piece)] = (
                    turned[m * piece:(m + 1) * piece])

    def part_of(color):
        return dp.at[:, pl.ds(color * half, half)]

    def lanes(slot):
        return xg.at[:, :, pl.ds(pl.multiple_of(slot * Q, Q), Q)]

    def x_line(j):
        k, slot = (x + j) % NX, x * 2 + core
        peer = at(k, y, z, 0)
        return (send(xtp.at[k], lanes(slot), x_send.at[0, j], x_recv.at[slot], peer),
                send(part_of(0), pg.at[slot], p_send.at[0, j], p_recv.at[slot], peer))

    def y_line(j):
        k, slot = (y + j) % NY, y * 2 + core
        peer = at(x, k, z, 1)
        return (send(xtp.at[:, k], lanes(slot), x_send.at[1, j], x_recv.at[slot], peer),
                send(part_of(1), pg.at[slot], p_send.at[1, j], p_recv.at[slot], peer))

    def lines(what, act):
        for j in (2, 1, 3):
            act(x_line(j)[what])
            act(y_line(j)[what])

        @pl.when(core == 0)
        def _():
            act(y_line(0)[what])

        @pl.when(core == 1)
        def _():
            act(x_line(0)[what])

    lines(0, lambda copy: copy.start())

    @pl.when(core == 0)
    def _():
        pltpu.make_async_copy(xtp.at[x], lanes(x * 2), x_recv.at[x * 2]).start()

    @pl.when(core == 1)
    def _():
        pltpu.make_async_copy(xtp.at[:, y], lanes(y * 2 + 1), x_recv.at[y * 2 + 1]).start()

    for k in range((hp + 2 * N) // Q):
        part = acc[:, k * Q:(k + 1) * Q]
        if k < hp // Q:
            part = jnp.where(valid_col, part, 0.0)
        proj[:, k * Q:(k + 1) * Q] = part.astype(b16)
        xt[k * Q:(k + 1) * Q] = part.T.astype(b16)

    b_nat, c_nat = proj[:, hp:hp + N], proj[:, hp + N:hp + 2 * N]
    b_t, c_t = xt[hp:hp + N], xt[hp + N:hp + 2 * N]

    def rows(g, i):
        return pl.ds(pl.multiple_of((g * group + i) * P_SIZE, P_SIZE), P_SIZE)

    def local_states(g):
        for i in range(group):
            h = g * group + i
            xw[h] = (xt[rows(g, i)].astype(f32) * tail[pl.ds(h, 1)]).astype(b16)
        states = dot(xw[pl.ds(g * group, group)].reshape(group * P_SIZE, Q), b_nat)
        snd1[pl.ds(g * group, group)] = states.astype(b16).reshape(group, P_SIZE, N)

    loop(0, H // group, local_states)
    fwd_out[0]()

    scores = dot(b_nat, c_t)

    def inside(g):
        for i in range(group):
            h = g * group + i
            mix[h] = (wts[h] * scores).astype(b16)
            yin[h] = dot(xt[rows(g, i)], mix[h])

    loop(0, H // group, inside)
    logs[1]()
    fwd_out[1]()

    def scan(parts, out, reverse):
        def body(k, state):
            i = n_tm - 1 - k if reverse else k
            out[i] = state.astype(b16).reshape(P_SIZE, N)
            decay = jnp.exp(lgot[i])
            return decay[None] * state + parts[i].astype(f32).reshape(P_SIZE // 8, 8, N)
        lax.fori_loop(0, n_tm, body, jnp.zeros((P_SIZE // 8, 8, N), f32))

    scan(got1, snd2, False)
    fwd_back[0]()
    fwd_back[1]()

    def norm_step(g):
        carried = dot(sin[pl.ds(g * group, group)].reshape(group * P_SIZE, N), c_t)
        for i in range(group):
            h = g * group + i
            up = lift[pl.ds(h, 1)]
            raw = yin[h] + up * carried[i * P_SIZE:(i + 1) * P_SIZE]
            inv = lax.rsqrt(jnp.mean(raw * raw, axis=0, keepdims=True) + epsilon)
            normed = raw * inv
            scaled = gain[rows(g, i)]
            lot[rows(g, i)] = normed * scaled
            d_normed = gt[rows(g, i)].astype(f32) * scaled
            d_out = inv * (d_normed - normed * jnp.mean(d_normed * normed, axis=0, keepdims=True))
            dt[h] = d_out.astype(b16)
            dl[h] = (d_out * up).astype(b16)
        states = dot(dl[pl.ds(g * group, group)].reshape(group * P_SIZE, Q), c_nat)
        snd3[pl.ds(g * group, group)] = states.astype(b16).reshape(group, P_SIZE, N)

    loop(0, H // group, norm_step)
    bwd_out[0]()

    first = subs_of((2 * P_SIZE, Q)) < P_SIZE

    def pairs(g, total):
        for i in range(0, group, 2):
            h = g * group + i
            d_two = dt[pl.ds(h, 2)].reshape(2 * P_SIZE, Q)
            zero = jnp.zeros_like(d_two)
            spread = jnp.concatenate([jnp.where(first, d_two, zero), jnp.where(first, zero, d_two)], axis=1)
            x_two = proj[:, pl.ds(pl.multiple_of(h * P_SIZE, 2 * P_SIZE), 2 * P_SIZE)]
            both = dot(x_two, spread)
            total = total + wts[h] * both[:, :Q] + wts[h + 1] * both[:, Q:]
            din[h] = dot_t(dt[h], mix[h])
            din[h + 1] = dot_t(dt[h + 1], mix[h + 1])
        return total

    pair_sum = lax.fori_loop(0, H // group, pairs, jnp.zeros((Q, Q), f32)).astype(b16)
    bwd_out[1]()
    scan(got3, snd4, True)
    bwd_back[0]()
    d_c = t_dot(pair_sum, b_nat) + t_dot(dl[...].reshape(hp, Q), sin[...].reshape(hp, N))
    d_b = dot(pair_sum, c_nat)
    dp[:, hp + N:hp + 2 * N] = d_c.astype(b16)
    for k in range(hp // Q):
        out_ref[:, k * Q:(k + 1) * Q] = lot[k * Q:(k + 1) * Q].T.astype(b16)
    bwd_back[1]()
    d_b = d_b + t_dot(xw[...].reshape(hp, Q), rin[...].reshape(hp, N))
    dp[:, hp:hp + N] = d_b.astype(b16)
    for k in range(H // 2):
        after = dot(rin[2 * k:2 * k + 2].reshape(2 * P_SIZE, N), b_t)
        two = [din[2 * k + i] + tail[2 * k + i:2 * k + i + 1] * after[i * P_SIZE:(i + 1) * P_SIZE] for i in range(2)]
        dp[:, k * Q:(k + 1) * Q] = (jnp.concatenate(two, axis=0) * valid).T.astype(b16)

    lines(1, lambda copy: copy.start())

    @pl.when(core == 0)
    def _():
        pltpu.make_async_copy(part_of(0), pg.at[x * 2], p_recv.at[x * 2]).start()

    @pl.when(core == 1)
    def _():
        pltpu.make_async_copy(part_of(1), pg.at[y * 2 + 1], p_recv.at[y * 2 + 1]).start()

    def e_copy(j):
        return send(rows_out.at[j], demb_ref.at[z], e_send.at[j], e_recv.at[j], ((z + 1 + j) % NZ, me))

    e_home = pltpu.make_async_copy(rows_out.at[NZ - 1], demb_ref.at[z], e_recv.at[NZ - 1])
    for j in (3, 2, 4, 1, 5, 0, 6, 7):
        rows_out[j] = dot_t(dp[...], wv[(z + 1 + j) % NZ]).astype(b16)
        if j < NZ - 1:
            e_copy(j).start()
        else:
            e_home.start()

    for slot in range(8):
        pltpu.make_async_copy(xtp.at[0], lanes(slot), x_recv.at[slot]).wait()
        pltpu.make_async_copy(part_of(0), pg.at[slot], p_recv.at[slot]).wait()

    p = (1 - core) * y + core * x

    def second(j):
        k = (p + 1 + j) % NX
        peer = at((1 - core) * x + core * k, (1 - core) * k + core * y, z, core)
        return send(s2.at[j], r2.at[j], send5.at[j], recv5.at[j], peer)

    right = pg[...].reshape(8 * Q, half)
    for j in (1, 0, 2, 3):
        part = dot(xg[(p + 1 + j) % NX], right)
        if j < NX - 1:
            s2[j] = part.astype(b16)
            second(j).start()
        else:
            own[...] = part
    for j in range(NX - 1):
        second(j).wait_recv()
    own[...] = (own[...] + r2[0].astype(f32) + r2[1].astype(f32) + r2[2].astype(f32)) * scale
    line = z * 2 + core
    for slot in range(2 * NZ):
        s3[slot] = own[8 * slot:8 * slot + 8].astype(b16)

    def third(j):
        slot = (line + j) % (2 * NZ)
        return send(s3.at[slot], r3.at[line], send6.at[j], recv6.at[line], at(x, y, slot // 2, slot % 2))

    def third_arrival(j):
        slot = (line + j) % (2 * NZ)
        return send(s3.at[0], r3.at[slot], send6.at[j], recv6.at[slot], at(x, y, slot // 2, slot % 2))

    for j in (8, 7, 9, 6, 10, 5, 11, 4, 12, 3, 13, 2, 14, 1, 15):
        third(j).start()
    r3[line] = s3[line]
    for j in range(1, 2 * NZ):
        third_arrival(j).wait_recv()
    for color in range(2):
        sums = r3[color].astype(f32)
        for c in range(1, NZ):
            sums = sums + r3[2 * c + color].astype(f32)
        dw_ref[:, color * half:(color + 1) * half] = sums

    for j in range(NZ - 1):
        a_copy(j).wait_send()
        e_copy(j).wait_send()
        e_copy(j).wait_recv()
    e_home.wait()
    for _, _, sent in (logs, fwd_out, fwd_back, bwd_out, bwd_back):
        sent()
    lines(0, lambda copy: copy.wait_send())
    lines(1, lambda copy: copy.wait_send())
    for j in range(NX - 1):
        second(j).wait_send()
    for j in range(1, 2 * NZ):
        third(j).wait_send()


def on_device(embeds, w_in, log_decay, clip_keep, clip_starts, valid_len, norm_gain, g_out):
    n_cam, t, width = embeds.shape
    d, e = w_in.shape
    n_tm = lax.axis_size("tm")
    half, part = e // 2, d // NX // NY
    scale = 1.0 / math.sqrt(n_cam * t * n_tm)
    dma = pltpu.SemaphoreType.DMA
    vmem = pl.BlockSpec(memory_space=pltpu.VMEM)
    smem = pl.BlockSpec(memory_space=pltpu.SMEM)
    hbm = pl.BlockSpec(memory_space=pl.ANY)
    f32, b16 = jnp.float32, jnp.bfloat16
    scratch = lambda dtype, *shape: pltpu.VMEM(shape, dtype)
    layer_out, d_embeds, d_w_in = pl.pallas_call(
        functools.partial(layer_kernel, scale),
        name="layer",
        out_shape=(jax.ShapeDtypeStruct((t, HP), b16), jax.ShapeDtypeStruct((n_cam, t, width), b16),
                   jax.ShapeDtypeStruct((part // n_cam // 2, e), f32)),
        in_specs=[smem, smem, hbm, hbm, vmem, vmem, vmem, vmem],
        out_specs=(vmem, hbm, vmem),
        scratch_shapes=[
            scratch(b16, n_cam, width, e), scratch(b16, t, d), scratch(f32, t, e), scratch(b16, t, e), scratch(b16, e, t),
            scratch(b16, NX, NY, part, t), scratch(b16, HP, t), scratch(f32, HP, t), scratch(f32, H, t, t),
            scratch(f32, H, t), scratch(f32, H, t), scratch(f32, H, t), scratch(f32, H, t),
            scratch(b16, H, P_SIZE, t), scratch(b16, H, t, t), scratch(f32, H, P_SIZE, t),
            scratch(b16, H, P_SIZE, t), scratch(b16, H, P_SIZE, t), scratch(f32, H, P_SIZE, t),
            scratch(f32, HP, t), scratch(f32, H, 8, N), scratch(f32, n_tm, 8, N),
        ] + [scratch(b16, n_tm, P_SIZE, N)] * 8 + [
            scratch(b16, t, e), scratch(b16, NX, part, 8 * t), scratch(b16, 8, t, half), scratch(b16, n_cam, t, width),
            scratch(b16, NX - 1, part, half), scratch(b16, NX - 1, part, half),
            scratch(b16, 2 * n_cam, part // n_cam // 2, half), scratch(b16, 2 * n_cam, part // n_cam // 2, half),
            scratch(f32, part, half),
            dma((n_cam,)), dma((n_cam,)), dma((n_cam,)),
        ] + [dma((n_tm,))] * 10 + [
            dma((2, NX)), dma((8,)), dma((2, NX)), dma((8,)), dma((n_cam,)), dma((n_cam,)),
            dma((NX,)), dma((NX,)), dma((2 * n_cam,)), dma((2 * n_cam,)),
        ],
        compiler_params=pltpu.CompilerParams(collective_id=0, has_side_effects=True, vmem_limit_bytes=60 * 1024 * 1024),
    )(clip_starts, valid_len, embeds, w_in, log_decay, clip_keep.reshape(1, H), norm_gain.reshape(HP // Q, Q), g_out)
    return (layer_out[None], d_embeds, d_w_in)


def solution(mesh):
    return jax.shard_map(
        on_device,
        mesh=mesh,
        in_specs=(
            P(None, "tm", "cam"),
            P(),
            P("cam", None, "tm"),
            P(),
            P("cam", None),
            P("cam"),
            P(),
            P("cam", "tm", None),
        ),
        out_specs=(P("cam", "tm", None), P(None, "tm", "cam"), P(("cam", "tm"), None)),
        check_vma=False,
    )
```

```python
import functools
import math

import jax
import jax.numpy as jnp
from jax import lax
from jax.experimental import pallas as pl
from jax.experimental.pallas import tpu as pltpu
from jax.sharding import PartitionSpec as P

D = 2048
H = 32
P_SIZE = 64
N = 128
Q = 128
HP = 2048
NCLIP = 3


epsilon = 1e-05
MESH = pl.DeviceIdType.MESH
NX, NY, NZ = 4, 4, 8
PIECES = 2
COLUMNS = ((0, 512), (512, 640))


def at(x, y, z, core):
    return (z, (x * NY + y) * 2 + core)


def send(src, dst, sem_a, sem_b, peer):
    return pltpu.make_async_remote_copy(
        src_ref=src, dst_ref=dst, send_sem=sem_a, recv_sem=sem_b, device_id=peer, device_id_type=MESH
    )


def loop(start, end, body):
    def step(k, _):
        body(k)
        return 0
    lax.fori_loop(start, end, step, 0)


def layer_kernel(scale, starts_ref, len_ref, emb_ref, w_ref, rate_ref, keep_ref, gain_ref, g_ref,
                 out_ref, demb_ref, dw_ref,
                 wv, xin, acc, proj, xt, xtp, gt, gain, wts, cum, tail, lift, tot,
                 xw, mix, yin, dt, dl, din, lot, lg, lgot, snd1, got1, snd2, sin, snd3, got3, snd4, rin,
                 dp, xg, pg, rows_out, s2, r2, s3, r3, own, lay,
                 w_sem, o_sem, a_send, a_recv,
                 l_send, l_recv, send1, recv1, send2, recv2, send3, recv3, send4, recv4,
                 x_send, x_recv, p_send, p_recv, e_send, e_recv, send5, recv5, send6, recv6):
    f32, b16 = jnp.float32, jnp.bfloat16
    me, z = lax.axis_index("tm"), lax.axis_index("cam")
    n_tm = 2 * NX * NY
    x, y, core = me // (2 * NY), (me // 2) % NY, me % 2
    hp = H * P_SIZE
    width = emb_ref.shape[2]
    half = dp.shape[1] // 2
    group = 4

    def w_copy(j):
        c = (z + NZ - 1 - j) % NZ
        return pltpu.make_async_copy(w_ref.at[pl.ds(pl.multiple_of(c * width, width), width)], wv.at[c], w_sem.at[j])

    barrier = pltpu.get_barrier_semaphore()

    def greet(peer):
        pl.semaphore_signal(barrier, inc=1, device_id=peer, device_id_type=MESH)

    loop(1, NZ, lambda j: greet(((z + j) % NZ, me)))
    loop(1, NZ, lambda j: greet(((z + j) % NZ, me + 1 - 2 * core)))
    loop(1, n_tm, lambda j: greet((z, (me + j) % n_tm)))
    for j in (7, 0, 6, 1, 5, 2, 4, 3):
        w_copy(j).start()

    def dot(a, b):
        return jnp.dot(a, b, preferred_element_type=f32)

    def dot_t(a, b):
        return lax.dot_general(a, b, (((1,), (1,)), ((), ())), preferred_element_type=f32)

    def t_dot(a, b):
        return lax.dot_general(a, b, (((0,), (0,)), ((), ())), preferred_element_type=f32)

    def lanes_of(shape):
        return lax.broadcasted_iota(jnp.int32, shape, len(shape) - 1)

    def subs_of(shape):
        return lax.broadcasted_iota(jnp.int32, shape, 0)

    base = me * Q
    here = lanes_of((1, Q)) + base
    is_start = here == starts_ref[0, 0]
    for k in range(1, NCLIP):
        is_start = is_start | (here == starts_ref[0, k])
    keep_log = jnp.log(keep_ref[...])
    keep_col = jnp.sum(jnp.where(lanes_of((H, H)) == subs_of((H, H)), keep_log, 0.0), axis=1, keepdims=True)
    rates = rate_ref[0] + jnp.where(is_start, keep_col, 0.0)
    upper = (subs_of((Q, Q)) <= lanes_of((Q, Q)))
    running = jnp.dot(rates, upper.astype(f32), precision=lax.Precision.HIGHEST, preferred_element_type=f32)
    cum[...] = running
    tail[...] = jnp.exp(running[:, Q - 1:Q] - running)
    lift[...] = jnp.exp(running)
    tot[...] = jnp.broadcast_to(running[:, Q - 1:Q], (H, Q))
    valid = (here < len_ref[0]).astype(f32)
    valid_col = (subs_of((Q, Q)) + base < len_ref[0])

    def logs_of(h):
        lg[h] = jnp.broadcast_to(tot[pl.ds(h, 1)], (8, Q))

    loop(0, H, logs_of)

    pl.semaphore_wait(barrier, 2 * (NZ - 1) + n_tm - 1)

    def a_copy(j):
        lanes = pl.ds(pl.multiple_of(z * width, width), width)
        return send(emb_ref.at[(z + 1 + j) % NZ], xin.at[:, lanes], a_send.at[j], a_recv.at[j], ((z + 1 + j) % NZ, me))

    def block(c):
        return xin.at[:, pl.ds(pl.multiple_of(c * width, width), width)]

    a_home = pltpu.make_async_copy(emb_ref.at[z], block(z), a_recv.at[NZ - 1])
    for j in (3, 2, 4, 1, 5, 0, 6):
        a_copy(j).start()
    a_home.start()

    def apart(i):
        return (2 + 3 * i + 3 * (i // 2) + 2 * (i // 3)) % 4

    def exchange(src, dst, sem_a, sem_b, part=None):
        def copy(j):
            dx, dy = apart(j // (2 * NY)), apart((j // 2) % NY)
            peer = (((x + dx) % NX) * NY + (y + dy) % NY) * 2 + (core + 1 + j) % 2
            if part is None:
                return send(src.at[peer], dst.at[me], sem_a.at[j], sem_b.at[j], (z, peer))
            return send(src.at[peer, part], dst.at[me, part], sem_a.at[j], sem_b.at[j], (z, peer))

        def start():
            loop(0, n_tm - 1, lambda j: copy(j).start())
            if part is None:
                dst[me] = src[me]
            else:
                dst[me, part] = src[me, part]

        return (start, lambda: loop(0, n_tm - 1, lambda j: copy(j).wait_recv()),
                lambda: loop(0, n_tm - 1, lambda j: copy(j).wait_send()))

    pieces = [pl.ds(k * (P_SIZE // PIECES), P_SIZE // PIECES) for k in range(PIECES)]

    def exchanges(src, dst, sem_a, sem_b):
        return [exchange(src, dst, sem_a.at[k], sem_b.at[k], piece) for k, piece in enumerate(pieces)]

    logs = exchange(lg, lgot, l_send, l_recv)
    fwd_out = exchanges(snd1, got1, send1, recv1)
    fwd_back = exchanges(snd2, sin, send2, recv2)
    bwd_out = exchanges(snd3, got3, send3, recv3)
    bwd_back = exchanges(snd4, rin, send4, recv4)
    logs[0]()

    def weights_of(h):
        row = jnp.broadcast_to(cum[pl.ds(h, 1)], (Q, Q))
        wts[h] = jnp.where(upper, jnp.exp(jnp.where(upper, row - row.T, 0.0)), 0.0)

    loop(0, H, weights_of)

    def columns_of(k):
        part = pl.ds(pl.multiple_of(k * Q, Q), Q)
        gt[part] = g_ref[0, :, part].astype(f32).T.astype(b16)
        gain[part] = jnp.broadcast_to(gain_ref[pl.ds(k, 1)], (Q, Q)).T * valid

    loop(0, hp // Q, columns_of)

    piece = Q // (2 * NY)
    for n, j in enumerate((7, 0, 6, 1, 5, 2, 4, 3)):
        c = (z + NZ - 1 - j) % NZ
        w_copy(j).wait()
        if j == NZ - 1:
            a_home.wait()
            c = z
        else:
            a_copy(j).wait_recv()
        got = block(c)[...]
        term = dot(got, wv[c])
        if n == 0:
            acc[...] = term
        else:
            acc[...] += term
        for k in range(width // Q):
            turned = got[:, k * Q:(k + 1) * Q].astype(f32).T.astype(b16)
            for m in range(Q // piece):
                feature = k * Q + m * piece
                xtp[feature // (NY * piece), (feature // piece) % NY, pl.ds(pl.multiple_of(c * piece, piece), piece)] = (
                    turned[m * piece:(m + 1) * piece])

    def part_of(color, q):
        return dp.at[:, pl.ds(color * half + COLUMNS[q][0], COLUMNS[q][1])]

    def p_slot(slot, q):
        return pg.at[slot, :, pl.ds(COLUMNS[q][0], COLUMNS[q][1])]

    def lanes(slot):
        return xg.at[:, :, pl.ds(pl.multiple_of(slot * Q, Q), Q)]

    def x_line(color, j):
        if color == 0:
            return send(xtp.at[(x + j) % NX], lanes(x * 2 + core), x_send.at[0, j], x_recv.at[x * 2 + core],
                        at((x + j) % NX, y, z, 0))
        return send(xtp.at[:, (y + j) % NY], lanes(y * 2 + core), x_send.at[1, j], x_recv.at[y * 2 + core],
                    at(x, (y + j) % NY, z, 1))

    def p_line(q):
        def copy(color, j):
            if color == 0:
                return send(part_of(0, q), p_slot(x * 2 + core, q), p_send.at[q, 0, j], p_recv.at[q, x * 2 + core],
                            at((x + j) % NX, y, z, 0))
            return send(part_of(1, q), p_slot(y * 2 + core, q), p_send.at[q, 1, j], p_recv.at[q, y * 2 + core],
                        at(x, (y + j) % NY, z, 1))
        return copy

    def lines(what, act):
        for j in (2, 1, 3):
            act(what(0, j))
            act(what(1, j))

        @pl.when(core == 0)
        def _():
            act(what(1, 0))

        @pl.when(core == 1)
        def _():
            act(what(0, 0))

    lines(x_line, lambda copy: copy.start())

    @pl.when(core == 0)
    def _():
        pltpu.make_async_copy(xtp.at[x], lanes(x * 2), x_recv.at[x * 2]).start()

    @pl.when(core == 1)
    def _():
        pltpu.make_async_copy(xtp.at[:, y], lanes(y * 2 + 1), x_recv.at[y * 2 + 1]).start()

    for k in range((hp + 2 * N) // Q):
        part = acc[:, k * Q:(k + 1) * Q]
        if k < hp // Q:
            part = jnp.where(valid_col, part, 0.0)
        proj[:, k * Q:(k + 1) * Q] = part.astype(b16)
        xt[k * Q:(k + 1) * Q] = part.T.astype(b16)

    b_nat, c_nat = proj[:, hp:hp + N], proj[:, hp + N:hp + 2 * N]
    b_t, c_t = xt[hp:hp + N], xt[hp + N:hp + 2 * N]

    def rows(g, i):
        return pl.ds(pl.multiple_of((g * group + i) * P_SIZE, P_SIZE), P_SIZE)

    def local_states(g):
        for i in range(group):
            h = g * group + i
            xw[h] = (xt[rows(g, i)].astype(f32) * tail[pl.ds(h, 1)]).astype(b16)
        states = dot(xw[pl.ds(g * group, group)].reshape(group * P_SIZE, Q), b_nat)
        snd1[pl.ds(g * group, group)] = states.astype(b16).reshape(group, P_SIZE, N)

    loop(0, H // group, local_states)
    for one in fwd_out:
        one[0]()

    scores = dot(b_nat, c_t)

    def inside(g):
        for i in range(group):
            h = g * group + i
            mix[h] = (wts[h] * scores).astype(b16)
            yin[h] = dot(xt[rows(g, i)], mix[h])

    loop(0, H // group, inside)
    logs[1]()
    size = P_SIZE // PIECES

    def scan(parts, out, piece, reverse):
        def body(k, state):
            i = n_tm - 1 - k if reverse else k
            out[i, piece] = state.astype(b16).reshape(size, N)
            decay = jnp.exp(lgot[i])
            return decay[None] * state + parts[i, piece].astype(f32).reshape(size // 8, 8, N)
        lax.fori_loop(0, n_tm, body, jnp.zeros((size // 8, 8, N), f32))

    for k, piece in enumerate(pieces):
        fwd_out[k][1]()
        scan(got1, snd2, piece, False)
        fwd_back[k][0]()
    for one in fwd_back:
        one[1]()

    def norm_step(g):
        carried = dot(sin[pl.ds(g * group, group)].reshape(group * P_SIZE, N), c_t)
        for i in range(group):
            h = g * group + i
            up = lift[pl.ds(h, 1)]
            raw = yin[h] + up * carried[i * P_SIZE:(i + 1) * P_SIZE]
            inv = lax.rsqrt(jnp.mean(raw * raw, axis=0, keepdims=True) + epsilon)
            normed = raw * inv
            scaled = gain[rows(g, i)]
            lot[rows(g, i)] = normed * scaled
            d_normed = gt[rows(g, i)].astype(f32) * scaled
            d_out = inv * (d_normed - normed * jnp.mean(d_normed * normed, axis=0, keepdims=True))
            dt[h] = d_out.astype(b16)
            dl[h] = (d_out * up).astype(b16)
        states = dot(dl[pl.ds(g * group, group)].reshape(group * P_SIZE, Q), c_nat)
        snd3[pl.ds(g * group, group)] = states.astype(b16).reshape(group, P_SIZE, N)

    loop(0, H // group, norm_step)
    for one in bwd_out:
        one[0]()

    first = subs_of((2 * P_SIZE, Q)) < P_SIZE

    def pairs(g, total):
        for i in range(0, group, 2):
            h = g * group + i
            d_two = dt[pl.ds(h, 2)].reshape(2 * P_SIZE, Q)
            zero = jnp.zeros_like(d_two)
            spread = jnp.concatenate([jnp.where(first, d_two, zero), jnp.where(first, zero, d_two)], axis=1)
            x_two = proj[:, pl.ds(pl.multiple_of(h * P_SIZE, 2 * P_SIZE), 2 * P_SIZE)]
            both = dot(x_two, spread)
            total = total + wts[h] * both[:, :Q] + wts[h + 1] * both[:, Q:]
            din[h] = dot_t(dt[h], mix[h])
            din[h + 1] = dot_t(dt[h + 1], mix[h + 1])
        return total

    pair_sum = lax.fori_loop(0, H // group, pairs, jnp.zeros((Q, Q), f32)).astype(b16)
    for k, piece in enumerate(pieces):
        bwd_out[k][1]()
        scan(got3, snd4, piece, True)
        bwd_back[k][0]()
    d_c = t_dot(pair_sum, b_nat) + t_dot(dl[...].reshape(hp, Q), sin[...].reshape(hp, N))
    d_b = dot(pair_sum, c_nat)
    dp[:, hp + N:hp + 2 * N] = d_c.astype(b16)
    for k in range(hp // Q):
        lay[:, k * Q:(k + 1) * Q] = lot[k * Q:(k + 1) * Q].T.astype(b16)
    lay_home = pltpu.make_async_copy(lay, out_ref, o_sem)
    lay_home.start()
    for one in bwd_back:
        one[1]()

    def inputs_of(k):
        after = dot(rin[2 * k:2 * k + 2].reshape(2 * P_SIZE, N), b_t)
        two = [din[2 * k + i] + tail[2 * k + i:2 * k + i + 1] * after[i * P_SIZE:(i + 1) * P_SIZE] for i in range(2)]
        dp[:, k * Q:(k + 1) * Q] = (jnp.concatenate(two, axis=0) * valid).T.astype(b16)

    done = set()
    for q, (off, many) in enumerate(COLUMNS):
        for k in range(hp // Q):
            if k not in done and any(color * half + off <= k * Q < color * half + off + many for color in range(2)):
                done.add(k)
                inputs_of(k)
        if q == len(COLUMNS) - 1:
            d_b = d_b + t_dot(xw[...].reshape(hp, Q), rin[...].reshape(hp, N))
            dp[:, hp:hp + N] = d_b.astype(b16)
        lines(p_line(q), lambda copy: copy.start())

        @pl.when(core == 0)
        def _():
            pltpu.make_async_copy(part_of(0, q), p_slot(x * 2, q), p_recv.at[q, x * 2]).start()

        @pl.when(core == 1)
        def _():
            pltpu.make_async_copy(part_of(1, q), p_slot(y * 2 + 1, q), p_recv.at[q, y * 2 + 1]).start()

    def e_copy(j):
        return send(rows_out.at[j], demb_ref.at[z], e_send.at[j], e_recv.at[j], ((z + 1 + j) % NZ, me))

    e_home = pltpu.make_async_copy(rows_out.at[NZ - 1], demb_ref.at[z], e_recv.at[NZ - 1])
    for j in (3, 2, 4, 1, 5, 0, 6, 7):
        rows_out[j] = dot_t(dp[...], wv[(z + 1 + j) % NZ]).astype(b16)
        if j < NZ - 1:
            e_copy(j).start()
        else:
            e_home.start()

    p = (1 - core) * y + core * x
    line = z * 2 + core

    def second(j, q):
        k = (p + 1 + j) % NX
        peer = at((1 - core) * x + core * k, (1 - core) * k + core * y, z, core)
        cols = pl.ds(*COLUMNS[q])
        return send(s2.at[j, :, cols], r2.at[j, :, cols], send5.at[q, j], recv5.at[q, j], peer)

    def third(j, q):
        slot = (line + j) % (2 * NZ)
        cols = pl.ds(*COLUMNS[q])
        return send(s3.at[slot, :, cols], r3.at[line, :, cols], send6.at[q, j], recv6.at[q, j], at(x, y, slot // 2, slot % 2))

    for slot in range(8):
        pltpu.make_async_copy(xtp.at[0], lanes(slot), x_recv.at[slot]).wait()

    for q, (off, many) in enumerate(COLUMNS):
        cols = slice(off, off + many)
        for slot in range(8):
            pltpu.make_async_copy(part_of(0, q), p_slot(slot, q), p_recv.at[q, slot]).wait()
        right = pg[:, :, cols].reshape(8 * Q, many)
        for j in (1, 0, 2, 3):
            part = dot(xg[(p + 1 + j) % NX], right)
            if j < NX - 1:
                s2[j, :, cols] = part.astype(b16)
                second(j, q).start()
            else:
                own[:, cols] = part
    for q, (off, many) in enumerate(COLUMNS):
        cols = slice(off, off + many)
        for j in range(NX - 1):
            second(j, q).wait_recv()
        own[:, cols] = (own[:, cols] + r2[0, :, cols].astype(f32) + r2[1, :, cols].astype(f32) + r2[2, :, cols].astype(f32)) * scale
        for slot in range(2 * NZ):
            s3[slot, :, cols] = own[8 * slot:8 * slot + 8, cols].astype(b16)
        for j in (8, 7, 9, 6, 10, 5, 11, 4, 12, 3, 13, 2, 14, 1, 15):
            third(j, q).start()
        r3[line, :, cols] = s3[line, :, cols]
    for q, (off, many) in enumerate(COLUMNS):
        for j in range(1, 2 * NZ):
            third(j, q).wait_recv()
        for color in range(2):
            sums = r3[color, :, off:off + many].astype(f32)
            for c in range(1, NZ):
                sums = sums + r3[2 * c + color, :, off:off + many].astype(f32)
            dw_ref[:, color * half + off:color * half + off + many] = sums

    lay_home.wait()
    for j in range(NZ - 1):
        a_copy(j).wait_send()
        e_copy(j).wait_send()
        e_copy(j).wait_recv()
    e_home.wait()
    for one in [logs] + fwd_out + fwd_back + bwd_out + bwd_back:
        one[2]()
    lines(x_line, lambda copy: copy.wait_send())
    for q in range(len(COLUMNS)):
        lines(p_line(q), lambda copy: copy.wait_send())
        for j in range(NX - 1):
            second(j, q).wait_send()
        for j in range(1, 2 * NZ):
            third(j, q).wait_send()


def finish_kernel(*refs):
    half = len(refs) // 4
    ins, outs, held, sems = refs[:half], refs[half:2 * half], refs[2 * half:3 * half], refs[3 * half:]
    loads = [pltpu.make_async_copy(a, b, sem.at[0]) for a, b, sem in zip(ins, held, sems)]
    stores = [pltpu.make_async_copy(a, b, sem.at[1]) for a, b, sem in zip(held, outs, sems)]
    for one in loads:
        one.start()
    for load, store in zip(loads, stores):
        load.wait()
        store.start()
    for one in stores:
        one.wait()


def finish(*arrays):
    hbm = pl.BlockSpec(memory_space=pl.ANY)
    return pl.pallas_call(
        finish_kernel,
        name="finish",
        out_shape=[jax.ShapeDtypeStruct(a.shape, a.dtype) for a in arrays],
        in_specs=[hbm] * len(arrays),
        out_specs=[hbm] * len(arrays),
        scratch_shapes=[pltpu.VMEM(a.shape, a.dtype) for a in arrays] + [pltpu.SemaphoreType.DMA((2,)) for _ in arrays],
    )(*arrays)


def on_device(embeds, w_in, log_decay, clip_keep, clip_starts, valid_len, norm_gain, g_out):
    n_cam, t, width = embeds.shape
    d, e = w_in.shape
    n_tm = lax.axis_size("tm")
    half, part, many = e // 2, d // NX // NY, len(COLUMNS)
    scale = 1.0 / math.sqrt(n_cam * t * n_tm)
    dma = pltpu.SemaphoreType.DMA
    vmem = pl.BlockSpec(memory_space=pltpu.VMEM)
    smem = pl.BlockSpec(memory_space=pltpu.SMEM)
    hbm = pl.BlockSpec(memory_space=pl.ANY)
    f32, b16 = jnp.float32, jnp.bfloat16
    scratch = lambda dtype, *shape: pltpu.VMEM(shape, dtype)
    layer_out, d_embeds, d_w_in = pl.pallas_call(
        functools.partial(layer_kernel, scale),
        name="layer",
        out_shape=(jax.ShapeDtypeStruct((t, HP), b16), jax.ShapeDtypeStruct((n_cam, t, width), b16),
                   jax.ShapeDtypeStruct((part // n_cam // 2, e), f32)),
        in_specs=[smem, smem, hbm, hbm, vmem, vmem, vmem, vmem],
        out_specs=(hbm, hbm, vmem),
        scratch_shapes=[
            scratch(b16, n_cam, width, e), scratch(b16, t, d), scratch(f32, t, e), scratch(b16, t, e), scratch(b16, e, t),
            scratch(b16, NX, NY, part, t), scratch(b16, HP, t), scratch(f32, HP, t), scratch(f32, H, t, t),
            scratch(f32, H, t), scratch(f32, H, t), scratch(f32, H, t), scratch(f32, H, t),
            scratch(b16, H, P_SIZE, t), scratch(b16, H, t, t), scratch(f32, H, P_SIZE, t),
            scratch(b16, H, P_SIZE, t), scratch(b16, H, P_SIZE, t), scratch(f32, H, P_SIZE, t),
            scratch(f32, HP, t), scratch(f32, H, 8, N), scratch(f32, n_tm, 8, N),
        ] + [scratch(b16, n_tm, P_SIZE, N)] * 8 + [
            scratch(b16, t, e), scratch(b16, NX, part, 8 * t), scratch(b16, 8, t, half), scratch(b16, n_cam, t, width),
            scratch(b16, NX - 1, part, half), scratch(b16, NX - 1, part, half),
            scratch(b16, 2 * n_cam, part // n_cam // 2, half), scratch(b16, 2 * n_cam, part // n_cam // 2, half),
            scratch(f32, part, half), scratch(b16, t, HP),
            dma((n_cam,)), dma, dma((n_cam,)), dma((n_cam,)),
        ] + [dma((n_tm,))] * 2 + [dma((PIECES, n_tm))] * 8 + [
            dma((2, NX)), dma((8,)), dma((many, 2, NX)), dma((many, 8)), dma((n_cam,)), dma((n_cam,)),
            dma((many, NX)), dma((many, NX)), dma((many, 2 * n_cam)), dma((many, 2 * n_cam)),
        ],
        compiler_params=pltpu.CompilerParams(collective_id=0, has_side_effects=True, vmem_limit_bytes=60 * 1024 * 1024),
    )(clip_starts, valid_len, embeds, w_in, log_decay, clip_keep.reshape(1, H), norm_gain.reshape(HP // Q, Q), g_out)
    layer_out, d_embeds, d_w_in = finish(layer_out, d_embeds, d_w_in)
    return (layer_out[None], d_embeds, d_w_in)


def solution(mesh):
    return jax.shard_map(
        on_device,
        mesh=mesh,
        in_specs=(
            P(None, "tm", "cam"),
            P(),
            P("cam", None, "tm"),
            P(),
            P("cam", None),
            P("cam"),
            P(),
            P("cam", "tm", None),
        ),
        out_specs=(P("cam", "tm", None), P(None, "tm", "cam"), P(("cam", "tm"), None)),
        check_vma=False,
    )
```

```python
import functools
import math

import jax
import jax.numpy as jnp
from jax import lax
from jax.experimental import pallas as pl
from jax.experimental.pallas import tpu as pltpu
from jax.sharding import PartitionSpec as P

D = 2048
H = 32
P_SIZE = 64
N = 128
Q = 128
HP = 2048
NCLIP = 3


epsilon = 1e-05
MESH = pl.DeviceIdType.MESH
NX, NY, NZ = 4, 4, 8
PIECES = 2
COLUMNS = ((0, 512), (512, 384), (896, 256))


def at(x, y, z, core):
    return (z, (x * NY + y) * 2 + core)


def send(src, dst, sem_a, sem_b, peer):
    return pltpu.make_async_remote_copy(
        src_ref=src, dst_ref=dst, send_sem=sem_a, recv_sem=sem_b, device_id=peer, device_id_type=MESH
    )


def wait_for(ref, sem):
    pltpu.make_async_copy(ref, ref, sem).wait()


def loop(start, end, body):
    def step(k, _):
        body(k)
        return 0
    lax.fori_loop(start, end, step, 0)


def layer_kernel(scale, starts_ref, len_ref, emb_ref, w_ref, rate_ref, keep_ref, gain_ref, g_ref,
                 out_ref, demb_ref, dw_ref,
                 wv, xin, acc, proj, xt, xtp, gt, gain, wts, cum, tail, lift, tot,
                 xw, mix, yin, dt, dl, din, lot, lg, lgot, snd1, got1, snd2, sin, snd3, got3, snd4, rin,
                 dp, xg, pg, rows_out, s2, r2, s3, r3, own, lay,
                 w_sem, o_sem, a_send, a_recv,
                 l_send, l_recv, send1, recv1, send2, recv2, send3, recv3, send4, recv4,
                 x_send, x_recv, p_send, p_recv, e_send, e_recv, send5, recv5, send6, recv6):
    f32, b16 = jnp.float32, jnp.bfloat16
    me, z = lax.axis_index("tm"), lax.axis_index("cam")
    n_tm = 2 * NX * NY
    x, y, core = me // (2 * NY), (me // 2) % NY, me % 2
    hp = H * P_SIZE
    width = emb_ref.shape[2]
    half = dp.shape[1] // 2
    group = 4

    def w_copy(j):
        c = (z + NZ - 1 - j) % NZ
        return pltpu.make_async_copy(w_ref.at[pl.ds(pl.multiple_of(c * width, width), width)], wv.at[c], w_sem.at[j])

    barrier = pltpu.get_barrier_semaphore()

    def greet(peer):
        pl.semaphore_signal(barrier, inc=1, device_id=peer, device_id_type=MESH)

    loop(1, NZ, lambda j: greet(((z + j) % NZ, me)))
    loop(1, NZ, lambda j: greet(((z + j) % NZ, me + 1 - 2 * core)))
    loop(1, n_tm, lambda j: greet((z, (me + j) % n_tm)))
    for j in (7, 0, 6, 1, 5, 2, 4, 3):
        w_copy(j).start()

    def dot(a, b):
        return jnp.dot(a, b, preferred_element_type=f32)

    def dot_t(a, b):
        return lax.dot_general(a, b, (((1,), (1,)), ((), ())), preferred_element_type=f32)

    def t_dot(a, b):
        return lax.dot_general(a, b, (((0,), (0,)), ((), ())), preferred_element_type=f32)

    def lanes_of(shape):
        return lax.broadcasted_iota(jnp.int32, shape, len(shape) - 1)

    def subs_of(shape):
        return lax.broadcasted_iota(jnp.int32, shape, 0)

    base = me * Q
    here = lanes_of((1, Q)) + base
    is_start = here == starts_ref[0, 0]
    for k in range(1, NCLIP):
        is_start = is_start | (here == starts_ref[0, k])
    keep_log = jnp.log(keep_ref[...])
    keep_col = jnp.sum(jnp.where(lanes_of((H, H)) == subs_of((H, H)), keep_log, 0.0), axis=1, keepdims=True)
    rates = rate_ref[0] + jnp.where(is_start, keep_col, 0.0)
    upper = (subs_of((Q, Q)) <= lanes_of((Q, Q)))
    running = jnp.dot(rates, upper.astype(f32), precision=lax.Precision.HIGHEST, preferred_element_type=f32)
    cum[...] = running
    tail[...] = jnp.exp(running[:, Q - 1:Q] - running)
    lift[...] = jnp.exp(running)
    tot[...] = jnp.broadcast_to(running[:, Q - 1:Q], (H, Q))
    valid = (here < len_ref[0]).astype(f32)
    valid_col = (subs_of((Q, Q)) + base < len_ref[0])

    def logs_of(h):
        lg[h] = jnp.broadcast_to(tot[pl.ds(h, 1)], (8, Q))

    loop(0, H, logs_of)

    pl.semaphore_wait(barrier, 2 * (NZ - 1) + n_tm - 1)

    def a_copy(j):
        lanes = pl.ds(pl.multiple_of(z * width, width), width)
        return send(emb_ref.at[(z + 1 + j) % NZ], xin.at[:, lanes], a_send, a_recv.at[j], ((z + 1 + j) % NZ, me))

    def block(c):
        return xin.at[:, pl.ds(pl.multiple_of(c * width, width), width)]

    a_home = pltpu.make_async_copy(emb_ref.at[z], block(z), a_recv.at[NZ - 1])
    for j in (3, 2, 4, 1, 5, 0, 6):
        a_copy(j).start()
    a_home.start()

    def apart(i):
        return (2 + 3 * i + 3 * (i // 2) + 2 * (i // 3)) % 4

    def exchange(src, dst, sem_a, sem_b, part=None):
        def copy(peer):
            if part is None:
                return send(src.at[peer], dst.at[me], sem_a, sem_b, (z, peer))
            return send(src.at[peer, part], dst.at[me, part], sem_a, sem_b, (z, peer))

        def own_block():
            if part is None:
                dst[me] = src[me]
            else:
                dst[me, part] = src[me, part]

        def start():
            def one(j):
                dx, dy = apart(j // (2 * NY)), apart((j // 2) % NY)
                copy((((x + dx) % NX) * NY + (y + dy) % NY) * 2 + (core + 1 + j) % 2).start()
            loop(0, n_tm - 1, one)
            own_block()

        def heads_of(g):
            for i in range(group):
                peer = g * group + i

                @pl.when(peer != me)
                def _():
                    copy(peer).start()

        others = pl.ds(0, n_tm - 1)

        def wait(ref, sem):
            wait_for(ref.at[others] if part is None else ref.at[others, part], sem)

        return start, lambda: wait(dst, sem_b), lambda: wait(src, sem_a), heads_of, own_block

    pieces = [pl.ds(k * (P_SIZE // PIECES), P_SIZE // PIECES) for k in range(PIECES)]

    def exchanges(src, dst, sem_a, sem_b):
        return [exchange(src, dst, sem_a.at[k], sem_b.at[k], piece) for k, piece in enumerate(pieces)]

    logs = exchange(lg, lgot, l_send, l_recv)
    fwd_out = exchanges(snd1, got1, send1, recv1)
    fwd_back = exchanges(snd2, sin, send2, recv2)
    bwd_out = exchanges(snd3, got3, send3, recv3)
    bwd_back = exchanges(snd4, rin, send4, recv4)
    logs[0]()

    def weights_of(h):
        row = jnp.broadcast_to(cum[pl.ds(h, 1)], (Q, Q))
        wts[h] = jnp.where(upper, jnp.exp(jnp.where(upper, row - row.T, 0.0)), 0.0)

    loop(0, H, weights_of)

    def columns_of(k):
        part = pl.ds(pl.multiple_of(k * Q, Q), Q)
        gt[part] = g_ref[0, :, part].astype(f32).T.astype(b16)
        gain[part] = jnp.broadcast_to(gain_ref[pl.ds(k, 1)], (Q, Q)).T * valid

    loop(0, hp // Q, columns_of)

    piece = Q // (2 * NY)
    for n, j in enumerate((7, 0, 6, 1, 5, 2, 4, 3)):
        c = (z + NZ - 1 - j) % NZ
        w_copy(j).wait()
        if j == NZ - 1:
            a_home.wait()
            c = z
        else:
            a_copy(j).wait_recv()
        got = block(c)[...]
        term = dot(got, wv[c])
        if n == 0:
            acc[...] = term
        else:
            acc[...] += term
        for k in range(width // Q):
            turned = got[:, k * Q:(k + 1) * Q].astype(f32).T.astype(b16)
            for m in range(Q // piece):
                feature = k * Q + m * piece
                xtp[feature // (NY * piece), (feature // piece) % NY, pl.ds(pl.multiple_of(c * piece, piece), piece)] = (
                    turned[m * piece:(m + 1) * piece])

    def part_of(color, q):
        return dp.at[:, pl.ds(color * half + COLUMNS[q][0], COLUMNS[q][1])]

    def p_slot(slot, q):
        return pg.at[slot, :, pl.ds(COLUMNS[q][0], COLUMNS[q][1])]

    def x_slot(slot, u):
        return xg.at[pl.ds(2 * u, 2), :, pl.ds(pl.multiple_of(slot * Q, Q), Q)]

    def x_line(u):
        two = pl.ds(2 * u, 2)

        def copy(color, j):
            if color == 0:
                return send(xtp.at[(x + j) % NX, two], x_slot(x * 2 + core, u), x_send.at[u], x_recv.at[u],
                            at((x + j) % NX, y, z, 0))
            return send(xtp.at[two, (y + j) % NY], x_slot(y * 2 + core, u), x_send.at[u], x_recv.at[u],
                        at(x, (y + j) % NY, z, 1))
        return copy

    def p_line(q):
        def copy(color, j):
            if color == 0:
                return send(part_of(0, q), p_slot(x * 2 + core, q), p_send.at[q], p_recv.at[q],
                            at((x + j) % NX, y, z, 0))
            return send(part_of(1, q), p_slot(y * 2 + core, q), p_send.at[q], p_recv.at[q],
                        at(x, (y + j) % NY, z, 1))
        return copy

    def lines(what, act):
        for j in (2, 1, 3):
            act(what(0, j))
            act(what(1, j))

        @pl.when(core == 0)
        def _():
            act(what(1, 0))

        @pl.when(core == 1)
        def _():
            act(what(0, 0))

    def x_rows(u):
        two = pl.ds(2 * u, 2)
        lines(x_line(u), lambda copy: copy.start())

        @pl.when(core == 0)
        def _():
            pltpu.make_async_copy(xtp.at[x, two], x_slot(x * 2, u), x_recv.at[u]).start()

        @pl.when(core == 1)
        def _():
            pltpu.make_async_copy(xtp.at[two, y], x_slot(y * 2 + 1, u), x_recv.at[u]).start()

    x_rows(0)

    for k in range((hp + 2 * N) // Q):
        part = acc[:, k * Q:(k + 1) * Q]
        if k < hp // Q:
            part = jnp.where(valid_col, part, 0.0)
        proj[:, k * Q:(k + 1) * Q] = part.astype(b16)
        xt[k * Q:(k + 1) * Q] = part.T.astype(b16)

    b_nat, c_nat = proj[:, hp:hp + N], proj[:, hp + N:hp + 2 * N]
    b_t, c_t = xt[hp:hp + N], xt[hp + N:hp + 2 * N]

    def rows(g, i):
        return pl.ds(pl.multiple_of((g * group + i) * P_SIZE, P_SIZE), P_SIZE)

    def turn(gg):
        return (gg + 1 + me // group) % (H // group)

    def in_turns(body, piece):
        def step(gg):
            body(turn(gg))

            @pl.when(gg > 0)
            def _():
                piece[3](turn(gg - 1))
        loop(0, H // group, step)
        piece[3](turn(H // group - 1))
        piece[4]()

    def local_states(g):
        for i in range(group):
            h = g * group + i
            xw[h] = (xt[rows(g, i)].astype(f32) * tail[pl.ds(h, 1)]).astype(b16)
        states = dot(xw[pl.ds(g * group, group)].reshape(group * P_SIZE, Q), b_nat)
        snd1[pl.ds(g * group, group)] = states.astype(b16).reshape(group, P_SIZE, N)

    in_turns(local_states, fwd_out[0])
    for one in fwd_out[1:]:
        one[0]()

    scores = dot(b_nat, c_t)

    def inside(g):
        for i in range(group):
            h = g * group + i
            mix[h] = (wts[h] * scores).astype(b16)
            yin[h] = dot(xt[rows(g, i)], mix[h])

    loop(0, H // group, inside)
    logs[1]()
    size = P_SIZE // PIECES

    def scan(parts, out, piece, reverse):
        def body(k, state):
            i = n_tm - 1 - k if reverse else k
            out[i, piece] = state.astype(b16).reshape(size, N)
            decay = jnp.exp(lgot[i])
            return decay[None] * state + parts[i, piece].astype(f32).reshape(size // 8, 8, N)
        lax.fori_loop(0, n_tm, body, jnp.zeros((size // 8, 8, N), f32))

    for k, piece in enumerate(pieces):
        fwd_out[k][1]()
        scan(got1, snd2, piece, False)
        fwd_back[k][0]()
    for one in fwd_back:
        one[1]()
    x_rows(1)

    def norm_step(g):
        carried = dot(sin[pl.ds(g * group, group)].reshape(group * P_SIZE, N), c_t)
        for i in range(group):
            h = g * group + i
            up = lift[pl.ds(h, 1)]
            raw = yin[h] + up * carried[i * P_SIZE:(i + 1) * P_SIZE]
            inv = lax.rsqrt(jnp.mean(raw * raw, axis=0, keepdims=True) + epsilon)
            normed = raw * inv
            scaled = gain[rows(g, i)]
            lot[rows(g, i)] = normed * scaled
            d_normed = gt[rows(g, i)].astype(f32) * scaled
            d_out = inv * (d_normed - normed * jnp.mean(d_normed * normed, axis=0, keepdims=True))
            dt[h] = d_out.astype(b16)
            dl[h] = (d_out * up).astype(b16)
        states = dot(dl[pl.ds(g * group, group)].reshape(group * P_SIZE, Q), c_nat)
        snd3[pl.ds(g * group, group)] = states.astype(b16).reshape(group, P_SIZE, N)

    in_turns(norm_step, bwd_out[0])
    for one in bwd_out[1:]:
        one[0]()

    first = subs_of((2 * P_SIZE, Q)) < P_SIZE

    def pairs(g, total):
        for i in range(0, group, 2):
            h = g * group + i
            d_two = dt[pl.ds(h, 2)].reshape(2 * P_SIZE, Q)
            zero = jnp.zeros_like(d_two)
            spread = jnp.concatenate([jnp.where(first, d_two, zero), jnp.where(first, zero, d_two)], axis=1)
            x_two = proj[:, pl.ds(pl.multiple_of(h * P_SIZE, 2 * P_SIZE), 2 * P_SIZE)]
            both = dot(x_two, spread)
            total = total + wts[h] * both[:, :Q] + wts[h + 1] * both[:, Q:]
            din[h] = dot_t(dt[h], mix[h])
            din[h + 1] = dot_t(dt[h + 1], mix[h + 1])
        return total

    pair_sum = lax.fori_loop(0, H // group, pairs, jnp.zeros((Q, Q), f32)).astype(b16)
    for k, piece in enumerate(pieces):
        bwd_out[k][1]()
        scan(got3, snd4, piece, True)
        bwd_back[k][0]()
    d_c = t_dot(pair_sum, b_nat) + t_dot(dl[...].reshape(hp, Q), sin[...].reshape(hp, N))
    d_b = dot(pair_sum, c_nat)
    dp[:, hp + N:hp + 2 * N] = d_c.astype(b16)
    for k in range(hp // Q):
        lay[:, k * Q:(k + 1) * Q] = lot[k * Q:(k + 1) * Q].T.astype(b16)
    lay_home = pltpu.make_async_copy(lay, out_ref, o_sem)
    lay_home.start()
    for one in bwd_back:
        one[1]()

    def inputs_of(k):
        after = dot(rin[2 * k:2 * k + 2].reshape(2 * P_SIZE, N), b_t)
        two = [din[2 * k + i] + tail[2 * k + i:2 * k + i + 1] * after[i * P_SIZE:(i + 1) * P_SIZE] for i in range(2)]
        dp[:, k * Q:(k + 1) * Q] = (jnp.concatenate(two, axis=0) * valid).T.astype(b16)

    done = set()
    for q, (off, many) in enumerate(COLUMNS):
        for k in range(hp // Q):
            if k not in done and any(color * half + off <= k * Q < color * half + off + many for color in range(2)):
                done.add(k)
                inputs_of(k)
        if q == len(COLUMNS) - 1:
            d_b = d_b + t_dot(xw[...].reshape(hp, Q), rin[...].reshape(hp, N))
            dp[:, hp:hp + N] = d_b.astype(b16)
        lines(p_line(q), lambda copy: copy.start())

        @pl.when(core == 0)
        def _():
            pltpu.make_async_copy(part_of(0, q), p_slot(x * 2, q), p_recv.at[q]).start()

        @pl.when(core == 1)
        def _():
            pltpu.make_async_copy(part_of(1, q), p_slot(y * 2 + 1, q), p_recv.at[q]).start()

    def e_copy(j):
        return send(rows_out.at[j], demb_ref.at[z], e_send, e_recv, ((z + 1 + j) % NZ, me))

    e_home = pltpu.make_async_copy(rows_out.at[NZ - 1], demb_ref.at[z], e_recv)
    for j in (3, 2, 4, 1, 5, 0, 6, 7):
        rows_out[j] = dot_t(dp[...], wv[(z + 1 + j) % NZ]).astype(b16)
        if j < NZ - 1:
            e_copy(j).start()
        else:
            e_home.start()

    p = (1 - core) * y + core * x
    line = z * 2 + core

    def second(j, q):
        k = (p + 1 + j) % NX
        peer = at((1 - core) * x + core * k, (1 - core) * k + core * y, z, core)
        cols = pl.ds(*COLUMNS[q])
        return send(s2.at[j, :, cols], r2.at[j, :, cols], send5.at[q], recv5.at[q], peer)

    def third(j, q):
        slot = (line + j) % (2 * NZ)
        cols = pl.ds(*COLUMNS[q])
        return send(s3.at[slot, :, cols], r3.at[line, :, cols], send6.at[q], recv6.at[q], at(x, y, slot // 2, slot % 2))

    for u in range(2):
        wait_for(xg.at[pl.ds(2 * u, 2)], x_recv.at[u])

    def multiply(q):
        off, many = COLUMNS[q]
        cols = slice(off, off + many)
        wait_for(pg.at[:, :, pl.ds(off, many)], p_recv.at[q])
        right = pg[:, :, cols].reshape(8 * Q, many)
        for j in (1, 0, 2, 3):
            part = dot(xg[(p + 1 + j) % NX], right)
            if j < NX - 1:
                s2[j, :, cols] = part.astype(b16)
                second(j, q).start()
            else:
                own[:, cols] = part

    def add(q):
        off, many = COLUMNS[q]
        cols = slice(off, off + many)
        wait_for(r2.at[:, :, pl.ds(off, many)], recv5.at[q])
        own[:, cols] = (own[:, cols] + r2[0, :, cols].astype(f32) + r2[1, :, cols].astype(f32) + r2[2, :, cols].astype(f32)) * scale
        for slot in range(2 * NZ):
            s3[slot, :, cols] = own[8 * slot:8 * slot + 8, cols].astype(b16)
        for j in (8, 7, 9, 6, 10, 5, 11, 4, 12, 3, 13, 2, 14, 1, 15):
            third(j, q).start()
        r3[line, :, cols] = s3[line, :, cols]

    multiply(0)
    for q in range(1, len(COLUMNS)):
        multiply(q)
        add(q - 1)
    add(len(COLUMNS) - 1)
    others = pl.ds(0, 2 * NZ - 1)
    for q, (off, many) in enumerate(COLUMNS):
        wait_for(r3.at[others, :, pl.ds(off, many)], recv6.at[q])
        for color in range(2):
            sums = r3[color, :, off:off + many].astype(f32)
            for c in range(1, NZ):
                sums = sums + r3[2 * c + color, :, off:off + many].astype(f32)
            dw_ref[:, color * half + off:color * half + off + many] = sums

    lay_home.wait()
    wait_for(rows_out.at[pl.ds(0, NZ - 1)], a_send)
    wait_for(rows_out.at[pl.ds(0, NZ - 1)], e_send)
    wait_for(demb_ref, e_recv)
    for one in [logs] + fwd_out + fwd_back + bwd_out + bwd_back:
        one[2]()
    for u in range(2):
        wait_for(xg.at[pl.ds(2 * u, 2), :, pl.ds(0, 7 * Q)], x_send.at[u])
    for q, (off, many) in enumerate(COLUMNS):
        cols = pl.ds(off, many)
        wait_for(pg.at[pl.ds(0, 7), :, cols], p_send.at[q])
        wait_for(s2.at[:, :, cols], send5.at[q])
        wait_for(s3.at[others, :, cols], send6.at[q])


def finish_kernel(*refs):
    half = len(refs) // 4
    ins, outs, held, sems = refs[:half], refs[half:2 * half], refs[2 * half:3 * half], refs[3 * half:]
    loads = [pltpu.make_async_copy(a, b, sem.at[0]) for a, b, sem in zip(ins, held, sems)]
    stores = [pltpu.make_async_copy(a, b, sem.at[1]) for a, b, sem in zip(held, outs, sems)]
    for one in loads:
        one.start()
    for load, store in zip(loads, stores):
        load.wait()
        store.start()
    for one in stores:
        one.wait()


def finish(*arrays):
    hbm = pl.BlockSpec(memory_space=pl.ANY)
    return pl.pallas_call(
        finish_kernel,
        name="finish",
        out_shape=[jax.ShapeDtypeStruct(a.shape, a.dtype) for a in arrays],
        in_specs=[hbm] * len(arrays),
        out_specs=[hbm] * len(arrays),
        scratch_shapes=[pltpu.VMEM(a.shape, a.dtype) for a in arrays] + [pltpu.SemaphoreType.DMA((2,)) for _ in arrays],
    )(*arrays)


def on_device(embeds, w_in, log_decay, clip_keep, clip_starts, valid_len, norm_gain, g_out):
    n_cam, t, width = embeds.shape
    d, e = w_in.shape
    n_tm = lax.axis_size("tm")
    half, part, many = e // 2, d // NX // NY, len(COLUMNS)
    scale = 1.0 / math.sqrt(n_cam * t * n_tm)
    dma = pltpu.SemaphoreType.DMA
    vmem = pl.BlockSpec(memory_space=pltpu.VMEM)
    smem = pl.BlockSpec(memory_space=pltpu.SMEM)
    hbm = pl.BlockSpec(memory_space=pl.ANY)
    f32, b16 = jnp.float32, jnp.bfloat16
    scratch = lambda dtype, *shape: pltpu.VMEM(shape, dtype)
    layer_out, d_embeds, d_w_in = pl.pallas_call(
        functools.partial(layer_kernel, scale),
        name="layer",
        out_shape=(jax.ShapeDtypeStruct((t, HP), b16), jax.ShapeDtypeStruct((n_cam, t, width), b16),
                   jax.ShapeDtypeStruct((part // n_cam // 2, e), f32)),
        in_specs=[smem, smem, hbm, hbm, vmem, vmem, vmem, vmem],
        out_specs=(hbm, hbm, vmem),
        scratch_shapes=[
            scratch(b16, n_cam, width, e), scratch(b16, t, d), scratch(f32, t, e), scratch(b16, t, e), scratch(b16, e, t),
            scratch(b16, NX, NY, part, t), scratch(b16, HP, t), scratch(f32, HP, t), scratch(f32, H, t, t),
            scratch(f32, H, t), scratch(f32, H, t), scratch(f32, H, t), scratch(f32, H, t),
            scratch(b16, H, P_SIZE, t), scratch(b16, H, t, t), scratch(f32, H, P_SIZE, t),
            scratch(b16, H, P_SIZE, t), scratch(b16, H, P_SIZE, t), scratch(f32, H, P_SIZE, t),
            scratch(f32, HP, t), scratch(f32, H, 8, N), scratch(f32, n_tm, 8, N),
        ] + [scratch(b16, n_tm, P_SIZE, N)] * 8 + [
            scratch(b16, t, e), scratch(b16, NX, part, 8 * t), scratch(b16, 8, t, half), scratch(b16, n_cam, t, width),
            scratch(b16, NX - 1, part, half), scratch(b16, NX - 1, part, half),
            scratch(b16, 2 * n_cam, part // n_cam // 2, half), scratch(b16, 2 * n_cam, part // n_cam // 2, half),
            scratch(f32, part, half), scratch(b16, t, HP),
            dma((n_cam,)), dma, dma, dma((n_cam,)), dma, dma,
        ] + [dma((PIECES,))] * 8 + [
            dma((2,)), dma((2,)), dma((many,)), dma((many,)), dma, dma,
            dma((many,)), dma((many,)), dma((many,)), dma((many,)),
        ],
        compiler_params=pltpu.CompilerParams(collective_id=0, has_side_effects=True, vmem_limit_bytes=60 * 1024 * 1024),
    )(clip_starts, valid_len, embeds, w_in, log_decay, clip_keep.reshape(1, H), norm_gain.reshape(HP // Q, Q), g_out)
    layer_out, d_embeds, d_w_in = finish(layer_out, d_embeds, d_w_in)
    return (layer_out[None], d_embeds, d_w_in)


def solution(mesh):
    return jax.shard_map(
        on_device,
        mesh=mesh,
        in_specs=(
            P(None, "tm", "cam"),
            P(),
            P("cam", None, "tm"),
            P(),
            P("cam", None),
            P("cam"),
            P(),
            P("cam", "tm", None),
        ),
        out_specs=(P("cam", "tm", None), P(None, "tm", "cam"), P(("cam", "tm"), None)),
        check_vma=False,
    )
```

```python
import functools
import math

import jax
import jax.numpy as jnp
from jax import lax
from jax.experimental import pallas as pl
from jax.experimental.pallas import tpu as pltpu
from jax.sharding import PartitionSpec as P

D = 2048
H = 32
P_SIZE = 64
N = 128
Q = 128
HP = 2048
NCLIP = 3


epsilon = 1e-05
MESH = pl.DeviceIdType.MESH
NX, NY, NZ = 4, 4, 8
PIECES = 2
RELAY_AT = 6
COLUMNS = ((0, 512), (512, 384), (896, 256))


def at(x, y, z, core):
    return (z, (x * NY + y) * 2 + core)


def send(src, dst, sem_a, sem_b, peer):
    return pltpu.make_async_remote_copy(
        src_ref=src, dst_ref=dst, send_sem=sem_a, recv_sem=sem_b, device_id=peer, device_id_type=MESH
    )


def wait_for(ref, sem):
    pltpu.make_async_copy(ref, ref, sem).wait()


def loop(start, end, body):
    def step(k, _):
        body(k)
        return 0
    lax.fori_loop(start, end, step, 0)


def layer_kernel(scale, starts_ref, len_ref, emb_ref, w_ref, rate_ref, keep_ref, gain_ref, g_ref,
                 out_ref, demb_ref, dw_ref,
                 wv, xin, acc, proj, xt, xtp, gt, gain, wts, cum, tail, lift, tot,
                 xw, mix, yin, dt, dl, din, lot, lg, lgot, snd1, got1, snd2, sin, snd3, got3, snd4, rin,
                 dp, xg, pg, rows_out, s2, r2, s3, r3, own, lay,
                 w_sem, o_sem, a_send, a_recv,
                 l_send, l_recv, send1, recv1, send2, recv2, send3, recv3, send4, recv4,
                 x_send, x_recv, p_send, p_recv, p_near, e_send, e_recv, send5, recv5, send6, recv6):
    f32, b16 = jnp.float32, jnp.bfloat16
    me, z = lax.axis_index("tm"), lax.axis_index("cam")
    n_tm = 2 * NX * NY
    x, y, core = me // (2 * NY), (me // 2) % NY, me % 2
    hp = H * P_SIZE
    width = emb_ref.shape[2]
    half = dp.shape[1] // 2
    group = 4

    def w_copy(j):
        c = (z + NZ - 1 - j) % NZ
        return pltpu.make_async_copy(w_ref.at[pl.ds(pl.multiple_of(c * width, width), width)], wv.at[c], w_sem.at[j])

    barrier = pltpu.get_barrier_semaphore()

    def greet(peer):
        pl.semaphore_signal(barrier, inc=1, device_id=peer, device_id_type=MESH)

    loop(1, NZ, lambda j: greet(((z + j) % NZ, me)))
    loop(1, NZ, lambda j: greet(((z + j) % NZ, me + 1 - 2 * core)))
    loop(1, n_tm, lambda j: greet((z, (me + j) % n_tm)))
    for j in (7, 0, 6, 1, 5, 2, 4, 3):
        w_copy(j).start()

    def dot(a, b):
        return jnp.dot(a, b, preferred_element_type=f32)

    def dot_t(a, b):
        return lax.dot_general(a, b, (((1,), (1,)), ((), ())), preferred_element_type=f32)

    def t_dot(a, b):
        return lax.dot_general(a, b, (((0,), (0,)), ((), ())), preferred_element_type=f32)

    def lanes_of(shape):
        return lax.broadcasted_iota(jnp.int32, shape, len(shape) - 1)

    def subs_of(shape):
        return lax.broadcasted_iota(jnp.int32, shape, 0)

    base = me * Q
    here = lanes_of((1, Q)) + base
    is_start = here == starts_ref[0, 0]
    for k in range(1, NCLIP):
        is_start = is_start | (here == starts_ref[0, k])
    keep_log = jnp.log(keep_ref[...])
    keep_col = jnp.sum(jnp.where(lanes_of((H, H)) == subs_of((H, H)), keep_log, 0.0), axis=1, keepdims=True)
    rates = rate_ref[0] + jnp.where(is_start, keep_col, 0.0)
    upper = (subs_of((Q, Q)) <= lanes_of((Q, Q)))
    running = jnp.dot(rates, upper.astype(f32), precision=lax.Precision.HIGHEST, preferred_element_type=f32)
    cum[...] = running
    tail[...] = jnp.exp(running[:, Q - 1:Q] - running)
    lift[...] = jnp.exp(running)
    tot[...] = jnp.broadcast_to(running[:, Q - 1:Q], (H, Q))
    valid = (here < len_ref[0]).astype(f32)
    valid_col = (subs_of((Q, Q)) + base < len_ref[0])

    def logs_of(h):
        lg[h] = jnp.broadcast_to(tot[pl.ds(h, 1)], (8, Q))

    loop(0, H, logs_of)

    pl.semaphore_wait(barrier, 2 * (NZ - 1) + n_tm - 1)

    def a_copy(j):
        lanes = pl.ds(pl.multiple_of(z * width, width), width)
        return send(emb_ref.at[(z + 1 + j) % NZ], xin.at[:, lanes], a_send, a_recv.at[j], ((z + 1 + j) % NZ, me))

    def block(c):
        return xin.at[:, pl.ds(pl.multiple_of(c * width, width), width)]

    a_home = pltpu.make_async_copy(emb_ref.at[z], block(z), a_recv.at[NZ - 1])
    for j in (3, 2, 4, 1, 5, 0, 6):
        a_copy(j).start()
    a_home.start()

    def apart(i):
        return (2 + 3 * i + 3 * (i // 2) + 2 * (i // 3)) % 4

    beside = [((y + apart(k // 2)) % NY) * 2 + (core + 1 + k) % 2 for k in range(2 * NY)]

    def exchange(src, dst, sem_a, sem_b, part=None):
        def copy(peer):
            if part is None:
                return send(src.at[peer], dst.at[me], sem_a, sem_b, (z, peer))
            return send(src.at[peer, part], dst.at[me, part], sem_a, sem_b, (z, peer))

        def own_block():
            if part is None:
                dst[me] = src[me]
            else:
                dst[me, part] = src[me, part]

        def start():
            def chips_at(i):
                line_x = ((x + apart(i)) % NX) * (2 * NY)
                for k in range(2 * NY):
                    peer = line_x + beside[k]
                    if k < 2 * NY - 1:
                        copy(peer).start()
                    else:
                        @pl.when(i < NX - 1)
                        def _():
                            copy(peer).start()
            loop(0, NX, chips_at)
            own_block()

        def heads_of(g):
            for i in range(group):
                peer = g * group + i

                @pl.when(peer != me)
                def _():
                    copy(peer).start()

        others = pl.ds(0, n_tm - 1)

        def wait(ref, sem):
            wait_for(ref.at[others] if part is None else ref.at[others, part], sem)

        return start, lambda: wait(dst, sem_b), lambda: wait(src, sem_a), heads_of, own_block

    pieces = [pl.ds(k * (P_SIZE // PIECES), P_SIZE // PIECES) for k in range(PIECES)]

    def exchanges(src, dst, sem_a, sem_b):
        return [exchange(src, dst, sem_a.at[k], sem_b.at[k], piece) for k, piece in enumerate(pieces)]

    logs = exchange(lg, lgot, l_send, l_recv)
    fwd_out = exchanges(snd1, got1, send1, recv1)
    fwd_back = exchanges(snd2, sin, send2, recv2)
    bwd_out = exchanges(snd3, got3, send3, recv3)
    bwd_back = exchanges(snd4, rin, send4, recv4)
    logs[0]()

    def weights_of(h):
        row = jnp.broadcast_to(cum[pl.ds(h, 1)], (Q, Q))
        wts[h] = jnp.where(upper, jnp.exp(jnp.where(upper, row - row.T, 0.0)), 0.0)

    loop(0, H, weights_of)

    def columns_of(k):
        part = pl.ds(pl.multiple_of(k * Q, Q), Q)
        gt[part] = g_ref[0, :, part].astype(f32).T.astype(b16)
        gain[part] = jnp.broadcast_to(gain_ref[pl.ds(k, 1)], (Q, Q)).T * valid

    loop(0, hp // Q, columns_of)

    piece = Q // (2 * NY)
    for n, j in enumerate((7, 0, 6, 1, 5, 2, 4, 3)):
        c = (z + NZ - 1 - j) % NZ
        w_copy(j).wait()
        if j == NZ - 1:
            a_home.wait()
            c = z
        else:
            a_copy(j).wait_recv()
        got = block(c)[...]
        term = dot(got, wv[c])
        if n == 0:
            acc[...] = term
        else:
            acc[...] += term
        for k in range(width // Q):
            turned = got[:, k * Q:(k + 1) * Q].astype(f32).T.astype(b16)
            for m in range(Q // piece):
                feature = k * Q + m * piece
                xtp[feature // (NY * piece), (feature // piece) % NY, pl.ds(pl.multiple_of(c * piece, piece), piece)] = (
                    turned[m * piece:(m + 1) * piece])

    def part_of(color, q):
        return dp.at[:, pl.ds(color * half + COLUMNS[q][0], COLUMNS[q][1])]

    def p_slot(slot, q):
        return pg.at[slot, :, pl.ds(COLUMNS[q][0], COLUMNS[q][1])]

    def x_slot(slot, u):
        return xg.at[pl.ds(2 * u, 2), :, pl.ds(pl.multiple_of(slot * Q, Q), Q)]

    def x_line(u):
        two = pl.ds(2 * u, 2)

        def copy(color, j):
            if color == 0:
                return send(xtp.at[(x + j) % NX, two], x_slot(x * 2 + core, u), x_send.at[u], x_recv.at[u],
                            at((x + j) % NX, y, z, 0))
            return send(xtp.at[two, (y + j) % NY], x_slot(y * 2 + core, u), x_send.at[u], x_recv.at[u],
                        at(x, (y + j) % NY, z, 1))
        return copy

    def p_line(q):
        def copy(color, j):
            sem = p_recv.at[q] if j == 0 else p_near.at[q, j // 2]
            if color == 0:
                return send(part_of(0, q), p_slot(x * 2 + core, q), p_send.at[q], sem, at((x + j) % NX, y, z, 0))
            return send(part_of(1, q), p_slot(y * 2 + core, q), p_send.at[q], sem, at(x, (y + j) % NY, z, 1))
        return copy

    spot = (1 - core) * x + core * y

    def relay(q):
        off, many = COLUMNS[q]
        cols = pl.ds(off, many)
        for side, step in ((0, 1), (1, 3)):
            wait_for(pg.at[pl.ds(0, 2), :, cols], p_near.at[q, side])
            from_chip = pg.at[pl.ds(2 * ((spot + 4 - step) % 4), 2), pl.ds(side * (Q // 2), Q // 2), cols]
            peer = at((x + (1 - core) * step) % NX, (y + core * step) % NY, z, core)
            send(from_chip, from_chip, p_send.at[q], p_recv.at[q], peer).start()

    def lines(what, act, steps=(2, 1, 3)):
        for j in steps:
            act(what(0, j))
            act(what(1, j))

        @pl.when(core == 0)
        def _():
            act(what(1, 0))

        @pl.when(core == 1)
        def _():
            act(what(0, 0))

    def x_rows(u):
        two = pl.ds(2 * u, 2)
        lines(x_line(u), lambda copy: copy.start())

        @pl.when(core == 0)
        def _():
            pltpu.make_async_copy(xtp.at[x, two], x_slot(x * 2, u), x_recv.at[u]).start()

        @pl.when(core == 1)
        def _():
            pltpu.make_async_copy(xtp.at[two, y], x_slot(y * 2 + 1, u), x_recv.at[u]).start()

    for k in range((hp + 2 * N) // Q):
        part = acc[:, k * Q:(k + 1) * Q]
        if k < hp // Q:
            part = jnp.where(valid_col, part, 0.0)
        proj[:, k * Q:(k + 1) * Q] = part.astype(b16)
        xt[k * Q:(k + 1) * Q] = part.T.astype(b16)

    b_nat, c_nat = proj[:, hp:hp + N], proj[:, hp + N:hp + 2 * N]
    b_t, c_t = xt[hp:hp + N], xt[hp + N:hp + 2 * N]

    def rows(g, i):
        return pl.ds(pl.multiple_of((g * group + i) * P_SIZE, P_SIZE), P_SIZE)

    def turn(gg):
        return (gg + 1 + me // group) % (H // group)

    def in_turns(body, piece):
        def step(gg):
            body(turn(gg))

            @pl.when(gg > 0)
            def _():
                piece[3](turn(gg - 1))
        loop(0, H // group, step)
        piece[3](turn(H // group - 1))
        piece[4]()

    def local_states(g):
        for i in range(group):
            h = g * group + i
            xw[h] = (xt[rows(g, i)].astype(f32) * tail[pl.ds(h, 1)]).astype(b16)
        states = dot(xw[pl.ds(g * group, group)].reshape(group * P_SIZE, Q), b_nat)
        snd1[pl.ds(g * group, group)] = states.astype(b16).reshape(group, P_SIZE, N)

    in_turns(local_states, fwd_out[0])
    for one in fwd_out[1:]:
        one[0]()
    x_rows(0)

    scores = dot(b_nat, c_t)

    def inside(g):
        for i in range(group):
            h = g * group + i
            mix[h] = (wts[h] * scores).astype(b16)
            yin[h] = dot(xt[rows(g, i)], mix[h])

    loop(0, H // group, inside)
    logs[1]()
    size = P_SIZE // PIECES

    def scan(parts, out, piece, reverse):
        def body(k, state):
            i = n_tm - 1 - k if reverse else k
            out[i, piece] = state.astype(b16).reshape(size, N)
            decay = jnp.exp(lgot[i])
            return decay[None] * state + parts[i, piece].astype(f32).reshape(size // 8, 8, N)
        lax.fori_loop(0, n_tm, body, jnp.zeros((size // 8, 8, N), f32))

    for k, piece in enumerate(pieces):
        fwd_out[k][1]()
        scan(got1, snd2, piece, False)
        fwd_back[k][0]()
    for one in fwd_back:
        one[1]()

    def norm_step(g):
        carried = dot(sin[pl.ds(g * group, group)].reshape(group * P_SIZE, N), c_t)
        for i in range(group):
            h = g * group + i
            up = lift[pl.ds(h, 1)]
            raw = yin[h] + up * carried[i * P_SIZE:(i + 1) * P_SIZE]
            inv = lax.rsqrt(jnp.mean(raw * raw, axis=0, keepdims=True) + epsilon)
            normed = raw * inv
            scaled = gain[rows(g, i)]
            lot[rows(g, i)] = normed * scaled
            d_normed = gt[rows(g, i)].astype(f32) * scaled
            d_out = inv * (d_normed - normed * jnp.mean(d_normed * normed, axis=0, keepdims=True))
            dt[h] = d_out.astype(b16)
            dl[h] = (d_out * up).astype(b16)
        states = dot(dl[pl.ds(g * group, group)].reshape(group * P_SIZE, Q), c_nat)
        snd3[pl.ds(g * group, group)] = states.astype(b16).reshape(group, P_SIZE, N)

    in_turns(norm_step, bwd_out[0])
    for one in bwd_out[1:]:
        one[0]()
    x_rows(1)

    first = subs_of((2 * P_SIZE, Q)) < P_SIZE

    def pairs(g, total):
        for i in range(0, group, 2):
            h = g * group + i
            d_two = dt[pl.ds(h, 2)].reshape(2 * P_SIZE, Q)
            zero = jnp.zeros_like(d_two)
            spread = jnp.concatenate([jnp.where(first, d_two, zero), jnp.where(first, zero, d_two)], axis=1)
            x_two = proj[:, pl.ds(pl.multiple_of(h * P_SIZE, 2 * P_SIZE), 2 * P_SIZE)]
            both = dot(x_two, spread)
            total = total + wts[h] * both[:, :Q] + wts[h + 1] * both[:, Q:]
            din[h] = dot_t(dt[h], mix[h])
            din[h + 1] = dot_t(dt[h + 1], mix[h + 1])
        return total

    pair_sum = lax.fori_loop(0, H // group, pairs, jnp.zeros((Q, Q), f32)).astype(b16)
    for k, piece in enumerate(pieces):
        bwd_out[k][1]()
        scan(got3, snd4, piece, True)
        bwd_back[k][0]()
    d_c = t_dot(pair_sum, b_nat) + t_dot(dl[...].reshape(hp, Q), sin[...].reshape(hp, N))
    d_b = dot(pair_sum, c_nat)
    dp[:, hp + N:hp + 2 * N] = d_c.astype(b16)
    for k in range(hp // Q):
        lay[:, k * Q:(k + 1) * Q] = lot[k * Q:(k + 1) * Q].T.astype(b16)
    lay_home = pltpu.make_async_copy(lay, out_ref, o_sem)
    lay_home.start()
    for one in bwd_back:
        one[1]()

    def inputs_of(k):
        after = dot(rin[2 * k:2 * k + 2].reshape(2 * P_SIZE, N), b_t)
        two = [din[2 * k + i] + tail[2 * k + i:2 * k + i + 1] * after[i * P_SIZE:(i + 1) * P_SIZE] for i in range(2)]
        dp[:, k * Q:(k + 1) * Q] = (jnp.concatenate(two, axis=0) * valid).T.astype(b16)

    done = set()
    for q, (off, many) in enumerate(COLUMNS):
        for k in range(hp // Q):
            if k not in done and any(color * half + off <= k * Q < color * half + off + many for color in range(2)):
                done.add(k)
                inputs_of(k)
        if q == len(COLUMNS) - 1:
            d_b = d_b + t_dot(xw[...].reshape(hp, Q), rin[...].reshape(hp, N))
            dp[:, hp:hp + N] = d_b.astype(b16)
        lines(p_line(q), lambda copy: copy.start(), (1, 3))

        @pl.when(core == 0)
        def _():
            pltpu.make_async_copy(part_of(0, q), p_slot(x * 2, q), p_recv.at[q]).start()

        @pl.when(core == 1)
        def _():
            pltpu.make_async_copy(part_of(1, q), p_slot(y * 2 + 1, q), p_recv.at[q]).start()

    def e_copy(j):
        return send(rows_out.at[j], demb_ref.at[z], e_send, e_recv, ((z + 1 + j) % NZ, me))

    e_home = pltpu.make_async_copy(rows_out.at[NZ - 1], demb_ref.at[z], e_recv)
    for n, j in enumerate((3, 2, 4, 1, 5, 0, 6, 7)):
        if n == RELAY_AT:
            relay(0)
        rows_out[j] = dot_t(dp[...], wv[(z + 1 + j) % NZ]).astype(b16)
        if j < NZ - 1:
            e_copy(j).start()
        else:
            e_home.start()

    p = (1 - core) * y + core * x
    line = z * 2 + core

    def second(j, q):
        k = (p + 1 + j) % NX
        peer = at((1 - core) * x + core * k, (1 - core) * k + core * y, z, core)
        cols = pl.ds(*COLUMNS[q])
        return send(s2.at[j, :, cols], r2.at[j, :, cols], send5.at[q], recv5.at[q], peer)

    def third(j, q):
        slot = (line + j) % (2 * NZ)
        cols = pl.ds(*COLUMNS[q])
        return send(s3.at[slot, :, cols], r3.at[line, :, cols], send6.at[q], recv6.at[q], at(x, y, slot // 2, slot % 2))

    for u in range(2):
        wait_for(xg.at[pl.ds(2 * u, 2)], x_recv.at[u])

    def multiply(q):
        off, many = COLUMNS[q]
        cols = slice(off, off + many)
        wait_for(pg.at[pl.ds(0, 4), :, pl.ds(off, many)], p_recv.at[q])
        right = pg[:, :, cols].reshape(8 * Q, many)
        for j in (1, 0, 2, 3):
            part = dot(xg[(p + 1 + j) % NX], right)
            if j < NX - 1:
                s2[j, :, cols] = part.astype(b16)
                second(j, q).start()
            else:
                own[:, cols] = part

    def add(q):
        off, many = COLUMNS[q]
        cols = slice(off, off + many)
        wait_for(r2.at[:, :, pl.ds(off, many)], recv5.at[q])
        own[:, cols] = (own[:, cols] + r2[0, :, cols].astype(f32) + r2[1, :, cols].astype(f32) + r2[2, :, cols].astype(f32)) * scale
        for slot in range(2 * NZ):
            s3[slot, :, cols] = own[8 * slot:8 * slot + 8, cols].astype(b16)
        for j in (8, 7, 9, 6, 10, 5, 11, 4, 12, 3, 13, 2, 14, 1, 15):
            third(j, q).start()
        r3[line, :, cols] = s3[line, :, cols]

    for q in range(1, len(COLUMNS)):
        relay(q)
    multiply(0)
    for q in range(1, len(COLUMNS)):
        multiply(q)
        add(q - 1)
    add(len(COLUMNS) - 1)
    others = pl.ds(0, 2 * NZ - 1)
    for q, (off, many) in enumerate(COLUMNS):
        wait_for(r3.at[others, :, pl.ds(off, many)], recv6.at[q])
        for color in range(2):
            sums = r3[color, :, off:off + many].astype(f32)
            for c in range(1, NZ):
                sums = sums + r3[2 * c + color, :, off:off + many].astype(f32)
            dw_ref[:, color * half + off:color * half + off + many] = sums

    lay_home.wait()
    wait_for(rows_out.at[pl.ds(0, NZ - 1)], a_send)
    wait_for(rows_out.at[pl.ds(0, NZ - 1)], e_send)
    wait_for(demb_ref, e_recv)
    for one in [logs] + fwd_out + fwd_back + bwd_out + bwd_back:
        one[2]()
    for u in range(2):
        wait_for(xg.at[pl.ds(2 * u, 2), :, pl.ds(0, 7 * Q)], x_send.at[u])
    for q, (off, many) in enumerate(COLUMNS):
        cols = pl.ds(off, many)
        wait_for(pg.at[pl.ds(0, 7), :, cols], p_send.at[q])
        wait_for(s2.at[:, :, cols], send5.at[q])
        wait_for(s3.at[others, :, cols], send6.at[q])


def finish_kernel(*refs):
    half = len(refs) // 4
    ins, outs, held, sems = refs[:half], refs[half:2 * half], refs[2 * half:3 * half], refs[3 * half:]
    loads = [pltpu.make_async_copy(a, b, sem.at[0]) for a, b, sem in zip(ins, held, sems)]
    stores = [pltpu.make_async_copy(a, b, sem.at[1]) for a, b, sem in zip(held, outs, sems)]
    for one in loads:
        one.start()
    for load, store in zip(loads, stores):
        load.wait()
        store.start()
    for one in stores:
        one.wait()


def finish(*arrays):
    hbm = pl.BlockSpec(memory_space=pl.ANY)
    return pl.pallas_call(
        finish_kernel,
        name="finish",
        out_shape=[jax.ShapeDtypeStruct(a.shape, a.dtype) for a in arrays],
        in_specs=[hbm] * len(arrays),
        out_specs=[hbm] * len(arrays),
        scratch_shapes=[pltpu.VMEM(a.shape, a.dtype) for a in arrays] + [pltpu.SemaphoreType.DMA((2,)) for _ in arrays],
    )(*arrays)


def on_device(embeds, w_in, log_decay, clip_keep, clip_starts, valid_len, norm_gain, g_out):
    n_cam, t, width = embeds.shape
    d, e = w_in.shape
    n_tm = lax.axis_size("tm")
    half, part, many = e // 2, d // NX // NY, len(COLUMNS)
    scale = 1.0 / math.sqrt(n_cam * t * n_tm)
    dma = pltpu.SemaphoreType.DMA
    vmem = pl.BlockSpec(memory_space=pltpu.VMEM)
    smem = pl.BlockSpec(memory_space=pltpu.SMEM)
    hbm = pl.BlockSpec(memory_space=pl.ANY)
    f32, b16 = jnp.float32, jnp.bfloat16
    scratch = lambda dtype, *shape: pltpu.VMEM(shape, dtype)
    layer_out, d_embeds, d_w_in = pl.pallas_call(
        functools.partial(layer_kernel, scale),
        name="layer",
        out_shape=(jax.ShapeDtypeStruct((t, HP), b16), jax.ShapeDtypeStruct((n_cam, t, width), b16),
                   jax.ShapeDtypeStruct((part // n_cam // 2, e), f32)),
        in_specs=[smem, smem, hbm, hbm, vmem, vmem, vmem, vmem],
        out_specs=(hbm, hbm, vmem),
        scratch_shapes=[
            scratch(b16, n_cam, width, e), scratch(b16, t, d), scratch(f32, t, e), scratch(b16, t, e), scratch(b16, e, t),
            scratch(b16, NX, NY, part, t), scratch(b16, HP, t), scratch(f32, HP, t), scratch(f32, H, t, t),
            scratch(f32, H, t), scratch(f32, H, t), scratch(f32, H, t), scratch(f32, H, t),
            scratch(b16, H, P_SIZE, t), scratch(b16, H, t, t), scratch(f32, H, P_SIZE, t),
            scratch(b16, H, P_SIZE, t), scratch(b16, H, P_SIZE, t), scratch(f32, H, P_SIZE, t),
            scratch(f32, HP, t), scratch(f32, H, 8, N), scratch(f32, n_tm, 8, N),
        ] + [scratch(b16, n_tm, P_SIZE, N)] * 8 + [
            scratch(b16, t, e), scratch(b16, NX, part, 8 * t), scratch(b16, 8, t, half), scratch(b16, n_cam, t, width),
            scratch(b16, NX - 1, part, half), scratch(b16, NX - 1, part, half),
            scratch(b16, 2 * n_cam, part // n_cam // 2, half), scratch(b16, 2 * n_cam, part // n_cam // 2, half),
            scratch(f32, part, half), scratch(b16, t, HP),
            dma((n_cam,)), dma, dma, dma((n_cam,)), dma, dma,
        ] + [dma((PIECES,))] * 8 + [
            dma((2,)), dma((2,)), dma((many,)), dma((many,)), dma((many, 2)), dma, dma,
            dma((many,)), dma((many,)), dma((many,)), dma((many,)),
        ],
        compiler_params=pltpu.CompilerParams(collective_id=0, has_side_effects=True, vmem_limit_bytes=60 * 1024 * 1024),
    )(clip_starts, valid_len, embeds, w_in, log_decay, clip_keep.reshape(1, H), norm_gain.reshape(HP // Q, Q), g_out)
    layer_out, d_embeds, d_w_in = finish(layer_out, d_embeds, d_w_in)
    return (layer_out[None], d_embeds, d_w_in)


def solution(mesh):
    return jax.shard_map(
        on_device,
        mesh=mesh,
        in_specs=(
            P(None, "tm", "cam"),
            P(),
            P("cam", None, "tm"),
            P(),
            P("cam", None),
            P("cam"),
            P(),
            P("cam", "tm", None),
        ),
        out_specs=(P("cam", "tm", None), P(None, "tm", "cam"), P(("cam", "tm"), None)),
        check_vma=False,
    )
```

```python
import functools
import math

import jax
import jax.numpy as jnp
from jax import lax
from jax.experimental import pallas as pl
from jax.experimental.pallas import tpu as pltpu
from jax.sharding import PartitionSpec as P

D = 2048
H = 32
P_SIZE = 64
N = 128
Q = 128
HP = 2048
NCLIP = 3


epsilon = 1e-05
MESH = pl.DeviceIdType.MESH
NX, NY, NZ = 4, 4, 8
PIECES = 2
RELAY_AT = 6
COLUMNS = ((0, 512), (512, 384), (896, 256))


def at(x, y, z, core):
    return (z, (x * NY + y) * 2 + core)


def send(src, dst, sem_a, sem_b, peer):
    return pltpu.make_async_remote_copy(
        src_ref=src, dst_ref=dst, send_sem=sem_a, recv_sem=sem_b, device_id=peer, device_id_type=MESH
    )


def wait_for(ref, sem):
    pltpu.make_async_copy(ref, ref, sem).wait()


def loop(start, end, body):
    def step(k, _):
        body(k)
        return 0
    lax.fori_loop(start, end, step, 0)


def layer_kernel(scale, starts_ref, len_ref, emb_ref, w_ref, rate_hbm, keep_ref, gain_hbm, g_hbm,
                 out_ref, demb_ref, dw_ref,
                 wv, xin, acc, proj, xt, xtp, gt, gain, wts, cum, tail, lift, tot,
                 xw, mix, yin, dt, dl, din, lot, lg, lgot, snd1, got1, snd2, sin, snd3, got3, snd4, rin,
                 dp, xg, pg, rows_out, s2, r2, s3, r3, own, lay, rate_ref, gain_ref, g_ref,
                 w_sem, o_sem, in_sem, a_send, a_recv,
                 l_send, l_recv, send1, recv1, send2, recv2, send3, recv3, send4, recv4,
                 x_send, x_recv, p_send, p_recv, p_near, e_send, e_recv, send5, recv5, send6, recv6):
    f32, b16 = jnp.float32, jnp.bfloat16
    me, z = lax.axis_index("tm"), lax.axis_index("cam")
    n_tm = 2 * NX * NY
    x, y, core = me // (2 * NY), (me // 2) % NY, me % 2
    hp = H * P_SIZE
    width = emb_ref.shape[2]
    half = dp.shape[1] // 2
    group = 8

    def w_copy(j):
        c = (z + NZ - 1 - j) % NZ
        return pltpu.make_async_copy(w_ref.at[pl.ds(pl.multiple_of(c * width, width), width)], wv.at[c], w_sem.at[j])

    loads = [pltpu.make_async_copy(a, b, in_sem.at[k]) for k, (a, b) in enumerate(
        ((rate_hbm, rate_ref), (gain_hbm, gain_ref), (g_hbm, g_ref)))]
    for one in loads:
        one.start()
    barrier = pltpu.get_barrier_semaphore()

    def greet(peer):
        pl.semaphore_signal(barrier, inc=1, device_id=peer, device_id_type=MESH)

    loop(1, NZ, lambda j: greet(((z + j) % NZ, me)))
    loop(1, NZ, lambda j: greet(((z + j) % NZ, me + 1 - 2 * core)))
    loop(1, n_tm, lambda j: greet((z, (me + j) % n_tm)))
    for j in (7, 0, 6, 1, 5, 2, 4, 3):
        w_copy(j).start()

    def dot(a, b):
        return jnp.dot(a, b, preferred_element_type=f32)

    def dot_t(a, b):
        return lax.dot_general(a, b, (((1,), (1,)), ((), ())), preferred_element_type=f32)

    def t_dot(a, b):
        return lax.dot_general(a, b, (((0,), (0,)), ((), ())), preferred_element_type=f32)

    def lanes_of(shape):
        return lax.broadcasted_iota(jnp.int32, shape, len(shape) - 1)

    def subs_of(shape):
        return lax.broadcasted_iota(jnp.int32, shape, 0)

    base = me * Q
    here = lanes_of((1, Q)) + base
    is_start = here == starts_ref[0, 0]
    for k in range(1, NCLIP):
        is_start = is_start | (here == starts_ref[0, k])
    keep_log = jnp.log(keep_ref[...])
    keep_col = jnp.sum(jnp.where(lanes_of((H, H)) == subs_of((H, H)), keep_log, 0.0), axis=1, keepdims=True)
    loads[0].wait()
    rates = rate_ref[0] + jnp.where(is_start, keep_col, 0.0)
    upper = (subs_of((Q, Q)) <= lanes_of((Q, Q)))
    running = jnp.dot(rates, upper.astype(f32), precision=lax.Precision.HIGHEST, preferred_element_type=f32)
    cum[...] = running
    tail[...] = jnp.exp(running[:, Q - 1:Q] - running)
    lift[...] = jnp.exp(running)
    tot[...] = jnp.broadcast_to(running[:, Q - 1:Q], (H, Q))
    valid = (here < len_ref[0]).astype(f32)
    valid_col = (subs_of((Q, Q)) + base < len_ref[0])

    def logs_of(h):
        lg[h] = jnp.broadcast_to(tot[pl.ds(h, 1)], (8, Q))

    loop(0, H, logs_of)

    pl.semaphore_wait(barrier, 2 * (NZ - 1) + n_tm - 1)

    def a_copy(j):
        lanes = pl.ds(pl.multiple_of(z * width, width), width)
        return send(emb_ref.at[(z + 1 + j) % NZ], xin.at[:, lanes], a_send, a_recv.at[j], ((z + 1 + j) % NZ, me))

    def block(c):
        return xin.at[:, pl.ds(pl.multiple_of(c * width, width), width)]

    a_home = pltpu.make_async_copy(emb_ref.at[z], block(z), a_recv.at[NZ - 1])
    for j in (3, 2, 4, 1, 5, 0, 6):
        a_copy(j).start()
    a_home.start()

    def apart(i):
        return (2 + 3 * i + 3 * (i // 2) + 2 * (i // 3)) % 4

    beside = [((y + apart(k // 2)) % NY) * 2 + (core + 1 + k) % 2 for k in range(2 * NY)]

    def exchange(src, dst, sem_a, sem_b, part=None):
        def copy(peer):
            if part is None:
                return send(src.at[peer], dst.at[me], sem_a, sem_b, (z, peer))
            return send(src.at[peer, part], dst.at[me, part], sem_a, sem_b, (z, peer))

        def own_block():
            if part is None:
                dst[me] = src[me]
            else:
                dst[me, part] = src[me, part]

        def start():
            def chips_at(i):
                line_x = ((x + apart(i)) % NX) * (2 * NY)
                for k in range(2 * NY):
                    peer = line_x + beside[k]
                    if k < 2 * NY - 1:
                        copy(peer).start()
                    else:
                        @pl.when(i < NX - 1)
                        def _():
                            copy(peer).start()
            loop(0, NX, chips_at)
            own_block()

        def heads_of(g):
            for i in range(group):
                peer = g * group + i

                @pl.when(peer != me)
                def _():
                    copy(peer).start()

        others = pl.ds(0, n_tm - 1)

        def wait(ref, sem):
            wait_for(ref.at[others] if part is None else ref.at[others, part], sem)

        return start, lambda: wait(dst, sem_b), lambda: wait(src, sem_a), heads_of, own_block

    pieces = [pl.ds(k * (P_SIZE // PIECES), P_SIZE // PIECES) for k in range(PIECES)]

    def exchanges(src, dst, sem_a, sem_b):
        return [exchange(src, dst, sem_a.at[k], sem_b.at[k], piece) for k, piece in enumerate(pieces)]

    logs = exchange(lg, lgot, l_send, l_recv)
    fwd_out = exchanges(snd1, got1, send1, recv1)
    fwd_back = exchanges(snd2, sin, send2, recv2)
    bwd_out = exchanges(snd3, got3, send3, recv3)
    bwd_back = exchanges(snd4, rin, send4, recv4)
    logs[0]()

    def weights_of(h):
        row = jnp.broadcast_to(cum[pl.ds(h, 1)], (Q, Q))
        wts[h] = jnp.where(upper, jnp.exp(jnp.where(upper, row - row.T, 0.0)), 0.0)

    loop(0, H, weights_of)

    loads[1].wait()
    loads[2].wait()

    def columns_of(k):
        part = pl.ds(pl.multiple_of(k * Q, Q), Q)
        gt[part] = g_ref[0, :, part].astype(f32).T.astype(b16)
        gain[part] = jnp.broadcast_to(gain_ref[pl.ds(k, 1)], (Q, Q)).T * valid

    loop(0, hp // Q, columns_of)

    piece = Q // (2 * NY)
    for n, j in enumerate((7, 0, 6, 1, 5, 2, 4, 3)):
        c = (z + NZ - 1 - j) % NZ
        w_copy(j).wait()
        if j == NZ - 1:
            a_home.wait()
            c = z
        else:
            a_copy(j).wait_recv()
        got = block(c)[...]
        term = dot(got, wv[c])
        if n == 0:
            acc[...] = term
        else:
            acc[...] += term
        for k in range(width // Q):
            turned = got[:, k * Q:(k + 1) * Q].astype(f32).T.astype(b16)
            for m in range(Q // piece):
                feature = k * Q + m * piece
                xtp[feature // (NY * piece), (feature // piece) % NY, pl.ds(pl.multiple_of(c * piece, piece), piece)] = (
                    turned[m * piece:(m + 1) * piece])

    def part_of(color, q):
        return dp.at[:, pl.ds(color * half + COLUMNS[q][0], COLUMNS[q][1])]

    def p_slot(slot, q):
        return pg.at[slot, :, pl.ds(COLUMNS[q][0], COLUMNS[q][1])]

    def x_slot(slot, u):
        return xg.at[pl.ds(2 * u, 2), :, pl.ds(pl.multiple_of(slot * Q, Q), Q)]

    def x_line(u):
        two = pl.ds(2 * u, 2)

        def copy(color, j):
            if color == 0:
                return send(xtp.at[(x + j) % NX, two], x_slot(x * 2 + core, u), x_send.at[u], x_recv.at[u],
                            at((x + j) % NX, y, z, 0))
            return send(xtp.at[two, (y + j) % NY], x_slot(y * 2 + core, u), x_send.at[u], x_recv.at[u],
                        at(x, (y + j) % NY, z, 1))
        return copy

    def p_line(q):
        def copy(color, j):
            sem = p_recv.at[q] if j == 0 else p_near.at[q, j // 2]
            if color == 0:
                return send(part_of(0, q), p_slot(x * 2 + core, q), p_send.at[q], sem, at((x + j) % NX, y, z, 0))
            return send(part_of(1, q), p_slot(y * 2 + core, q), p_send.at[q], sem, at(x, (y + j) % NY, z, 1))
        return copy

    spot = (1 - core) * x + core * y

    def relay(q):
        off, many = COLUMNS[q]
        cols = pl.ds(off, many)
        for side, step in ((0, 1), (1, 3)):
            wait_for(pg.at[pl.ds(0, 2), :, cols], p_near.at[q, side])
            from_chip = pg.at[pl.ds(2 * ((spot + 4 - step) % 4), 2), pl.ds(side * (Q // 2), Q // 2), cols]
            peer = at((x + (1 - core) * step) % NX, (y + core * step) % NY, z, core)
            send(from_chip, from_chip, p_send.at[q], p_recv.at[q], peer).start()

    def lines(what, act, steps=(2, 1, 3)):
        for j in steps:
            act(what(0, j))
            act(what(1, j))

        @pl.when(core == 0)
        def _():
            act(what(1, 0))

        @pl.when(core == 1)
        def _():
            act(what(0, 0))

    def x_rows(u):
        two = pl.ds(2 * u, 2)
        lines(x_line(u), lambda copy: copy.start())

        @pl.when(core == 0)
        def _():
            pltpu.make_async_copy(xtp.at[x, two], x_slot(x * 2, u), x_recv.at[u]).start()

        @pl.when(core == 1)
        def _():
            pltpu.make_async_copy(xtp.at[two, y], x_slot(y * 2 + 1, u), x_recv.at[u]).start()

    for k in range((hp + 2 * N) // Q):
        part = acc[:, k * Q:(k + 1) * Q]
        if k < hp // Q:
            part = jnp.where(valid_col, part, 0.0)
        proj[:, k * Q:(k + 1) * Q] = part.astype(b16)
        xt[k * Q:(k + 1) * Q] = part.T.astype(b16)

    b_nat, c_nat = proj[:, hp:hp + N], proj[:, hp + N:hp + 2 * N]
    b_t, c_t = xt[hp:hp + N], xt[hp + N:hp + 2 * N]

    def rows(g, i):
        return pl.ds(pl.multiple_of((g * group + i) * P_SIZE, P_SIZE), P_SIZE)

    def turn(gg):
        return (gg + 1 + me // group) % (H // group)

    def in_turns(body, piece):
        def step(gg):
            body(turn(gg))

            @pl.when(gg > 0)
            def _():
                piece[3](turn(gg - 1))
        loop(0, H // group, step)
        piece[3](turn(H // group - 1))
        piece[4]()

    def local_states(g):
        for i in range(group):
            h = g * group + i
            xw[h] = (xt[rows(g, i)].astype(f32) * tail[pl.ds(h, 1)]).astype(b16)
        states = dot(xw[pl.ds(g * group, group)].reshape(group * P_SIZE, Q), b_nat)
        snd1[pl.ds(g * group, group)] = states.astype(b16).reshape(group, P_SIZE, N)

    in_turns(local_states, fwd_out[0])
    for one in fwd_out[1:]:
        one[0]()
    x_rows(0)

    scores = dot(b_nat, c_t)

    def inside(g):
        for i in range(group):
            h = g * group + i
            mix[h] = (wts[h] * scores).astype(b16)
            yin[h] = dot(xt[rows(g, i)], mix[h])

    loop(0, H // group, inside)
    logs[1]()
    size = P_SIZE // PIECES

    def scan(parts, out, piece, reverse):
        def body(k, state):
            i = n_tm - 1 - k if reverse else k
            out[i, piece] = state.astype(b16).reshape(size, N)
            decay = jnp.exp(lgot[i])
            return decay[None] * state + parts[i, piece].astype(f32).reshape(size // 8, 8, N)
        lax.fori_loop(0, n_tm, body, jnp.zeros((size // 8, 8, N), f32))

    for k, piece in enumerate(pieces):
        fwd_out[k][1]()
        scan(got1, snd2, piece, False)
        fwd_back[k][0]()
    for one in fwd_back:
        one[1]()

    def norm_step(g):
        carried = dot(sin[pl.ds(g * group, group)].reshape(group * P_SIZE, N), c_t)
        for i in range(group):
            h = g * group + i
            up = lift[pl.ds(h, 1)]
            raw = yin[h] + up * carried[i * P_SIZE:(i + 1) * P_SIZE]
            inv = lax.rsqrt(jnp.mean(raw * raw, axis=0, keepdims=True) + epsilon)
            normed = raw * inv
            scaled = gain[rows(g, i)]
            lot[rows(g, i)] = normed * scaled
            d_normed = gt[rows(g, i)].astype(f32) * scaled
            d_out = inv * (d_normed - normed * jnp.mean(d_normed * normed, axis=0, keepdims=True))
            dt[h] = d_out.astype(b16)
            dl[h] = (d_out * up).astype(b16)
        states = dot(dl[pl.ds(g * group, group)].reshape(group * P_SIZE, Q), c_nat)
        snd3[pl.ds(g * group, group)] = states.astype(b16).reshape(group, P_SIZE, N)

    in_turns(norm_step, bwd_out[0])
    for one in bwd_out[1:]:
        one[0]()
    x_rows(1)

    first = subs_of((2 * P_SIZE, Q)) < P_SIZE

    def pairs(g, total):
        for i in range(0, group, 2):
            h = g * group + i
            d_two = dt[pl.ds(h, 2)].reshape(2 * P_SIZE, Q)
            zero = jnp.zeros_like(d_two)
            spread = jnp.concatenate([jnp.where(first, d_two, zero), jnp.where(first, zero, d_two)], axis=1)
            x_two = proj[:, pl.ds(pl.multiple_of(h * P_SIZE, 2 * P_SIZE), 2 * P_SIZE)]
            both = dot(x_two, spread)
            total = total + wts[h] * both[:, :Q] + wts[h + 1] * both[:, Q:]
            din[h] = dot_t(dt[h], mix[h])
            din[h + 1] = dot_t(dt[h + 1], mix[h + 1])
        return total

    pair_sum = lax.fori_loop(0, H // group, pairs, jnp.zeros((Q, Q), f32)).astype(b16)
    for k, piece in enumerate(pieces):
        bwd_out[k][1]()
        scan(got3, snd4, piece, True)
        bwd_back[k][0]()
    d_c = t_dot(pair_sum, b_nat) + t_dot(dl[...].reshape(hp, Q), sin[...].reshape(hp, N))
    d_b = dot(pair_sum, c_nat)
    dp[:, hp + N:hp + 2 * N] = d_c.astype(b16)
    for k in range(hp // Q):
        lay[:, k * Q:(k + 1) * Q] = lot[k * Q:(k + 1) * Q].T.astype(b16)
    lay_home = pltpu.make_async_copy(lay, out_ref, o_sem)
    lay_home.start()
    for one in bwd_back:
        one[1]()

    def inputs_of(k):
        after = dot(rin[2 * k:2 * k + 2].reshape(2 * P_SIZE, N), b_t)
        two = [din[2 * k + i] + tail[2 * k + i:2 * k + i + 1] * after[i * P_SIZE:(i + 1) * P_SIZE] for i in range(2)]
        dp[:, k * Q:(k + 1) * Q] = (jnp.concatenate(two, axis=0) * valid).T.astype(b16)

    done = set()
    for q, (off, many) in enumerate(COLUMNS):
        for k in range(hp // Q):
            if k not in done and any(color * half + off <= k * Q < color * half + off + many for color in range(2)):
                done.add(k)
                inputs_of(k)
        if q == len(COLUMNS) - 1:
            d_b = d_b + t_dot(xw[...].reshape(hp, Q), rin[...].reshape(hp, N))
            dp[:, hp:hp + N] = d_b.astype(b16)
        lines(p_line(q), lambda copy: copy.start(), (1, 3))

        @pl.when(core == 0)
        def _():
            pltpu.make_async_copy(part_of(0, q), p_slot(x * 2, q), p_recv.at[q]).start()

        @pl.when(core == 1)
        def _():
            pltpu.make_async_copy(part_of(1, q), p_slot(y * 2 + 1, q), p_recv.at[q]).start()

    def e_copy(j):
        return send(rows_out.at[j], demb_ref.at[z], e_send, e_recv, ((z + 1 + j) % NZ, me))

    e_home = pltpu.make_async_copy(rows_out.at[NZ - 1], demb_ref.at[z], e_recv)
    for n, j in enumerate((3, 2, 4, 1, 5, 0, 6, 7)):
        if n == RELAY_AT:
            relay(0)
        rows_out[j] = dot_t(dp[...], wv[(z + 1 + j) % NZ]).astype(b16)
        if j < NZ - 1:
            e_copy(j).start()
        else:
            e_home.start()

    p = (1 - core) * y + core * x
    line = z * 2 + core

    def second(j, q):
        k = (p + 1 + j) % NX
        peer = at((1 - core) * x + core * k, (1 - core) * k + core * y, z, core)
        cols = pl.ds(*COLUMNS[q])
        return send(s2.at[j, :, cols], r2.at[j, :, cols], send5.at[q], recv5.at[q], peer)

    def third(j, q):
        slot = (line + j) % (2 * NZ)
        cols = pl.ds(*COLUMNS[q])
        return send(s3.at[slot, :, cols], r3.at[line, :, cols], send6.at[q], recv6.at[q], at(x, y, slot // 2, slot % 2))

    for u in range(2):
        wait_for(xg.at[pl.ds(2 * u, 2)], x_recv.at[u])

    def multiply(q):
        off, many = COLUMNS[q]
        cols = slice(off, off + many)
        wait_for(pg.at[pl.ds(0, 4), :, pl.ds(off, many)], p_recv.at[q])
        right = pg[:, :, cols].reshape(8 * Q, many)
        for j in (1, 0, 2, 3):
            part = dot(xg[(p + 1 + j) % NX], right)
            if j < NX - 1:
                s2[j, :, cols] = part.astype(b16)
                second(j, q).start()
            else:
                own[:, cols] = part

    def add(q):
        off, many = COLUMNS[q]
        cols = slice(off, off + many)
        wait_for(r2.at[:, :, pl.ds(off, many)], recv5.at[q])
        own[:, cols] = (own[:, cols] + r2[0, :, cols].astype(f32) + r2[1, :, cols].astype(f32) + r2[2, :, cols].astype(f32)) * scale
        for slot in range(2 * NZ):
            s3[slot, :, cols] = own[8 * slot:8 * slot + 8, cols].astype(b16)
        for j in (8, 7, 9, 6, 10, 5, 11, 4, 12, 3, 13, 2, 14, 1, 15):
            third(j, q).start()
        r3[line, :, cols] = s3[line, :, cols]

    for q in range(1, len(COLUMNS)):
        relay(q)
    multiply(0)
    for q in range(1, len(COLUMNS)):
        multiply(q)
        add(q - 1)
    add(len(COLUMNS) - 1)
    others = pl.ds(0, 2 * NZ - 1)
    for q, (off, many) in enumerate(COLUMNS):
        wait_for(r3.at[others, :, pl.ds(off, many)], recv6.at[q])
        for color in range(2):
            sums = r3[color, :, off:off + many].astype(f32)
            for c in range(1, NZ):
                sums = sums + r3[2 * c + color, :, off:off + many].astype(f32)
            dw_ref[:, color * half + off:color * half + off + many] = sums

    lay_home.wait()
    wait_for(rows_out.at[pl.ds(0, NZ - 1)], a_send)
    wait_for(rows_out.at[pl.ds(0, NZ - 1)], e_send)
    wait_for(demb_ref, e_recv)
    for one in [logs] + fwd_out + fwd_back + bwd_out + bwd_back:
        one[2]()
    for u in range(2):
        wait_for(xg.at[pl.ds(2 * u, 2), :, pl.ds(0, 7 * Q)], x_send.at[u])
    for q, (off, many) in enumerate(COLUMNS):
        cols = pl.ds(off, many)
        wait_for(pg.at[pl.ds(0, 7), :, cols], p_send.at[q])
        wait_for(s2.at[:, :, cols], send5.at[q])
        wait_for(s3.at[others, :, cols], send6.at[q])


def finish_kernel(*refs):
    half = len(refs) // 4
    ins, outs, held, sems = refs[:half], refs[half:2 * half], refs[2 * half:3 * half], refs[3 * half:]
    loads = [pltpu.make_async_copy(a, b, sem.at[0]) for a, b, sem in zip(ins, held, sems)]
    stores = [pltpu.make_async_copy(a, b, sem.at[1]) for a, b, sem in zip(held, outs, sems)]
    for one in loads:
        one.start()
    for load, store in zip(loads, stores):
        load.wait()
        store.start()
    for one in stores:
        one.wait()


def finish(*arrays):
    hbm = pl.BlockSpec(memory_space=pl.ANY)
    return pl.pallas_call(
        finish_kernel,
        name="finish",
        out_shape=[jax.ShapeDtypeStruct(a.shape, a.dtype) for a in arrays],
        in_specs=[hbm] * len(arrays),
        out_specs=[hbm] * len(arrays),
        scratch_shapes=[pltpu.VMEM(a.shape, a.dtype) for a in arrays] + [pltpu.SemaphoreType.DMA((2,)) for _ in arrays],
    )(*arrays)


def on_device(embeds, w_in, log_decay, clip_keep, clip_starts, valid_len, norm_gain, g_out):
    n_cam, t, width = embeds.shape
    d, e = w_in.shape
    n_tm = lax.axis_size("tm")
    half, part, many = e // 2, d // NX // NY, len(COLUMNS)
    scale = 1.0 / math.sqrt(n_cam * t * n_tm)
    dma = pltpu.SemaphoreType.DMA
    vmem = pl.BlockSpec(memory_space=pltpu.VMEM)
    smem = pl.BlockSpec(memory_space=pltpu.SMEM)
    hbm = pl.BlockSpec(memory_space=pl.ANY)
    f32, b16 = jnp.float32, jnp.bfloat16
    scratch = lambda dtype, *shape: pltpu.VMEM(shape, dtype)
    layer_out, d_embeds, d_w_in = pl.pallas_call(
        functools.partial(layer_kernel, scale),
        name="layer",
        out_shape=(jax.ShapeDtypeStruct((t, HP), b16), jax.ShapeDtypeStruct((n_cam, t, width), b16),
                   jax.ShapeDtypeStruct((part // n_cam // 2, e), f32)),
        in_specs=[smem, smem, hbm, hbm, hbm, vmem, hbm, hbm],
        out_specs=(hbm, hbm, vmem),
        scratch_shapes=[
            scratch(b16, n_cam, width, e), scratch(b16, t, d), scratch(f32, t, e), scratch(b16, t, e), scratch(b16, e, t),
            scratch(b16, NX, NY, part, t), scratch(b16, HP, t), scratch(f32, HP, t), scratch(f32, H, t, t),
            scratch(f32, H, t), scratch(f32, H, t), scratch(f32, H, t), scratch(f32, H, t),
            scratch(b16, H, P_SIZE, t), scratch(b16, H, t, t), scratch(f32, H, P_SIZE, t),
            scratch(b16, H, P_SIZE, t), scratch(b16, H, P_SIZE, t), scratch(f32, H, P_SIZE, t),
            scratch(f32, HP, t), scratch(f32, H, 8, N), scratch(f32, n_tm, 8, N),
        ] + [scratch(b16, n_tm, P_SIZE, N)] * 8 + [
            scratch(b16, t, e), scratch(b16, NX, part, 8 * t), scratch(b16, 8, t, half), scratch(b16, n_cam, t, width),
            scratch(b16, NX - 1, part, half), scratch(b16, NX - 1, part, half),
            scratch(b16, 2 * n_cam, part // n_cam // 2, half), scratch(b16, 2 * n_cam, part // n_cam // 2, half),
            scratch(f32, part, half), scratch(b16, t, HP),
            scratch(f32, 1, H, t), scratch(f32, HP // Q, Q), scratch(b16, 1, t, HP),
            dma((n_cam,)), dma, dma((3,)), dma, dma((n_cam,)), dma, dma,
        ] + [dma((PIECES,))] * 8 + [
            dma((2,)), dma((2,)), dma((many,)), dma((many,)), dma((many, 2)), dma, dma,
            dma((many,)), dma((many,)), dma((many,)), dma((many,)),
        ],
        compiler_params=pltpu.CompilerParams(collective_id=0, has_side_effects=True, vmem_limit_bytes=60 * 1024 * 1024),
    )(clip_starts, valid_len, embeds, w_in, log_decay, clip_keep.reshape(1, H), norm_gain.reshape(HP // Q, Q), g_out)
    layer_out, d_embeds, d_w_in = finish(layer_out, d_embeds, d_w_in)
    return (layer_out[None], d_embeds, d_w_in)


def solution(mesh):
    return jax.shard_map(
        on_device,
        mesh=mesh,
        in_specs=(
            P(None, "tm", "cam"),
            P(),
            P("cam", None, "tm"),
            P(),
            P("cam", None),
            P("cam"),
            P(),
            P("cam", "tm", None),
        ),
        out_specs=(P("cam", "tm", None), P(None, "tm", "cam"), P(("cam", "tm"), None)),
        check_vma=False,
    )
```

```python
import functools
import math

import jax
import jax.numpy as jnp
from jax import lax
from jax.experimental import pallas as pl
from jax.experimental.pallas import tpu as pltpu
from jax.sharding import PartitionSpec as P

D = 2048
H = 32
P_SIZE = 64
N = 128
Q = 128
HP = 2048
NCLIP = 3


epsilon = 1e-05
MESH = pl.DeviceIdType.MESH
NX, NY, NZ = 4, 4, 8
PIECES = 2
RELAY_AT = 6
COLUMNS = ((0, 512), (512, 384), (896, 256))


def at(x, y, z, core):
    return (z, (x * NY + y) * 2 + core)


def send(src, dst, sem_a, sem_b, peer):
    return pltpu.make_async_remote_copy(
        src_ref=src, dst_ref=dst, send_sem=sem_a, recv_sem=sem_b, device_id=peer, device_id_type=MESH
    )


def wait_for(ref, sem):
    pltpu.make_async_copy(ref, ref, sem).wait()


def loop(start, end, body):
    def step(k, _):
        body(k)
        return 0
    lax.fori_loop(start, end, step, 0)


def layer_kernel(scale, starts_ref, len_ref, emb_ref, w_ref, rate_hbm, keep_ref, gain_hbm, g_hbm,
                 out_ref, demb_ref, dw_ref,
                 wv, xin, acc, proj, xt, xtp, gt, gain, wts, cum, tail, lift, tot,
                 xw, mix, yin, dt, dl, din, lot, lg, lgot, snd1, got1, snd2, sin, snd3, got3, snd4, rin,
                 dp, xg, pg, rows_out, s2, r2, s3, r3, own, lay, rate_ref, gain_ref, g_ref,
                 w_sem, o_sem, in_sem, a_send, a_recv,
                 l_send, l_recv, send1, recv1, send2, recv2, send3, recv3, send4, recv4,
                 x_send, x_recv, p_send, p_recv, p_near, e_send, e_recv, send5, recv5, send6, recv6):
    f32, b16 = jnp.float32, jnp.bfloat16
    me, z = lax.axis_index("tm"), lax.axis_index("cam")
    n_tm = 2 * NX * NY
    x, y, core = me // (2 * NY), (me // 2) % NY, me % 2
    hp = H * P_SIZE
    width = emb_ref.shape[2]
    half = dp.shape[1] // 2
    group = 8

    def w_copy(j):
        c = (z + NZ - 1 - j) % NZ
        return pltpu.make_async_copy(w_ref.at[pl.ds(pl.multiple_of(c * width, width), width)], wv.at[c], w_sem.at[j])

    loads = [pltpu.make_async_copy(a, b, in_sem.at[k]) for k, (a, b) in enumerate(
        ((rate_hbm, rate_ref), (gain_hbm, gain_ref), (g_hbm, g_ref)))]
    for one in loads:
        one.start()
    barrier = pltpu.get_barrier_semaphore()

    def greet(peer):
        pl.semaphore_signal(barrier, inc=1, device_id=peer, device_id_type=MESH)

    loop(1, NZ, lambda j: greet(((z + j) % NZ, me)))
    loop(1, NZ, lambda j: greet(((z + j) % NZ, me + 1 - 2 * core)))
    loop(1, n_tm, lambda j: greet((z, (me + j) % n_tm)))
    for j in (7, 0, 6, 1, 5, 2, 4, 3):
        w_copy(j).start()

    def dot(a, b):
        return jnp.dot(a, b, preferred_element_type=f32)

    def dot_t(a, b):
        return lax.dot_general(a, b, (((1,), (1,)), ((), ())), preferred_element_type=f32)

    def t_dot(a, b):
        return lax.dot_general(a, b, (((0,), (0,)), ((), ())), preferred_element_type=f32)

    def lanes_of(shape):
        return lax.broadcasted_iota(jnp.int32, shape, len(shape) - 1)

    def subs_of(shape):
        return lax.broadcasted_iota(jnp.int32, shape, 0)

    base = me * Q
    here = lanes_of((1, Q)) + base
    is_start = here == starts_ref[0, 0]
    for k in range(1, NCLIP):
        is_start = is_start | (here == starts_ref[0, k])
    keep_log = jnp.log(keep_ref[...])
    keep_col = jnp.sum(jnp.where(lanes_of((H, H)) == subs_of((H, H)), keep_log, 0.0), axis=1, keepdims=True)
    loads[0].wait()
    rates = rate_ref[0] + jnp.where(is_start, keep_col, 0.0)
    upper = (subs_of((Q, Q)) <= lanes_of((Q, Q)))
    running = jnp.dot(rates, upper.astype(f32), precision=lax.Precision.HIGHEST, preferred_element_type=f32)
    cum[...] = running
    tail[...] = jnp.exp(running[:, Q - 1:Q] - running)
    lift[...] = jnp.exp(running)
    tot[...] = jnp.broadcast_to(running[:, Q - 1:Q], (H, Q))
    valid = (here < len_ref[0]).astype(f32)
    valid_col = (subs_of((Q, Q)) + base < len_ref[0])

    def logs_of(h):
        lg[h] = jnp.broadcast_to(tot[pl.ds(h, 1)], (8, Q))

    loop(0, H, logs_of)

    pl.semaphore_wait(barrier, 2 * (NZ - 1) + n_tm - 1)

    def a_copy(j):
        lanes = pl.ds(pl.multiple_of(z * width, width), width)
        return send(emb_ref.at[(z + 1 + j) % NZ], xin.at[:, lanes], a_send, a_recv.at[j], ((z + 1 + j) % NZ, me))

    def block(c):
        return xin.at[:, pl.ds(pl.multiple_of(c * width, width), width)]

    a_home = pltpu.make_async_copy(emb_ref.at[z], block(z), a_recv.at[NZ - 1])
    for j in (3, 2, 4, 1, 5, 0, 6):
        a_copy(j).start()
    a_home.start()

    def apart(i):
        return (2 + 3 * i + 3 * (i // 2) + 2 * (i // 3)) % 4

    beside = [((y + apart(k // 2)) % NY) * 2 + (core + 1 + k) % 2 for k in range(2 * NY)]

    def exchange(src, dst, sem_a, sem_b, part=None):
        def copy(peer):
            if part is None:
                return send(src.at[peer], dst.at[me], sem_a, sem_b, (z, peer))
            return send(src.at[peer, part], dst.at[me, part], sem_a, sem_b, (z, peer))

        def own_block():
            if part is None:
                dst[me] = src[me]
            else:
                dst[me, part] = src[me, part]

        def start():
            def chips_at(i):
                line_x = ((x + apart(i)) % NX) * (2 * NY)
                for k in range(2 * NY):
                    peer = line_x + beside[k]
                    if k < 2 * NY - 1:
                        copy(peer).start()
                    else:
                        @pl.when(i < NX - 1)
                        def _():
                            copy(peer).start()
            loop(0, NX, chips_at)
            own_block()

        def heads_of(g):
            for i in range(group):
                peer = g * group + i

                @pl.when(peer != me)
                def _():
                    copy(peer).start()

        others = pl.ds(0, n_tm - 1)

        def wait(ref, sem):
            wait_for(ref.at[others] if part is None else ref.at[others, part], sem)

        return start, lambda: wait(dst, sem_b), lambda: wait(src, sem_a), heads_of, own_block

    pieces = [pl.ds(k * (P_SIZE // PIECES), P_SIZE // PIECES) for k in range(PIECES)]

    def exchanges(src, dst, sem_a, sem_b):
        return [exchange(src, dst, sem_a.at[k], sem_b.at[k], piece) for k, piece in enumerate(pieces)]

    logs = exchange(lg, lgot, l_send, l_recv)
    fwd_out = exchanges(snd1, got1, send1, recv1)
    fwd_back = exchanges(snd2, sin, send2, recv2)
    bwd_out = exchanges(snd3, got3, send3, recv3)
    bwd_back = exchanges(snd4, rin, send4, recv4)
    logs[0]()

    def weights_of(h):
        row = jnp.broadcast_to(cum[pl.ds(h, 1)], (Q, Q))
        wts[h] = jnp.where(upper, jnp.exp(jnp.where(upper, row - row.T, 0.0)), 0.0)

    loop(0, H, weights_of)

    loads[1].wait()
    loads[2].wait()

    def columns_of(k):
        part = pl.ds(pl.multiple_of(k * Q, Q), Q)
        gt[part] = g_ref[0, :, part].astype(f32).T.astype(b16)
        gain[part] = jnp.broadcast_to(gain_ref[pl.ds(k, 1)], (Q, Q)).T * valid

    loop(0, hp // Q, columns_of)

    piece = Q // (2 * NY)
    for n, j in enumerate((7, 0, 6, 1, 5, 2, 4, 3)):
        c = (z + NZ - 1 - j) % NZ
        w_copy(j).wait()
        if j == NZ - 1:
            a_home.wait()
            c = z
        else:
            a_copy(j).wait_recv()
        got = block(c)[...]
        term = dot(got, wv[c])
        if n == 0:
            acc[...] = term
        else:
            acc[...] += term
        for k in range(width // Q):
            turned = got[:, k * Q:(k + 1) * Q].astype(f32).T.astype(b16)
            for m in range(Q // piece):
                feature = k * Q + m * piece
                xtp[feature // (NY * piece), (feature // piece) % NY, pl.ds(pl.multiple_of(c * piece, piece), piece)] = (
                    turned[m * piece:(m + 1) * piece])

    def part_of(color, q):
        return dp.at[:, pl.ds(color * half + COLUMNS[q][0], COLUMNS[q][1])]

    def p_slot(slot, q):
        return pg.at[slot, :, pl.ds(COLUMNS[q][0], COLUMNS[q][1])]

    def x_slot(slot, u):
        return xg.at[pl.ds(2 * u, 2), :, pl.ds(pl.multiple_of(slot * Q, Q), Q)]

    def x_line(u):
        two = pl.ds(2 * u, 2)

        def copy(color, j):
            if color == 0:
                return send(xtp.at[(x + j) % NX, two], x_slot(x * 2 + core, u), x_send.at[u], x_recv.at[u],
                            at((x + j) % NX, y, z, 0))
            return send(xtp.at[two, (y + j) % NY], x_slot(y * 2 + core, u), x_send.at[u], x_recv.at[u],
                        at(x, (y + j) % NY, z, 1))
        return copy

    def p_line(q):
        def copy(color, j):
            sem = p_recv.at[q] if j == 0 else p_near.at[q, j // 2]
            if color == 0:
                return send(part_of(0, q), p_slot(x * 2 + core, q), p_send.at[q], sem, at((x + j) % NX, y, z, 0))
            return send(part_of(1, q), p_slot(y * 2 + core, q), p_send.at[q], sem, at(x, (y + j) % NY, z, 1))
        return copy

    spot = (1 - core) * x + core * y

    def relay(q):
        off, many = COLUMNS[q]
        cols = pl.ds(off, many)
        for side, step in ((0, 1), (1, 3)):
            wait_for(pg.at[pl.ds(0, 2), :, cols], p_near.at[q, side])
            from_chip = pg.at[pl.ds(2 * ((spot + 4 - step) % 4), 2), pl.ds(side * (Q // 2), Q // 2), cols]
            peer = at((x + (1 - core) * step) % NX, (y + core * step) % NY, z, core)
            send(from_chip, from_chip, p_send.at[q], p_recv.at[q], peer).start()

    def lines(what, act, steps=(2, 1, 3)):
        for j in steps:
            act(what(0, j))
            act(what(1, j))

        @pl.when(core == 0)
        def _():
            act(what(1, 0))

        @pl.when(core == 1)
        def _():
            act(what(0, 0))

    def x_rows(u):
        two = pl.ds(2 * u, 2)
        lines(x_line(u), lambda copy: copy.start())

        @pl.when(core == 0)
        def _():
            pltpu.make_async_copy(xtp.at[x, two], x_slot(x * 2, u), x_recv.at[u]).start()

        @pl.when(core == 1)
        def _():
            pltpu.make_async_copy(xtp.at[two, y], x_slot(y * 2 + 1, u), x_recv.at[u]).start()

    for k in range((hp + 2 * N) // Q):
        part = acc[:, k * Q:(k + 1) * Q]
        if k < hp // Q:
            part = jnp.where(valid_col, part, 0.0)
        proj[:, k * Q:(k + 1) * Q] = part.astype(b16)
        xt[k * Q:(k + 1) * Q] = part.T.astype(b16)

    b_nat, c_nat = proj[:, hp:hp + N], proj[:, hp + N:hp + 2 * N]
    b_t, c_t = xt[hp:hp + N], xt[hp + N:hp + 2 * N]

    def rows(g, i):
        return pl.ds(pl.multiple_of((g * group + i) * P_SIZE, P_SIZE), P_SIZE)

    def turn(gg):
        return (gg + 1 + me // group) % (H // group)

    def in_turns(body, piece):
        def step(gg):
            body(turn(gg))

            @pl.when(gg > 0)
            def _():
                piece[3](turn(gg - 1))
        loop(0, H // group, step)
        piece[3](turn(H // group - 1))
        piece[4]()

    def local_states(g):
        for i in range(group):
            h = g * group + i
            xw[h] = (xt[rows(g, i)].astype(f32) * tail[pl.ds(h, 1)]).astype(b16)
        states = dot(xw[pl.ds(g * group, group)].reshape(group * P_SIZE, Q), b_nat)
        snd1[pl.ds(g * group, group)] = states.astype(b16).reshape(group, P_SIZE, N)

    in_turns(local_states, fwd_out[0])
    for one in fwd_out[1:]:
        one[0]()
    x_rows(0)

    scores = dot(b_nat, c_t)

    def inside(g):
        for i in range(group):
            h = g * group + i
            mix[h] = (wts[h] * scores).astype(b16)
            yin[h] = dot(xt[rows(g, i)], mix[h])

    loop(0, H // group, inside)
    logs[1]()
    size = P_SIZE // PIECES

    def scan(parts, out, piece, reverse):
        def body(m, state):
            for n in range(8):
                k = m * 8 + n
                i = n_tm - 1 - k if reverse else k
                out[i, piece] = state.astype(b16).reshape(size, N)
                decay = jnp.exp(lgot[i])
                state = decay[None] * state + parts[i, piece].astype(f32).reshape(size // 8, 8, N)
            return state
        lax.fori_loop(0, n_tm // 8, body, jnp.zeros((size // 8, 8, N), f32))

    for k, piece in enumerate(pieces):
        fwd_out[k][1]()
        scan(got1, snd2, piece, False)
        fwd_back[k][0]()
    for one in fwd_back:
        one[1]()

    def norm_step(g):
        carried = dot(sin[pl.ds(g * group, group)].reshape(group * P_SIZE, N), c_t)
        for i in range(group):
            h = g * group + i
            up = lift[pl.ds(h, 1)]
            raw = yin[h] + up * carried[i * P_SIZE:(i + 1) * P_SIZE]
            inv = lax.rsqrt(jnp.mean(raw * raw, axis=0, keepdims=True) + epsilon)
            normed = raw * inv
            scaled = gain[rows(g, i)]
            lot[rows(g, i)] = normed * scaled
            d_normed = gt[rows(g, i)].astype(f32) * scaled
            d_out = inv * (d_normed - normed * jnp.mean(d_normed * normed, axis=0, keepdims=True))
            dt[h] = d_out.astype(b16)
            dl[h] = (d_out * up).astype(b16)
        states = dot(dl[pl.ds(g * group, group)].reshape(group * P_SIZE, Q), c_nat)
        snd3[pl.ds(g * group, group)] = states.astype(b16).reshape(group, P_SIZE, N)

    in_turns(norm_step, bwd_out[0])
    for one in bwd_out[1:]:
        one[0]()
    x_rows(1)

    first = subs_of((2 * P_SIZE, Q)) < P_SIZE

    def pairs(g, total):
        for i in range(0, group, 2):
            h = g * group + i
            d_two = dt[pl.ds(h, 2)].reshape(2 * P_SIZE, Q)
            zero = jnp.zeros_like(d_two)
            spread = jnp.concatenate([jnp.where(first, d_two, zero), jnp.where(first, zero, d_two)], axis=1)
            x_two = proj[:, pl.ds(pl.multiple_of(h * P_SIZE, 2 * P_SIZE), 2 * P_SIZE)]
            both = dot(x_two, spread)
            total = total + wts[h] * both[:, :Q] + wts[h + 1] * both[:, Q:]
            din[h] = dot_t(dt[h], mix[h])
            din[h + 1] = dot_t(dt[h + 1], mix[h + 1])
        return total

    pair_sum = lax.fori_loop(0, H // group, pairs, jnp.zeros((Q, Q), f32)).astype(b16)
    for k, piece in enumerate(pieces):
        bwd_out[k][1]()
        scan(got3, snd4, piece, True)
        bwd_back[k][0]()
    d_c = t_dot(pair_sum, b_nat) + t_dot(dl[...].reshape(hp, Q), sin[...].reshape(hp, N))
    d_b = dot(pair_sum, c_nat)
    dp[:, hp + N:hp + 2 * N] = d_c.astype(b16)
    for k in range(hp // Q):
        lay[:, k * Q:(k + 1) * Q] = lot[k * Q:(k + 1) * Q].T.astype(b16)
    lay_home = pltpu.make_async_copy(lay, out_ref, o_sem)
    lay_home.start()
    for one in bwd_back:
        one[1]()

    def inputs_of(k):
        after = dot(rin[2 * k:2 * k + 2].reshape(2 * P_SIZE, N), b_t)
        two = [din[2 * k + i] + tail[2 * k + i:2 * k + i + 1] * after[i * P_SIZE:(i + 1) * P_SIZE] for i in range(2)]
        dp[:, k * Q:(k + 1) * Q] = (jnp.concatenate(two, axis=0) * valid).T.astype(b16)

    done = set()
    for q, (off, many) in enumerate(COLUMNS):
        for k in range(hp // Q):
            if k not in done and any(color * half + off <= k * Q < color * half + off + many for color in range(2)):
                done.add(k)
                inputs_of(k)
        if q == len(COLUMNS) - 1:
            d_b = d_b + t_dot(xw[...].reshape(hp, Q), rin[...].reshape(hp, N))
            dp[:, hp:hp + N] = d_b.astype(b16)
        lines(p_line(q), lambda copy: copy.start(), (1, 3))

        @pl.when(core == 0)
        def _():
            pltpu.make_async_copy(part_of(0, q), p_slot(x * 2, q), p_recv.at[q]).start()

        @pl.when(core == 1)
        def _():
            pltpu.make_async_copy(part_of(1, q), p_slot(y * 2 + 1, q), p_recv.at[q]).start()

    def e_copy(j):
        return send(rows_out.at[j], demb_ref.at[z], e_send, e_recv, ((z + 1 + j) % NZ, me))

    e_home = pltpu.make_async_copy(rows_out.at[NZ - 1], demb_ref.at[z], e_recv)
    for n, j in enumerate((3, 2, 4, 1, 5, 0, 6, 7)):
        if n == RELAY_AT:
            relay(0)
        rows_out[j] = dot_t(dp[...], wv[(z + 1 + j) % NZ]).astype(b16)
        if j < NZ - 1:
            e_copy(j).start()
        else:
            e_home.start()

    p = (1 - core) * y + core * x
    line = z * 2 + core

    def second(j, q):
        k = (p + 1 + j) % NX
        peer = at((1 - core) * x + core * k, (1 - core) * k + core * y, z, core)
        cols = pl.ds(*COLUMNS[q])
        return send(s2.at[j, :, cols], r2.at[j, :, cols], send5.at[q], recv5.at[q], peer)

    def third(j, q):
        slot = (line + j) % (2 * NZ)
        cols = pl.ds(*COLUMNS[q])
        return send(s3.at[slot, :, cols], r3.at[line, :, cols], send6.at[q], recv6.at[q], at(x, y, slot // 2, slot % 2))

    for u in range(2):
        wait_for(xg.at[pl.ds(2 * u, 2)], x_recv.at[u])

    def multiply(q):
        off, many = COLUMNS[q]
        cols = slice(off, off + many)
        wait_for(pg.at[pl.ds(0, 4), :, pl.ds(off, many)], p_recv.at[q])
        right = pg[:, :, cols].reshape(8 * Q, many)
        for j in (1, 0, 2, 3):
            part = dot(xg[(p + 1 + j) % NX], right)
            if j < NX - 1:
                s2[j, :, cols] = part.astype(b16)
                second(j, q).start()
            else:
                own[:, cols] = part

    def add(q):
        off, many = COLUMNS[q]
        cols = slice(off, off + many)
        wait_for(r2.at[:, :, pl.ds(off, many)], recv5.at[q])
        own[:, cols] = (own[:, cols] + r2[0, :, cols].astype(f32) + r2[1, :, cols].astype(f32) + r2[2, :, cols].astype(f32)) * scale
        for slot in range(2 * NZ):
            s3[slot, :, cols] = own[8 * slot:8 * slot + 8, cols].astype(b16)
        for j in (8, 7, 9, 6, 10, 5, 11, 4, 12, 3, 13, 2, 14, 1, 15):
            third(j, q).start()
        r3[line, :, cols] = s3[line, :, cols]

    for q in range(1, len(COLUMNS)):
        relay(q)
    multiply(0)
    for q in range(1, len(COLUMNS)):
        multiply(q)
        add(q - 1)
    add(len(COLUMNS) - 1)
    others = pl.ds(0, 2 * NZ - 1)
    for q, (off, many) in enumerate(COLUMNS):
        wait_for(r3.at[others, :, pl.ds(off, many)], recv6.at[q])
        for color in range(2):
            sums = r3[color, :, off:off + many].astype(f32)
            for c in range(1, NZ):
                sums = sums + r3[2 * c + color, :, off:off + many].astype(f32)
            dw_ref[:, color * half + off:color * half + off + many] = sums

    lay_home.wait()
    wait_for(rows_out.at[pl.ds(0, NZ - 1)], a_send)
    wait_for(rows_out.at[pl.ds(0, NZ - 1)], e_send)
    wait_for(demb_ref, e_recv)
    for one in [logs] + fwd_out + fwd_back + bwd_out + bwd_back:
        one[2]()
    for u in range(2):
        wait_for(xg.at[pl.ds(2 * u, 2), :, pl.ds(0, 7 * Q)], x_send.at[u])
    for q, (off, many) in enumerate(COLUMNS):
        cols = pl.ds(off, many)
        wait_for(pg.at[pl.ds(0, 7), :, cols], p_send.at[q])
        wait_for(s2.at[:, :, cols], send5.at[q])
        wait_for(s3.at[others, :, cols], send6.at[q])


def finish_kernel(*refs):
    half = len(refs) // 4
    ins, outs, held, sems = refs[:half], refs[half:2 * half], refs[2 * half:3 * half], refs[3 * half:]
    loads = [pltpu.make_async_copy(a, b, sem.at[0]) for a, b, sem in zip(ins, held, sems)]
    stores = [pltpu.make_async_copy(a, b, sem.at[1]) for a, b, sem in zip(held, outs, sems)]
    for one in loads:
        one.start()
    for load, store in zip(loads, stores):
        load.wait()
        store.start()
    for one in stores:
        one.wait()


def finish(*arrays):
    hbm = pl.BlockSpec(memory_space=pl.ANY)
    return pl.pallas_call(
        finish_kernel,
        name="finish",
        out_shape=[jax.ShapeDtypeStruct(a.shape, a.dtype) for a in arrays],
        in_specs=[hbm] * len(arrays),
        out_specs=[hbm] * len(arrays),
        scratch_shapes=[pltpu.VMEM(a.shape, a.dtype) for a in arrays] + [pltpu.SemaphoreType.DMA((2,)) for _ in arrays],
    )(*arrays)


def on_device(embeds, w_in, log_decay, clip_keep, clip_starts, valid_len, norm_gain, g_out):
    n_cam, t, width = embeds.shape
    d, e = w_in.shape
    n_tm = lax.axis_size("tm")
    half, part, many = e // 2, d // NX // NY, len(COLUMNS)
    scale = 1.0 / math.sqrt(n_cam * t * n_tm)
    dma = pltpu.SemaphoreType.DMA
    vmem = pl.BlockSpec(memory_space=pltpu.VMEM)
    smem = pl.BlockSpec(memory_space=pltpu.SMEM)
    hbm = pl.BlockSpec(memory_space=pl.ANY)
    f32, b16 = jnp.float32, jnp.bfloat16
    scratch = lambda dtype, *shape: pltpu.VMEM(shape, dtype)
    layer_out, d_embeds, d_w_in = pl.pallas_call(
        functools.partial(layer_kernel, scale),
        name="layer",
        out_shape=(jax.ShapeDtypeStruct((t, HP), b16), jax.ShapeDtypeStruct((n_cam, t, width), b16),
                   jax.ShapeDtypeStruct((part // n_cam // 2, e), f32)),
        in_specs=[smem, smem, hbm, hbm, hbm, vmem, hbm, hbm],
        out_specs=(hbm, hbm, vmem),
        scratch_shapes=[
            scratch(b16, n_cam, width, e), scratch(b16, t, d), scratch(f32, t, e), scratch(b16, t, e), scratch(b16, e, t),
            scratch(b16, NX, NY, part, t), scratch(b16, HP, t), scratch(f32, HP, t), scratch(f32, H, t, t),
            scratch(f32, H, t), scratch(f32, H, t), scratch(f32, H, t), scratch(f32, H, t),
            scratch(b16, H, P_SIZE, t), scratch(b16, H, t, t), scratch(f32, H, P_SIZE, t),
            scratch(b16, H, P_SIZE, t), scratch(b16, H, P_SIZE, t), scratch(f32, H, P_SIZE, t),
            scratch(f32, HP, t), scratch(f32, H, 8, N), scratch(f32, n_tm, 8, N),
        ] + [scratch(b16, n_tm, P_SIZE, N)] * 8 + [
            scratch(b16, t, e), scratch(b16, NX, part, 8 * t), scratch(b16, 8, t, half), scratch(b16, n_cam, t, width),
            scratch(b16, NX - 1, part, half), scratch(b16, NX - 1, part, half),
            scratch(b16, 2 * n_cam, part // n_cam // 2, half), scratch(b16, 2 * n_cam, part // n_cam // 2, half),
            scratch(f32, part, half), scratch(b16, t, HP),
            scratch(f32, 1, H, t), scratch(f32, HP // Q, Q), scratch(b16, 1, t, HP),
            dma((n_cam,)), dma, dma((3,)), dma, dma((n_cam,)), dma, dma,
        ] + [dma((PIECES,))] * 8 + [
            dma((2,)), dma((2,)), dma((many,)), dma((many,)), dma((many, 2)), dma, dma,
            dma((many,)), dma((many,)), dma((many,)), dma((many,)),
        ],
        compiler_params=pltpu.CompilerParams(collective_id=0, has_side_effects=True, vmem_limit_bytes=60 * 1024 * 1024),
    )(clip_starts, valid_len, embeds, w_in, log_decay, clip_keep.reshape(1, H), norm_gain.reshape(HP // Q, Q), g_out)
    layer_out, d_embeds, d_w_in = finish(layer_out, d_embeds, d_w_in)
    return (layer_out[None], d_embeds, d_w_in)


def solution(mesh):
    return jax.shard_map(
        on_device,
        mesh=mesh,
        in_specs=(
            P(None, "tm", "cam"),
            P(),
            P("cam", None, "tm"),
            P(),
            P("cam", None),
            P("cam"),
            P(),
            P("cam", "tm", None),
        ),
        out_specs=(P("cam", "tm", None), P(None, "tm", "cam"), P(("cam", "tm"), None)),
        check_vma=False,
    )
```
